128 devices in a mesh: facet: 4 (over x), sub: 32 (over z, y, core).
Axes of the slice: x: 4, y: 4, z: 4, core: 2. Of those that a mesh axis runs over, the one named last changes fastest.
Arguments:
- facet_slab: bfloat16 [4, 2, 512, 8192], P('facet', None, 'sub'), may hold values from -6 to 6
- facet_offsets: int32 [4, 2], P('facet'), may hold values from 0 to 24576
- visibility_position: float32 [2, 131072], P(None, ('facet', 'sub')), may hold values from -32 to 32
- observed: float32 [2, 131072], P(None, ('facet', 'sub')), may hold values from -3 to 3
- visibility_subgrid: int32 [131072, 1], P(('facet', 'sub')), may hold values from 0 to 255; in each aligned block of 1024 rows (0 to 1023, 1024 to 2047, ...) at most 8 rows name the same one
- clip_levels: int32 [4096], P(('facet', 'sub')), may hold values from 1 to 8
Outputs:
- facet_adjoint: float32 [4, 2, 512, 8192], P('facet', None, 'sub')
- weighted_residual: float32 [2, 131072], P(None, ('facet', 'sub'))
The draws below stay inside these ranges and needn't reach their ends.
Inputs may be any that keep to these rules, and one draw needn't show every extreme that they name: `visibility_subgrid`: subgrid p * 32 + q covers subgrid row block p and column block q; within the rows of one device no subgrid is named more than 8 times. `facet_offsets`: column 0 is a facet's first image row, column 1 its first image column.
All inputs are finite; a program needn't handle non-finite values.
Results may differ from the reference program's by a relative error of at most 0.012.
Values may be sent and summed in bfloat16 or wider, within the bound.
No kernel may reach another device: no remote copies, remote signals or barrier semaphores. Data moves between devices by JAX's collectives and lax.ppermute only.
A program may use at most 128 MiB of HBM per device.

```python
import math
import jax
import jax.numpy as jnp
import numpy as np
from jax import lax

FS = 8192
N_IMG = 32768
SUBG = 64
V_DEV = 1024
VIS_BLOCK = 32
FACETS = 4
ROWS = 512
NR = 8
NCOL = 32
NSG = 256
NVIS = 131072
MOST = 8
N_FACET = 4
N_SUB = 32


TWO_PI = 2.0 * math.pi


def tone_angles(count, frequency):
    position = jnp.arange(count, dtype=jnp.int32)
    phase_index = frequency[:, :, None] * position[None, None, :] % N_IMG
    return phase_index.astype(jnp.float32) * (TWO_PI / N_IMG)


def draw_facet_slab(key, part):
    keys = jax.random.split(jax.random.fold_in(key, 7301), 8)
    col_res = max(N_IMG // FS, 2)
    row_res = max(N_IMG // ROWS, 2)
    col_gap = jax.random.randint(keys[0], (FACETS, NCOL), col_res // 2 + 1, 2 * col_res + 1)
    col_side = jax.random.randint(keys[1], (FACETS, NCOL), 0, 2)
    col_base = jnp.arange(NCOL, dtype=jnp.int32)[None, :] * (N_IMG // NCOL)
    col_freq = (col_base + jnp.where(col_side == 1, SUBG - 1 + col_gap, N_IMG - col_gap)) % N_IMG
    row_gap = jax.random.randint(keys[2], (FACETS, NR), row_res // 2 + 1, 2 * row_res + 1)
    row_side = jax.random.randint(keys[3], (FACETS, NR), 0, 2)
    row_base = jnp.arange(NR, dtype=jnp.int32)[None, :] * (N_IMG // NR)
    row_freq = (row_base + jnp.where(row_side == 1, SUBG - 1 + row_gap, N_IMG - row_gap)) % N_IMG
    col_angle = tone_angles(FS, col_freq.astype(jnp.int32))
    row_angle = tone_angles(ROWS, row_freq.astype(jnp.int32))
    col_real = jnp.cos(col_angle)
    col_imag = jnp.sin(col_angle)
    row_real = jnp.cos(row_angle)
    row_imag = jnp.sin(row_angle)
    magnitude = jax.random.uniform(keys[4], (FACETS, NR, NCOL), jnp.float32, 0.06, 0.12)
    turn = jax.random.uniform(keys[5], (FACETS, NR, NCOL), jnp.float32, -math.pi, math.pi)
    amp_real = magnitude * jnp.cos(turn)
    amp_imag = magnitude * jnp.sin(turn)
    high = lax.Precision.HIGHEST
    mixed_real = jnp.einsum('fpr,fpq->frq', row_real, amp_real, precision=high) - jnp.einsum('fpr,fpq->frq', row_imag, amp_imag, precision=high)
    mixed_imag = jnp.einsum('fpr,fpq->frq', row_real, amp_imag, precision=high) + jnp.einsum('fpr,fpq->frq', row_imag, amp_real, precision=high)
    slab_real = jnp.einsum('frq,fqj->frj', mixed_real, col_real, precision=high) - jnp.einsum('frq,fqj->frj', mixed_imag, col_imag, precision=high)
    slab_imag = jnp.einsum('frq,fqj->frj', mixed_real, col_imag, precision=high) + jnp.einsum('frq,fqj->frj', mixed_imag, col_real, precision=high)
    noise = 0.15 * jax.random.normal(keys[6], (FACETS, 2, ROWS, FS), jnp.float32)
    slab = jnp.stack([slab_real, slab_imag], 1) + noise
    return jnp.clip(slab, -6.0, 6.0).astype(jnp.bfloat16)


def plant(values, rng, least, top_value):
    longest = values.shape.index(max(values.shape))
    spots = []
    for shift in (0, 1):
        where = [jax.random.randint(jax.random.fold_in(rng, axis), (), 0, length) for axis, length in enumerate(values.shape)]
        where[longest] = (where[longest] + shift) % values.shape[longest]
        spots.append(tuple(where))
    return values.at[spots[0]].set(least).at[spots[1]].set(top_value)


def level_of(own_key, extent, cuts, smallest, top_value):
    level, own = 1.0, jax.random.fold_in(own_key, 6)
    for dim, blocks in cuts:
        heights = jnp.exp(jax.random.uniform(jax.random.fold_in(own, dim), (blocks,), jnp.float32, smallest / len(cuts), top_value / len(cuts)))
        level = level * jnp.repeat(heights, extent[dim] // blocks).reshape([-1 if axis == dim else 1 for axis in range(len(extent))])
    return level


def shared_out(own_key, own, number, rows, number_of, top, bound, skew):
    ranking = jax.random.permutation(own_key, number_of)
    packed, common = portions_of(number_of, rows * top, bound, skew, True), portions_of(number_of, rows * top, bound, skew, False)
    places = jnp.arange(number_of)

    def named(tallies, turn):
        used = int((tallies > 0).sum())
        fixed = max(1, used // 4)
        passed = fixed + (places - fixed + turn * (used - fixed)) % max(1, number_of - fixed)
        return jnp.zeros((number_of,), jnp.int32).at[ranking[jnp.where(places < fixed, places, passed)]].set(jnp.asarray(tallies, jnp.int32))

    tallies = jnp.where(number % 4 == 0, named(packed, number // 4), named(common, number - number // 4 - 1))
    mixed = jax.random.permutation(jax.random.fold_in(own, 3), number_of)
    source_of, taker = mixed[0:number_of // 2 * 2:2], mixed[1:number_of // 2 * 2:2]
    margin = jnp.minimum(tallies[source_of] - 1, bound - tallies[taker]) // 2
    margin = jnp.where((source_of == ranking[0]) | (taker == ranking[0]) | (tallies[taker] == 0), 0, jnp.maximum(margin, 0))
    passed = jax.random.randint(jax.random.fold_in(own, 4), (number_of // 2,), 0, 1 << 20) % (margin + 1)
    tallies = tallies.at[source_of].add(-passed).at[taker].add(passed)
    members = jnp.searchsorted(jnp.cumsum(tallies), jnp.arange(rows * top), side="right").astype(jnp.int32)
    table = members.reshape(top, rows).T
    table = table[jax.random.permutation(jax.random.fold_in(own, 1), rows)]
    turn = jax.random.randint(jax.random.fold_in(own, 2), (rows, 1), 0, top)
    return jnp.take_along_axis(table, (jnp.arange(top)[None, :] + turn) % top, axis=1)


def portions_of(amount, total, reach, lean, full):
    loads = [(1 << 20) // math.isqrt(grade ** lean) + 1 for grade in range(1, amount + 1)]
    largest = reach if full else min(reach, max(-(-total // amount), total * loads[0] // sum(loads)))
    least = 1 if total - largest >= amount - 1 else 0
    holding, spare = [largest] + [least] * (amount - 1), total - largest - least * (amount - 1)
    while spare > 0:
        candidates = [i for i in range(1, amount) if holding[i] < largest] or [i for i in range(1, amount) if holding[i] < reach]
        pool, remaining = sum([loads[i] for i in candidates]), spare
        for i in candidates:
            more = min(reach - holding[i], max(1, remaining * loads[i] // pool), spare)
            holding[i] = holding[i] + more
            spare = spare - more
    return np.array(holding)


def normal_values(rng, shape, deviation, bound, cuts=(), kind=jnp.bfloat16):
    gain = level_of(rng, shape, cuts, -0.22, 0.18) if cuts else 1.0
    values = jax.random.normal(rng, shape, jnp.float32) * deviation * gain
    return jnp.minimum(jnp.maximum(values, -bound), bound).astype(kind)


def setup_inputs(seed: int = 0) -> dict:
    key_of = jax.random.split(jax.random.key(seed), 7)
    facet_slab = draw_facet_slab(jax.random.fold_in(key_of[6], 71), 0)
    facet_offsets = plant(jax.random.randint(key_of[1], (FACETS, 2), 0, N_IMG - FS + 1), jax.random.fold_in(key_of[1], 1), 0, N_IMG - FS).astype(jnp.int32)
    visibility_position = jnp.clip(jax.random.uniform(key_of[2], (2, NVIS), jnp.float32, -32.0, 32.0) * level_of(key_of[2], (2, NVIS), ((1, 128),), -0.4, 0.0), -32.0, 32.0)
    observed = normal_values(key_of[3], (2, NVIS), 0.5, 3.0, ((1, 128),), jnp.float32)
    visibility_subgrid_keys = jax.random.split(jax.random.fold_in(key_of[4], 1), NVIS // V_DEV)
    visibility_subgrid_turns = jax.random.permutation(jax.random.fold_in(key_of[4], 3), NVIS // V_DEV)
    visibility_subgrid = jax.vmap(lambda own, number: shared_out(jax.random.fold_in(key_of[4], 2), own, number, V_DEV, NSG, 1, MOST, 2))(visibility_subgrid_keys, visibility_subgrid_turns).reshape((NVIS, 1))
    clip_levels = plant(jax.random.randint(key_of[5], (NVIS // VIS_BLOCK,), 1, 9), jax.random.fold_in(key_of[5], 1), 1, 8).astype(jnp.int32)
    return {"facet_slab": facet_slab, "facet_offsets": facet_offsets, "visibility_position": visibility_position, "observed": observed, "visibility_subgrid": visibility_subgrid, "clip_levels": clip_levels}


TWO_PI = 2.0 * math.pi

def phase_pair(position, frequency, image_size, factor):
    phase_index = position[:, None] * frequency[None, :] % image_size
    angles = phase_index.astype(jnp.float32) * (-TWO_PI / image_size)
    return ((jnp.cos(angles) * factor).astype(jnp.bfloat16), (jnp.sin(angles) * factor).astype(jnp.bfloat16))

def column_tables(col_offset, facet_width, image_size, subgrid_size, column_count):
    position = col_offset + jnp.arange(facet_width, dtype=jnp.int32)
    fine_cos, fine_sin = phase_pair(position, jnp.arange(subgrid_size, dtype=jnp.int32), image_size, facet_width ** (-0.5))
    coarse_freq = jnp.arange(column_count, dtype=jnp.int32) * (image_size // column_count)
    coarse_cos, coarse_sin = phase_pair(position, coarse_freq, image_size, 1.0)
    return (fine_cos, fine_sin, coarse_cos, coarse_sin)

def row_tables(position, image_size, subgrid_size, row_blocks, total_rows):
    block_start = jnp.arange(row_blocks, dtype=jnp.int32)[:, None] * (image_size // row_blocks)
    frequency = (block_start + jnp.arange(subgrid_size, dtype=jnp.int32)[None, :]).reshape(-1)
    return phase_pair(position, frequency, image_size, 0.5 * total_rows ** (-0.5))

def column_forward(slab_real, slab_imag, tables):
    fine_cos, fine_sin, coarse_cos, coarse_sin = tables
    facet_width = fine_cos.shape[0]
    column_count = coarse_cos.shape[1]
    row_count = slab_real.shape[0]
    grouping = 4
    forward_matrix = jnp.concatenate([jnp.concatenate([fine_cos, fine_sin], 1), jnp.concatenate([-fine_sin, fine_cos], 1)], 0)
    real_wide = slab_real.astype(jnp.float32)[None]
    imag_wide = slab_imag.astype(jnp.float32)[None]

    def one_group(cos_sin):
        cos_group = cos_sin[0].astype(jnp.float32)[:, None, :]
        sin_group = cos_sin[1].astype(jnp.float32)[:, None, :]
        mod_real = (real_wide * cos_group - imag_wide * sin_group).astype(jnp.bfloat16)
        mod_imag = (real_wide * sin_group + imag_wide * cos_group).astype(jnp.bfloat16)
        joined = jnp.concatenate([mod_real, mod_imag], 2).reshape(grouping * row_count, 2 * facet_width)
        return jnp.dot(joined, forward_matrix, preferred_element_type=jnp.float32).reshape(grouping, row_count, -1)
    cos_groups = coarse_cos.T.reshape(column_count // grouping, grouping, facet_width)
    sin_groups = coarse_sin.T.reshape(column_count // grouping, grouping, facet_width)
    spectra = lax.map(one_group, (cos_groups, sin_groups))
    spectra = spectra.reshape(column_count, row_count, -1).transpose(1, 0, 2)
    return spectra.astype(jnp.bfloat16)

def row_forward(row_cos, row_sin, spectra):
    half_width = spectra.shape[2] // 2
    swapped = jnp.concatenate([-spectra[:, :, half_width:], spectra[:, :, :half_width]], 2)
    stacked = jnp.concatenate([spectra, swapped], 0)
    left_rows = jnp.concatenate([row_cos, row_sin], 0)
    flat = stacked.reshape(stacked.shape[0], -1)
    result = jnp.dot(left_rows.T, flat, preferred_element_type=jnp.float32)
    return result.reshape(left_rows.shape[1], spectra.shape[1], spectra.shape[2])

def row_adjoint(row_cos, row_sin, corrected_rows):
    half_width = corrected_rows.shape[2] // 2
    swapped = jnp.concatenate([corrected_rows[:, :, half_width:], -corrected_rows[:, :, :half_width]], 2)
    stacked = jnp.concatenate([corrected_rows, swapped], 0)
    left_rows = jnp.concatenate([row_cos, row_sin], 1)
    flat = stacked.reshape(stacked.shape[0], -1)
    result = jnp.dot(left_rows, flat, preferred_element_type=jnp.float32)
    return result.reshape(left_rows.shape[0], corrected_rows.shape[1], corrected_rows.shape[2])

def column_adjoint(images, tables):
    fine_cos, fine_sin, coarse_cos, coarse_sin = tables
    facet_width = fine_cos.shape[0]
    row_count = images.shape[0]
    column_count = images.shape[1]
    grouping = 4
    adjoint_matrix = jnp.concatenate([jnp.concatenate([fine_cos.T, -fine_sin.T], 1), jnp.concatenate([fine_sin.T, fine_cos.T], 1)], 0)
    image_groups = images.transpose(1, 0, 2).reshape(column_count // grouping, grouping * row_count, images.shape[2])
    cos_groups = coarse_cos.T.reshape(column_count // grouping, grouping, facet_width)
    sin_groups = coarse_sin.T.reshape(column_count // grouping, grouping, facet_width)

    def accumulate(running, inputs):
        image_group, cos_group, sin_group = inputs
        spread = jnp.dot(image_group, adjoint_matrix, preferred_element_type=jnp.float32).reshape(grouping, row_count, 2 * facet_width)
        spread_real = spread[:, :, :facet_width]
        spread_imag = spread[:, :, facet_width:]
        cos_wide = cos_group.astype(jnp.float32)[:, None, :]
        sin_wide = sin_group.astype(jnp.float32)[:, None, :]
        new_real = running[0] + lax.optimization_barrier(jnp.sum(cos_wide * spread_real + sin_wide * spread_imag, 0))
        new_imag = running[1] + lax.optimization_barrier(jnp.sum(cos_wide * spread_imag - sin_wide * spread_real, 0))
        return ((new_real, new_imag), None)
    initial = (jnp.zeros((row_count, facet_width), jnp.float32), jnp.zeros((row_count, facet_width), jnp.float32))
    finals, unused = lax.scan(accumulate, initial, (image_groups, cos_groups, sin_groups))
    return jnp.stack([finals[0], finals[1]])

def batched(pattern, left_operand, right_operand):
    return jnp.einsum(pattern, left_operand.astype(jnp.float32), right_operand.astype(jnp.float32))

def subgrid_pass(subgrids, payload, live_mask):
    subgrid_size = subgrids.shape[1]
    factor = subgrid_size ** (-0.5)
    offsets_grid = jnp.arange(subgrid_size, dtype=jnp.float32) * (TWO_PI / subgrid_size)
    angle_left = payload[0][:, :, None] * offsets_grid
    angle_right = payload[1][:, :, None] * offsets_grid
    left_real = jnp.cos(angle_left) * factor
    left_imag = jnp.sin(angle_left) * factor
    right_real = (jnp.cos(angle_right) * factor).astype(jnp.bfloat16)
    right_imag = (jnp.sin(angle_right) * factor).astype(jnp.bfloat16)
    first_basis = jnp.concatenate([right_real, -right_imag], 2)
    second_basis = jnp.concatenate([right_imag, right_real], 2)
    inner_real = batched('ksc,knc->kns', subgrids, first_basis)
    inner_imag = batched('ksc,knc->kns', subgrids, second_basis)
    predicted_real = lax.optimization_barrier(jnp.sum(left_real * inner_real - left_imag * inner_imag, 2))
    predicted_imag = lax.optimization_barrier(jnp.sum(left_real * inner_imag + left_imag * inner_real, 2))
    misfit_real = payload[2] - predicted_real
    misfit_imag = payload[3] - predicted_imag
    threshold = payload[4] + (1.0 - live_mask)
    magnitude = jnp.sqrt(misfit_real * misfit_real + misfit_imag * misfit_imag)
    weight = live_mask * threshold / jnp.maximum(magnitude, threshold)
    weighted_real = weight * misfit_real
    weighted_imag = weight * misfit_imag
    phasor_real = (left_real * weighted_real[:, :, None] + left_imag * weighted_imag[:, :, None]).astype(jnp.bfloat16)
    phasor_imag = (left_real * weighted_imag[:, :, None] - left_imag * weighted_real[:, :, None]).astype(jnp.bfloat16)
    gridded = batched('kms,kmc->ksc', jnp.concatenate([phasor_real, phasor_imag], 1), jnp.concatenate([first_basis, second_basis], 1))
    return (gridded.astype(jnp.bfloat16), weighted_real, weighted_imag)

def reference(facet_slab, facet_offsets, visibility_position, observed, visibility_subgrid, clip_levels):
    visibility_count = visibility_position.shape[1]
    total_rows = facet_slab.shape[2]
    kept_tables = []
    kept_rows = []
    summed = None
    for facet_index in range(FACETS):
        tables = column_tables(facet_offsets[facet_index, 1], FS, N_IMG, SUBG, NCOL)
        spectra = column_forward(facet_slab[facet_index, 0], facet_slab[facet_index, 1], tables)
        row_position = facet_offsets[facet_index, 0] + jnp.arange(total_rows, dtype=jnp.int32)
        row_cos, row_sin = row_tables(row_position, N_IMG, SUBG, NR, total_rows)
        contribution = row_forward(row_cos, row_sin, spectra)
        summed = contribution if summed is None else summed + contribution
        kept_tables.append(tables)
        kept_rows.append((row_cos, row_sin))
    subgrids = summed.reshape(NR, SUBG, NCOL, 2 * SUBG).transpose(0, 2, 1, 3).reshape(NSG, SUBG, 2 * SUBG).astype(jnp.bfloat16)
    identity = visibility_subgrid[:, 0]
    sort_order = jnp.argsort(identity, stable=True).astype(jnp.int32)
    sorted_ids = identity[sort_order]
    first_seen = jnp.searchsorted(sorted_ids, sorted_ids, side='left').astype(jnp.int32)
    ranked = jnp.arange(visibility_count, dtype=jnp.int32) - first_seen
    capacity = N_FACET * N_SUB * MOST
    slot_table = jnp.full((NSG, capacity), visibility_count, jnp.int32).at[sorted_ids, ranked].set(sort_order)
    levels = jnp.repeat(clip_levels, VIS_BLOCK).astype(jnp.float32) * 0.25
    rows_all = jnp.stack([visibility_position[0], visibility_position[1], observed[0], observed[1], levels])
    rows_all = jnp.concatenate([rows_all, jnp.zeros((5, 1), jnp.float32)], 1)
    live_all = jnp.concatenate([jnp.ones((visibility_count,), jnp.float32), jnp.zeros((1,), jnp.float32)])

    def per_subgrid(element):
        index_row, subgrid = element
        payload = rows_all[:, index_row][:, None, :]
        live_mask = live_all[index_row][None, :]
        gridded, weighted_real, weighted_imag = subgrid_pass(subgrid[None], payload, live_mask)
        return (gridded[0], weighted_real[0], weighted_imag[0])
    corrected, result_real, result_imag = lax.map(per_subgrid, (slot_table, subgrids))
    weighted = jnp.zeros((2, visibility_count + 1), jnp.float32)
    weighted = weighted.at[0, slot_table].set(result_real).at[1, slot_table].set(result_imag)
    weighted_residual = weighted[:, :visibility_count]
    corrected_rows = corrected.reshape(NR, NCOL, SUBG, 2 * SUBG).transpose(0, 2, 1, 3).reshape(NR * SUBG, NCOL, 2 * SUBG)
    adjoints = []
    for facet_index in range(FACETS):
        row_cos, row_sin = kept_rows[facet_index]
        images = row_adjoint(row_cos, row_sin, corrected_rows).astype(jnp.bfloat16)
        adjoints.append(column_adjoint(images, kept_tables[facet_index]))
    return (jnp.stack(adjoints), weighted_residual)
```

```python
import math

import jax
import jax.numpy as jnp
import numpy as np
from jax import lax
from jax.experimental import pallas as pl
from jax.experimental.pallas import tpu as pltpu
from jax.sharding import PartitionSpec as P

N_IMG = 32768
SUBG = 64
VIS_BLOCK = 32
LANES = 128
NQ = 32
NF = 4
NDEV = 128
RD = 16
NA = 64
NV = 1024
SLOT = 16
ROWS_MSG = 24
TWO_PI = 2.0 * math.pi
BF = jnp.bfloat16
F32 = jnp.float32
ALL = ("facet", "sub")


def unit(index, period):
    angle = TWO_PI * (np.asarray(index, np.int64) % period) / period
    return np.cos(angle), np.sin(angle)


def host_tables():
    block = np.arange(NA)
    lane = np.arange(LANES)
    fine = np.arange(SUBG)
    coarse = np.arange(NQ)
    c, s = unit(fine[:, None] * block[None, :], 256)
    c, s = c / 64.0, s / 64.0
    col_fwd = np.block([[c, s], [-s, c]])
    col_adj = np.block([[c.T, -s.T], [s.T, c.T]])
    tw_c, tw_s = unit(fine[:, None] * lane[None, :], N_IMG)
    twiddle_fwd = np.stack([tw_c, -tw_s])
    twiddle_adj = np.stack([np.tile(tw_c.T, (1, 2)), np.tile(tw_s.T, (1, 2))])
    wc, ws = unit(coarse[:, None] * lane[None, :], 32)
    coarse_fwd = np.concatenate([wc, -ws], 1)
    coarse_adj = np.concatenate([wc.T, ws.T], 0)
    k_row = (np.arange(8)[:, None] * 4096 + fine[None, :]).reshape(NF, 2 * SUBG)
    rc, rs = unit(k_row[:, :, None] * np.arange(NQ * RD)[None, None, :], N_IMG)
    rc, rs = rc / 64.0, rs / 64.0
    row_fwd = np.concatenate([rc, -rs], 1)
    row_adj = np.ascontiguousarray(row_fwd.transpose(0, 2, 1))
    bf = lambda x: np.asarray(x, np.float32).astype(jnp.bfloat16)
    return dict(
        col_fwd=bf(col_fwd),
        col_adj=bf(col_adj),
        tw_fwd=np.asarray(twiddle_fwd, np.float32),
        tw_adj=np.asarray(twiddle_adj, np.float32),
        coarse_fwd=bf(coarse_fwd),
        coarse_adj=bf(coarse_adj),
        row_fwd=bf(row_fwd),
        row_adj=bf(row_adj),
    )


def sincos_turn(turn):
    quarter = jnp.floor(turn * 4.0 + 0.5)
    y = (turn - quarter * 0.25) * TWO_PI
    y2 = y * y
    s = y * (1.0 + y2 * (-1.0 / 6 + y2 * (1.0 / 120 + y2 * (-1.0 / 5040 + y2 * (1.0 / 362880)))))
    c = 1.0 + y2 * (-0.5 + y2 * (1.0 / 24 + y2 * (-1.0 / 720 + y2 * (1.0 / 40320))))
    turns = quarter.astype(jnp.int32)
    odd = (turns & 1) == 1
    cos = jnp.where(odd, s, c)
    sin = jnp.where(odd, c, s)
    cos = jnp.where(((turns + 1) & 2) == 2, -cos, cos)
    sin = jnp.where((turns & 2) == 2, -sin, sin)
    return cos, sin


def phase_of(offset, frequency):
    index = (offset * frequency) & (N_IMG - 1)
    return sincos_turn(index.astype(F32) * (1.0 / N_IMG))


def swap(x):
    return pltpu.roll(x, SUBG, x.ndim - 1)


def iota(shape, dim):
    return lax.broadcasted_iota(jnp.int32, shape, dim)


def split3(x):
    high = x.astype(BF)
    rest = x - high.astype(F32)
    middle = rest.astype(BF)
    low = (rest - middle.astype(F32)).astype(BF)
    return high, middle, low


def lane_sign(rows):
    return jnp.where(iota((rows, LANES), 1) < SUBG, 1.0, -1.0).astype(F32)


def send_kernel(
    off_ref, slab_ref, pos_ref, obs_ref, ids_ref, clip_ref, col_ref, tw_ref, coarse_ref,
    msg_ref, meta_ref, wide, rows, extra,
):
    for part in range(2):
        for a in range(NA):
            wide[part, a * RD:(a + 1) * RD, :] = slab_ref[
                0, part, :, a * LANES:(a + 1) * LANES
            ].astype(F32)
    freq = iota((NQ, LANES), 0) * (N_IMG // NQ) + (iota((NQ, LANES), 1) & (SUBG - 1))
    ph_c, ph_s = phase_of(off_ref[0, 1], freq)
    ph_s = ph_s * lane_sign(NQ)
    tw_c, tw_s = tw_ref[0], tw_ref[1]
    group = 4
    for base in range(0, RD, group):
        cols = []
        for r in range(base, base + group):
            cols.append(
                jnp.concatenate(
                    [wide[0, pl.ds(r, NA, stride=RD), :], wide[1, pl.ds(r, NA, stride=RD), :]], 0
                ).astype(BF)
            )
        y = jnp.dot(col_ref[...], jnp.concatenate(cols, 1), preferred_element_type=F32)
        stacked = []
        for i in range(group):
            yr = y[:SUBG, i * LANES:(i + 1) * LANES]
            yi = y[SUBG:, i * LANES:(i + 1) * LANES]
            zr = yr * tw_c - yi * tw_s
            zi = yr * tw_s + yi * tw_c
            stacked.append(jnp.concatenate([zr, -zi], 1).astype(BF))
            stacked.append(jnp.concatenate([zi, zr], 1).astype(BF))
        out = lax.dot_general(
            coarse_ref[...], jnp.concatenate(stacked, 0), (((1,), (1,)), ((), ())),
            preferred_element_type=F32,
        )
        for i in range(group):
            piece = out[:, i * LANES:(i + 1) * LANES]
            rows[pl.ds(base + i, NQ, stride=RD), :] = piece * ph_c + swap(piece) * ph_s
    spectra = rows[...].astype(BF).reshape(NQ, RD, LANES)
    for f in range(NF):
        msg_ref[f * NQ:(f + 1) * NQ, 0:RD, :] = spectra

    ids = ids_ref[...]
    upper = jnp.where(iota((LANES, LANES), 0) < iota((LANES, LANES), 1), 1.0, 0.0).astype(BF)
    counter = jnp.concatenate([upper, jnp.ones((LANES, LANES), BF)], 1)
    before = jnp.zeros((2 * LANES, LANES), F32)
    ranks = []
    for b in range(NV // LANES):
        hot = iota((2 * LANES, LANES), 0) == ids[:, b * LANES:(b + 1) * LANES]
        hot_f = jnp.where(hot, 1.0, 0.0)
        count = jnp.dot(hot_f.astype(BF), counter, preferred_element_type=F32)
        ranks.append(jnp.sum(hot_f * (count[:, :LANES] + before), 0, keepdims=True))
        before = before + count[:, LANES:]
    rank = jnp.concatenate(ranks, 1).astype(jnp.int32)
    owner = (ids >> 6) * NQ + (ids & (NQ - 1))
    place = ((ids >> 5) & 1) * 8 + rank
    meta_ref[0:1, :] = owner
    meta_ref[1:2, :] = place
    here = iota((SLOT, NV), 0) == place
    picked = jnp.where(
        iota((NV // VIS_BLOCK, NV), 1) // VIS_BLOCK == iota((NV // VIS_BLOCK, NV), 0),
        clip_ref[...].astype(F32) * 0.25, 0.0,
    )
    level = jnp.sum(picked, 0, keepdims=True)
    values = [pos_ref[0:1, :], pos_ref[1:2, :], obs_ref[0:1, :], obs_ref[1:2, :], level]
    pieces = [split3(v) for v in values]
    own = jnp.where(iota((NDEV, NV), 0) == owner, 1.0, 0.0).astype(BF)
    zeros = jnp.zeros((LANES - 5 * SLOT, NV), BF)
    for part in range(3):
        table = jnp.concatenate(
            [jnp.where(here, p[part].astype(F32), 0.0).astype(BF) for p in pieces] + [zeros], 0
        )
        extra[pl.ds(part, NDEV, stride=8), :] = lax.dot_general(
            own, table, (((1,), (1,)), ((), ())), preferred_element_type=F32
        )
    row_offset = off_ref[0, 0]
    extra[pl.ds(3, NDEV, stride=8), :] = jnp.full((NDEV, LANES), row_offset >> 8, jnp.int32).astype(F32)
    extra[pl.ds(4, NDEV, stride=8), :] = jnp.full((NDEV, LANES), row_offset & 255, jnp.int32).astype(F32)
    for i in range(5, 8):
        extra[pl.ds(i, NDEV, stride=8), :] = jnp.zeros((NDEV, LANES), F32)
    msg_ref[:, RD:ROWS_MSG, :] = extra[...].astype(BF).reshape(NDEV, 8, LANES)


def powers(turn):
    sub = iota((8, LANES), 0).astype(F32)
    low = sincos_turn(turn * sub)
    high = sincos_turn(turn * (sub * 8.0))
    re, im = [], []
    for a in range(8):
        hr, hi = high[0][a:a + 1, :], high[1][a:a + 1, :]
        re.append(hr * low[0] - hi * low[1])
        im.append(hr * low[1] + hi * low[0])
    return jnp.concatenate(re, 0), jnp.concatenate(im, 0)


def owner_kernel(
    facet_ref, got_ref, fwd_ref, adj_ref, msg_ref, extra, left, right, inner, phasor, basis,
):
    sign = lane_sign(2 * SUBG)
    extra[...] = got_ref[:, RD:ROWS_MSG, :].astype(F32).reshape(NDEV * 8, LANES)
    row = iota((2 * SUBG, LANES), 0)
    k_row = (facet_ref[0] * 2 + row // SUBG) * (N_IMG // 8) + (row & (SUBG - 1))
    lane = iota((1, LANES), 1)
    offset = jnp.zeros((1, LANES), F32)
    for f in range(NF):
        at = f * NQ * 8
        value = extra[at + 3:at + 4, :] * 256.0 + extra[at + 4:at + 5, :]
        offset = jnp.where(lane == f, value, offset)
    rho_c, rho_s = phase_of(offset.astype(jnp.int32), k_row)
    real = jnp.zeros((2 * SUBG, LANES), F32)
    turned = jnp.zeros((2 * SUBG, LANES), F32)
    for f in range(NF):
        spectra = got_ref[f * NQ:(f + 1) * NQ, 0:RD, :].reshape(NQ * RD, LANES)
        both = jnp.dot(fwd_ref[0], spectra, preferred_element_type=F32)
        rc, rs = rho_c[:, f:f + 1], rho_s[:, f:f + 1]
        first, second = both[:2 * SUBG], both[2 * SUBG:]
        real = real + (rc * first + rs * second)
        turned = turned + (rc * second - rs * first)
    subgrids = (real - swap(turned) * sign).astype(BF).astype(F32)

    got = (
        extra[pl.ds(0, NDEV, stride=8), :]
        + extra[pl.ds(1, NDEV, stride=8), :]
        + extra[pl.ds(2, NDEV, stride=8), :]
    ).T
    sums = []
    returned = [[None, None], [None, None]]
    for l in range(2):
        def rows_of(c):
            return got[c * SLOT + l * 8:c * SLOT + l * 8 + 8, :]

        u, w, obs_r, obs_i, level = [rows_of(c) for c in range(5)]
        u, w = u * (1.0 / SUBG), w * (1.0 / SUBG)
        for k in range(8):
            at = slice(k * LANES, (k + 1) * LANES)
            cr, ci = powers(w[k:k + 1, :])
            basis[0:SUBG, at] = (cr * 0.125).astype(BF)
            basis[SUBG:, at] = (ci * 0.125).astype(BF)
        sub = subgrids[l * SUBG:(l + 1) * SUBG]
        matrix = jnp.concatenate([sub * sign[:SUBG], swap(sub)], 0).astype(BF)
        inner[...] = jnp.dot(matrix, basis[...], preferred_element_type=F32)
        pred_r, pred_i = [], []
        for k in range(8):
            at = slice(k * LANES, (k + 1) * LANES)
            lr, li = powers(u[k:k + 1, :])
            lr, li = lr * 0.125, li * 0.125
            left[0:SUBG, at] = lr
            left[SUBG:, at] = li
            ir, ii = inner[0:SUBG, at], inner[SUBG:, at]
            pred_r.append(jnp.sum(lr * ir - li * ii, 0, keepdims=True))
            pred_i.append(jnp.sum(lr * ii + li * ir, 0, keepdims=True))
        mis_r = obs_r - jnp.concatenate(pred_r, 0)
        mis_i = obs_i - jnp.concatenate(pred_i, 0)
        live = level > 0.0
        threshold = jnp.where(live, level, 1.0)
        magnitude = jnp.sqrt(mis_r * mis_r + mis_i * mis_i)
        weight = jnp.where(live, threshold / jnp.maximum(magnitude, threshold), 0.0)
        wr, wi = weight * mis_r, weight * mis_i
        returned[0][l], returned[1][l] = wr, wi
        for k in range(8):
            at = slice(k * LANES, (k + 1) * LANES)
            lr, li = left[0:SUBG, at], left[SUBG:, at]
            vr, vi = wr[k:k + 1, :], wi[k:k + 1, :]
            phasor[0:SUBG, at] = (lr * vr + li * vi).astype(BF)
            phasor[SUBG:, at] = (lr * vi - li * vr).astype(BF)
        product = lax.dot_general(
            phasor[...], basis[...], (((1,), (1,)), ((), ())), preferred_element_type=F32
        )
        sums.append(product[:SUBG] * sign[:SUBG] + swap(product[SUBG:]))
    corrected = jnp.concatenate(sums, 0)
    corrected = corrected.astype(BF).astype(F32)
    cols = []
    for f in range(NF):
        rc, rs = rho_c[:, f:f + 1], rho_s[:, f:f + 1]
        d = corrected * rc - swap(corrected) * (sign * rs)
        cols.append(jnp.concatenate([d, swap(d) * sign], 0).astype(BF))
    images = jnp.dot(adj_ref[0], jnp.concatenate(cols, 1), preferred_element_type=F32)
    for f in range(NF):
        msg_ref[f * NQ:(f + 1) * NQ, 0:RD, :] = (
            images[:, f * LANES:(f + 1) * LANES].astype(BF).reshape(NQ, RD, LANES)
        )
    back = jnp.concatenate(
        [returned[0][0], returned[0][1], returned[1][0], returned[1][1],
         jnp.zeros((LANES - 2 * SLOT, LANES), F32)], 0
    ).T
    for i, part in enumerate(split3(back)):
        extra[pl.ds(i, NDEV, stride=8), :] = part.astype(F32)
    msg_ref[:, RD:ROWS_MSG, :] = extra[...].astype(BF).reshape(NDEV, 8, LANES)


def facet_kernel(
    off_ref, got_ref, meta_ref, coarse_ref, tw_ref, col_ref, out_ref, res_ref, rows, extra, flat,
):
    freq = iota((NQ, LANES), 0) * (N_IMG // NQ) + (iota((NQ, LANES), 1) & (SUBG - 1))
    ph_c, ph_s = phase_of(off_ref[0, 1], freq)
    ph_s = -ph_s * lane_sign(NQ)
    for q in range(NQ):
        image = got_ref[q, 0:RD, :].astype(F32)
        for f in range(1, NF):
            image = image + got_ref[f * NQ + q, 0:RD, :].astype(F32)
        rows[q * RD:(q + 1) * RD, :] = image * ph_c[q:q + 1, :] + swap(image) * ph_s[q:q + 1, :]
    tw_c, tw_s = tw_ref[0], tw_ref[1]
    sign = lane_sign(LANES)
    group = 4
    for base in range(0, RD, group):
        image = jnp.concatenate(
            [rows[pl.ds(base + i, NQ, stride=RD), :].astype(BF) for i in range(group)], 1
        )
        spread = jnp.dot(coarse_ref[...], image, preferred_element_type=F32)
        stacked = []
        for i in range(group):
            first = spread[:LANES, i * LANES:(i + 1) * LANES]
            second = spread[LANES:, i * LANES:(i + 1) * LANES]
            z = (tw_c * first - tw_s * second) - swap(tw_s * first + tw_c * second) * sign
            stacked.append(z.astype(BF))
        out = lax.dot_general(
            col_ref[...], jnp.concatenate(stacked, 0), (((1,), (1,)), ((), ())),
            preferred_element_type=F32,
        )
        for i in range(group):
            r = base + i
            for part in range(2):
                at = (part * 2 + r // 8) * NA * 8 + r % 8
                flat[pl.ds(at, NA, stride=8), :] = out[
                    part * NA:(part + 1) * NA, i * LANES:(i + 1) * LANES
                ]
    for part in range(2):
        for half in range(2):
            for a in range(NA):
                at = ((part * 2 + half) * NA + a) * 8
                out_ref[0, part, half * 8:(half + 1) * 8, a * LANES:(a + 1) * LANES] = flat[at:at + 8, :]

    extra[...] = got_ref[:, RD:ROWS_MSG, :].astype(F32).reshape(NDEV * 8, LANES)
    back = (
        extra[pl.ds(0, NDEV, stride=8), :]
        + extra[pl.ds(1, NDEV, stride=8), :]
        + extra[pl.ds(2, NDEV, stride=8), :]
    ).T[:2 * SLOT]
    owner, place = meta_ref[0:1, :], meta_ref[1:2, :]
    own = jnp.where(iota((NDEV, NV), 0) == owner, 1.0, 0.0).astype(BF)
    found = jnp.dot(jnp.concatenate(split3(back), 0), own, preferred_element_type=F32)
    found = found[:2 * SLOT] + found[2 * SLOT:4 * SLOT] + found[4 * SLOT:]
    here = iota((SLOT, NV), 0) == place
    for c in range(2):
        res_ref[c:c + 1, :] = jnp.sum(
            jnp.where(here, found[c * SLOT:(c + 1) * SLOT], 0.0), 0, keepdims=True
        )


VMEM = pl.BlockSpec(memory_space=pltpu.VMEM)
SMEM = pl.BlockSpec(memory_space=pltpu.SMEM)
TABLES = host_tables()


def on_device(slab, offsets, position, observed, subgrid_of, clip):
    t = {name: jnp.asarray(value) for name, value in TABLES.items()}
    limit = pltpu.CompilerParams(vmem_limit_bytes=48 << 20)
    message = jax.ShapeDtypeStruct((NDEV, ROWS_MSG, LANES), BF)
    sent, meta = pl.pallas_call(
        send_kernel,
        out_shape=(message, jax.ShapeDtypeStruct((8, NV), jnp.int32)),
        in_specs=[SMEM] + [VMEM] * 8,
        out_specs=(VMEM, VMEM),
        scratch_shapes=[
            pltpu.VMEM((2, NA * RD, LANES), F32),
            pltpu.VMEM((NQ * RD, LANES), F32),
            pltpu.VMEM((NDEV * 8, LANES), F32),
        ],
        compiler_params=limit,
        name="send",
    )(
        offsets, slab, position, observed, subgrid_of.reshape(1, NV),
        clip.reshape(NV // VIS_BLOCK, 1), t["col_fwd"], t["tw_fwd"], t["coarse_fwd"],
    )
    got = lax.all_to_all(sent, ALL, split_axis=0, concat_axis=0, tiled=True)
    facet = lax.axis_index("facet").astype(jnp.int32).reshape(1)
    whole = lambda *shape: pl.BlockSpec(shape, lambda i, f: (0,) * len(shape))
    answer = pl.pallas_call(
        owner_kernel,
        out_shape=message,
        grid_spec=pltpu.PrefetchScalarGridSpec(
            num_scalar_prefetch=1,
            grid=(1,),
            in_specs=[
                whole(NDEV, ROWS_MSG, LANES),
                pl.BlockSpec((1, 4 * SUBG, NQ * RD), lambda i, f: (f[0], 0, 0)),
                pl.BlockSpec((1, NQ * RD, 4 * SUBG), lambda i, f: (f[0], 0, 0)),
            ],
            out_specs=whole(NDEV, ROWS_MSG, LANES),
            scratch_shapes=[
                pltpu.VMEM((NDEV * 8, LANES), F32),
                pltpu.VMEM((2 * SUBG, NV), F32),
                pltpu.VMEM((8, LANES), F32),
                pltpu.VMEM((2 * SUBG, NV), F32),
                pltpu.VMEM((2 * SUBG, NV), BF),
                pltpu.VMEM((2 * SUBG, NV), BF),
            ],
        ),
        compiler_params=limit,
        name="owner",
    )(facet, got, t["row_fwd"], t["row_adj"])
    back = lax.all_to_all(answer, ALL, split_axis=0, concat_axis=0, tiled=True)
    facet_adjoint, residual = pl.pallas_call(
        facet_kernel,
        out_shape=(
            jax.ShapeDtypeStruct((1, 2, RD, NA * LANES), F32),
            jax.ShapeDtypeStruct((2, NV), F32),
        ),
        in_specs=[SMEM] + [VMEM] * 5,
        out_specs=(VMEM, VMEM),
        scratch_shapes=[
            pltpu.VMEM((NQ * RD, LANES), F32),
            pltpu.VMEM((NDEV * 8, LANES), F32),
            pltpu.VMEM((4 * NA * 8, LANES), F32),
        ],
        compiler_params=limit,
        name="facet",
    )(offsets, back, meta, t["coarse_adj"], t["tw_adj"], t["col_adj"])
    return (facet_adjoint, residual)


def solution(mesh):
    placed = (
        P("facet", None, "sub", None),
        P("facet", None),
        P(None, ALL),
        P(None, ALL),
        P(ALL, None),
        P(ALL),
    )
    return jax.shard_map(
        on_device,
        mesh=mesh,
        in_specs=placed,
        out_specs=(P("facet", None, "sub", None), P(None, ALL)),
        check_vma=False,
    )
```

```python
import math

import jax
import jax.numpy as jnp
import numpy as np
from jax import lax
from jax.experimental import pallas as pl
from jax.experimental.pallas import tpu as pltpu
from jax.sharding import PartitionSpec as P

N_IMG = 32768
SUBG = 64
VIS_BLOCK = 32
LANES = 128
NQ = 32
NF = 4
NDEV = 128
RD = 16
NA = 64
NV = 1024
SLOT = 16
ROWS_MSG = 18
A_HIGH = 3 * 5 * SLOT
TWO_PI = 2.0 * math.pi
BF = jnp.bfloat16
F32 = jnp.float32
ALL = ("facet", "sub")


def unit(index, period):
    angle = TWO_PI * (np.asarray(index, np.int64) % period) / period
    return np.cos(angle), np.sin(angle)


def host_tables():
    block = np.arange(NA)
    lane = np.arange(LANES)
    fine = np.arange(SUBG)
    coarse = np.arange(NQ)
    c, s = unit(fine[:, None] * block[None, :], 256)
    c, s = c / 64.0, s / 64.0
    col_fwd = np.block([[c, s], [-s, c]])
    col_adj = np.block([[c.T, -s.T], [s.T, c.T]])
    tw_c, tw_s = unit(fine[:, None] * lane[None, :], N_IMG)
    twiddle_fwd = np.concatenate([tw_c, -tw_s], 0)
    twiddle_adj = np.stack([np.tile(tw_c.T, (1, 2)), np.tile(tw_s.T, (1, 2))])
    wc, ws = unit(coarse[:, None] * lane[None, :], 32)
    column = np.concatenate([col_fwd, wc, -ws], 0)
    coarse_adj = np.concatenate([wc.T, ws.T], 0)
    k_row = (np.arange(8)[:, None] * 4096 + fine[None, :]).reshape(NF, 2 * SUBG)
    rc, rs = unit(k_row[:, :, None] * np.arange(NQ * RD)[None, None, :], N_IMG)
    swapped = lambda x: x.reshape(NF, 2 * SUBG, NQ, RD).swapaxes(2, 3).reshape(x.shape) / 64.0
    rc, rs = swapped(rc), swapped(rs)
    row_fwd = np.concatenate([rc, -rs], 1)
    row_adj = np.ascontiguousarray(row_fwd.transpose(0, 2, 1))
    bf = lambda x: np.asarray(x, np.float32).astype(jnp.bfloat16)
    return dict(
        column=bf(column),
        col_adj=bf(col_adj),
        tw_fwd=np.asarray(twiddle_fwd, np.float32),
        tw_adj=np.asarray(twiddle_adj, np.float32),
        coarse_adj=bf(coarse_adj),
        row_fwd=bf(row_fwd),
        row_adj=bf(row_adj),
    )


def sincos_turn(turn):
    quarter = jnp.floor(turn * 4.0 + 0.5)
    y = (turn - quarter * 0.25) * TWO_PI
    y2 = y * y
    s = y * (1.0 + y2 * (-1.0 / 6 + y2 * (1.0 / 120 + y2 * (-1.0 / 5040 + y2 * (1.0 / 362880)))))
    c = 1.0 + y2 * (-0.5 + y2 * (1.0 / 24 + y2 * (-1.0 / 720 + y2 * (1.0 / 40320))))
    turns = quarter.astype(jnp.int32)
    odd = (turns & 1) == 1
    cos = jnp.where(odd, s, c)
    sin = jnp.where(odd, c, s)
    cos = jnp.where(((turns + 1) & 2) == 2, -cos, cos)
    sin = jnp.where((turns & 2) == 2, -sin, sin)
    return cos, sin


def phase_of(offset, frequency):
    index = (offset * frequency) & (N_IMG - 1)
    return sincos_turn(index.astype(F32) * (1.0 / N_IMG))


def swap(x):
    return pltpu.roll(x, SUBG, x.ndim - 1)


def iota(shape, dim):
    return lax.broadcasted_iota(jnp.int32, shape, dim)


def split3(x):
    high = x.astype(BF)
    rest = x - high.astype(F32)
    middle = rest.astype(BF)
    low = (rest - middle.astype(F32)).astype(BF)
    return high, middle, low


def lane_sign(rows):
    return jnp.where(iota((rows, LANES), 1) < SUBG, 1.0, -1.0).astype(F32)


def send_kernel(
    off_hbm, slab_hbm, pos_hbm, obs_hbm, ids_hbm, clip_hbm, table_hbm, tw_hbm,
    msg_ref, meta_ref, off_ref, slab_ref, pos_ref, obs_ref, ids_ref, clip_ref, table_ref, tw_ref,
    wide, flat, sems,
):
    pairs = [
        (ids_hbm, ids_ref), (clip_hbm, clip_ref), (pos_hbm, pos_ref), (obs_hbm, obs_ref),
        (off_hbm, off_ref), (slab_hbm, slab_ref), (table_hbm, table_ref), (tw_hbm, tw_ref),
    ]
    copies = [pltpu.make_async_copy(a, b, sems.at[i]) for i, (a, b) in enumerate(pairs)]
    for copy in copies:
        copy.start()

    copies[0].wait()
    ids = ids_ref[...]
    upper = jnp.where(iota((LANES, LANES), 0) < iota((LANES, LANES), 1), 1.0, 0.0).astype(BF)
    counter = jnp.concatenate([upper, jnp.ones((LANES, LANES), BF)], 1)
    before = jnp.zeros((2 * LANES, LANES), F32)
    ranks = []
    for b in range(NV // LANES):
        hot = iota((2 * LANES, LANES), 0) == ids[:, b * LANES:(b + 1) * LANES]
        hot_f = jnp.where(hot, 1.0, 0.0)
        count = jnp.dot(hot_f.astype(BF), counter, preferred_element_type=F32)
        ranks.append(jnp.sum(hot_f * (count[:, :LANES] + before), 0, keepdims=True))
        before = before + count[:, LANES:]
    rank = jnp.concatenate(ranks, 1).astype(jnp.int32)
    owner = (ids >> 6) * NQ + (ids & (NQ - 1))
    place = ((ids >> 5) & 1) * 8 + rank
    meta_ref[0:1, :] = owner
    meta_ref[1:2, :] = place
    here = iota((SLOT, NV), 0) == place
    copies[1].wait()
    n_block = NV // VIS_BLOCK
    clip = jnp.broadcast_to(clip_ref[...].astype(F32) * 0.25, (n_block, n_block))
    same = iota((n_block, n_block), 0) == iota((n_block, n_block), 1)
    clip = jnp.sum(jnp.where(same, clip, 0.0), 1, keepdims=True)
    block = iota((n_block, NV), 1) // VIS_BLOCK == iota((n_block, NV), 0)
    level = jnp.sum(jnp.where(block, clip, 0.0), 0, keepdims=True)
    copies[2].wait()
    copies[3].wait()
    values = [pos_ref[0:1, :], pos_ref[1:2, :], obs_ref[0:1, :], obs_ref[1:2, :], level]
    pieces = [split3(v) for v in values]
    own = jnp.where(iota((NDEV, NV), 0) == owner, 1.0, 0.0).astype(BF)
    table = jnp.concatenate(
        [jnp.where(here, p[part].astype(F32), 0.0).astype(BF) for part in range(3) for p in pieces]
        + [jnp.zeros((SLOT, NV), BF)], 0
    )
    copies[4].wait()
    meta_ref[2:3, :] = jnp.full((1, NV), off_ref[0, 1], jnp.int32)
    payload = lax.dot_general(own, table, (((1,), (1,)), ((), ())), preferred_element_type=F32)
    lane = iota((NDEV, LANES), 1)
    tail = payload[:, LANES:]
    tail = jnp.where(lane == A_HIGH - LANES, (off_ref[0, 0] >> 8).astype(F32), tail)
    tail = jnp.where(lane == A_HIGH + 1 - LANES, (off_ref[0, 0] & 255).astype(F32), tail)
    flat[pl.ds(RD, NDEV, stride=ROWS_MSG), :] = payload[:, :LANES]
    flat[pl.ds(RD + 1, NDEV, stride=ROWS_MSG), :] = tail

    freq = iota((NQ, LANES), 0) * (N_IMG // NQ) + (iota((NQ, LANES), 1) & (SUBG - 1))
    ph_c, ph_s = phase_of(off_ref[0, 1], freq)
    ph_s = ph_s * lane_sign(NQ)
    for copy in copies[5:]:
        copy.wait()
    for part in range(2):
        for a in range(NA):
            wide[part, a * RD:(a + 1) * RD, :] = slab_ref[
                0, part, :, a * LANES:(a + 1) * LANES
            ].astype(F32)
    tw_c, tw_s = tw_ref[:SUBG], tw_ref[SUBG:]
    col = table_ref[:LANES]
    coarse = jnp.concatenate([table_ref[LANES:LANES + NQ], table_ref[LANES + NQ:]], 1)
    group = 4
    for base in range(0, RD, group):
        cols = []
        for r in range(base, base + group):
            cols.append(
                jnp.concatenate(
                    [wide[0, pl.ds(r, NA, stride=RD), :], wide[1, pl.ds(r, NA, stride=RD), :]], 0
                ).astype(BF)
            )
        y = jnp.dot(col, jnp.concatenate(cols, 1), preferred_element_type=F32)
        stacked = []
        for i in range(group):
            yr = y[:SUBG, i * LANES:(i + 1) * LANES]
            yi = y[SUBG:, i * LANES:(i + 1) * LANES]
            zr = yr * tw_c - yi * tw_s
            zi = yr * tw_s + yi * tw_c
            stacked.append(jnp.concatenate([zr, -zi], 1).astype(BF))
            stacked.append(jnp.concatenate([zi, zr], 1).astype(BF))
        out = lax.dot_general(
            coarse, jnp.concatenate(stacked, 0), (((1,), (1,)), ((), ())),
            preferred_element_type=F32,
        )
        for i in range(group):
            piece = out[:, i * LANES:(i + 1) * LANES]
            piece = piece * ph_c + swap(piece) * ph_s
            for f in range(NF):
                flat[pl.ds(f * NQ * ROWS_MSG + base + i, NQ, stride=ROWS_MSG), :] = piece
    msg_ref[...] = flat[...].astype(BF)


def powers(turn):
    sub = iota((8, LANES), 0).astype(F32)
    low = sincos_turn(turn * sub)
    high = sincos_turn(turn * (sub * 8.0))
    re, im = [], []
    for a in range(8):
        hr, hi = high[0][a:a + 1, :], high[1][a:a + 1, :]
        re.append(hr * low[0] - hi * low[1])
        im.append(hr * low[1] + hi * low[0])
    return jnp.concatenate(re, 0), jnp.concatenate(im, 0)


def owner_kernel(
    got_ref, fwd_hbm, adj_hbm, msg_ref, fwd_ref, adj_ref, flat, left, inner, phasor, basis, sems,
):
    facet = lax.axis_index("facet")
    tables = [
        pltpu.make_async_copy(fwd_hbm.at[facet], fwd_ref, sems.at[0]),
        pltpu.make_async_copy(adj_hbm.at[facet], adj_ref, sems.at[1]),
    ]
    for copy in tables:
        copy.start()
    sign = lane_sign(2 * SUBG)
    flat[...] = got_ref[...].astype(F32)
    got = jnp.concatenate(
        [flat[pl.ds(RD, NDEV, stride=ROWS_MSG), :].T, flat[pl.ds(RD + 1, NDEV, stride=ROWS_MSG), :].T], 0
    )
    row = iota((2 * SUBG, LANES), 0)
    k_row = (facet * 2 + row // SUBG) * (N_IMG // 8) + (row & (SUBG - 1))
    offset = got[A_HIGH:A_HIGH + 1] * 256.0 + got[A_HIGH + 1:A_HIGH + 2]
    rho_c, rho_s = phase_of(offset.astype(jnp.int32), k_row)
    n = 5 * SLOT
    got = got[:n] + got[n:2 * n] + got[2 * n:3 * n]

    def rows_of(c, l):
        return got[c * SLOT + l * 8:c * SLOT + l * 8 + 8, :]

    for l in range(2):
        u, w = rows_of(0, l) * (1.0 / SUBG), rows_of(1, l) * (1.0 / SUBG)
        for k in range(8):
            at = slice(k * LANES, (k + 1) * LANES)
            cr, ci = powers(w[k:k + 1, :])
            basis[l, 0:SUBG, at] = (cr * 0.125).astype(BF)
            basis[l, SUBG:, at] = (ci * 0.125).astype(BF)
            lr, li = powers(u[k:k + 1, :])
            left[l, 0:SUBG, at] = lr * 0.125
            left[l, SUBG:, at] = li * 0.125

    tables[0].wait()
    real = jnp.zeros((2 * SUBG, LANES), F32)
    turned = jnp.zeros((2 * SUBG, LANES), F32)
    for f in range(NF):
        spectra = jnp.concatenate(
            [
                flat[pl.ds(f * NQ * ROWS_MSG + r, NQ, stride=ROWS_MSG), :].astype(BF)
                for r in range(RD)
            ], 0
        )
        both = jnp.dot(fwd_ref[...], spectra, preferred_element_type=F32)
        rc, rs = rho_c[:, f * NQ:f * NQ + 1], rho_s[:, f * NQ:f * NQ + 1]
        first, second = both[:2 * SUBG], both[2 * SUBG:]
        real = real + (rc * first + rs * second)
        turned = turned + (rc * second - rs * first)
    subgrids = (real - swap(turned) * sign).astype(BF).astype(F32)

    sums = []
    returned = [[None, None], [None, None]]
    for l in range(2):
        obs_r, obs_i, level = [rows_of(c, l) for c in range(2, 5)]
        sub = subgrids[l * SUBG:(l + 1) * SUBG]
        matrix = jnp.concatenate([sub * sign[:SUBG], swap(sub)], 0).astype(BF)
        inner[l] = jnp.dot(matrix, basis[l], preferred_element_type=F32)
        pred_r, pred_i = [], []
        for k in range(8):
            at = slice(k * LANES, (k + 1) * LANES)
            lr, li = left[l, 0:SUBG, at], left[l, SUBG:, at]
            ir, ii = inner[l, 0:SUBG, at], inner[l, SUBG:, at]
            pred_r.append(jnp.sum(lr * ir - li * ii, 0, keepdims=True))
            pred_i.append(jnp.sum(lr * ii + li * ir, 0, keepdims=True))
        mis_r = obs_r - jnp.concatenate(pred_r, 0)
        mis_i = obs_i - jnp.concatenate(pred_i, 0)
        live = level > 0.0
        threshold = jnp.where(live, level, 1.0)
        magnitude = jnp.sqrt(mis_r * mis_r + mis_i * mis_i)
        weight = jnp.where(live, threshold / jnp.maximum(magnitude, threshold), 0.0)
        wr, wi = weight * mis_r, weight * mis_i
        returned[0][l], returned[1][l] = wr, wi
        for k in range(8):
            at = slice(k * LANES, (k + 1) * LANES)
            lr, li = left[l, 0:SUBG, at], left[l, SUBG:, at]
            vr, vi = wr[k:k + 1, :], wi[k:k + 1, :]
            phasor[l, 0:SUBG, at] = (lr * vr + li * vi).astype(BF)
            phasor[l, SUBG:, at] = (lr * vi - li * vr).astype(BF)
        product = lax.dot_general(
            phasor[l], basis[l], (((1,), (1,)), ((), ())), preferred_element_type=F32
        )
        sums.append(product[:SUBG] * sign[:SUBG] + swap(product[SUBG:]))
    corrected = jnp.concatenate(sums, 0)
    corrected = corrected.astype(BF).astype(F32)
    cols = []
    for f in range(NF):
        rc, rs = rho_c[:, f * NQ:f * NQ + 1], rho_s[:, f * NQ:f * NQ + 1]
        d = corrected * rc - swap(corrected) * (sign * rs)
        cols.append(jnp.concatenate([d, swap(d) * sign], 0).astype(BF))
    tables[1].wait()
    images = jnp.dot(adj_ref[...], jnp.concatenate(cols, 1), preferred_element_type=F32)
    for f in range(NF):
        for r in range(RD):
            flat[pl.ds(f * NQ * ROWS_MSG + r, NQ, stride=ROWS_MSG), :] = images[
                r * NQ:(r + 1) * NQ, f * LANES:(f + 1) * LANES
            ]
    back = jnp.concatenate([returned[0][0], returned[0][1], returned[1][0], returned[1][1]], 0)
    back = [part.astype(F32) for part in split3(back)]
    back = jnp.concatenate(back + [jnp.zeros((2 * SLOT, LANES), F32)], 0).T
    flat[pl.ds(RD, NDEV, stride=ROWS_MSG), :] = back
    flat[pl.ds(RD + 1, NDEV, stride=ROWS_MSG), :] = jnp.zeros((NDEV, LANES), F32)
    msg_ref[...] = flat[...].astype(BF)


def facet_kernel(
    got_ref, meta_ref, coarse_ref, tw_ref, col_ref, out_hbm, res_ref, flat, turned, out_ref, sems,
):
    flat[...] = got_ref[...].astype(F32)
    freq = iota((NQ, LANES), 0) * (N_IMG // NQ) + (iota((NQ, LANES), 1) & (SUBG - 1))
    ph_c, ph_s = phase_of(meta_ref[2:3, :LANES], freq)
    ph_s = -ph_s * lane_sign(NQ)
    tw_c, tw_s = tw_ref[0], tw_ref[1]
    sign = lane_sign(LANES)
    group = 4
    copies = []
    for base in range(0, RD, group):
        images = []
        for r in range(base, base + group):
            image = flat[pl.ds(r, NQ, stride=ROWS_MSG), :]
            for f in range(1, NF):
                image = image + flat[pl.ds(f * NQ * ROWS_MSG + r, NQ, stride=ROWS_MSG), :]
            images.append((image * ph_c + swap(image) * ph_s).astype(BF))
        spread = jnp.dot(coarse_ref[...], jnp.concatenate(images, 1), preferred_element_type=F32)
        stacked = []
        for i in range(group):
            first = spread[:LANES, i * LANES:(i + 1) * LANES]
            second = spread[LANES:, i * LANES:(i + 1) * LANES]
            z = (tw_c * first - tw_s * second) - swap(tw_s * first + tw_c * second) * sign
            stacked.append(z.astype(BF))
        out = lax.dot_general(
            col_ref[...], jnp.concatenate(stacked, 0), (((1,), (1,)), ((), ())),
            preferred_element_type=F32,
        )
        for i in range(group):
            r = base + i
            for part in range(2):
                at = (part * 2 + r // 8) * NA * 8 + r % 8
                turned[pl.ds(at, NA, stride=8), :] = out[
                    part * NA:(part + 1) * NA, i * LANES:(i + 1) * LANES
                ]
        if (base + group) % 8 == 0:
            half = base // 8
            for part in range(2):
                where = slice(half * 8, half * 8 + 8)
                for a in range(NA):
                    at = ((part * 2 + half) * NA + a) * 8
                    out_ref[part, where, a * LANES:(a + 1) * LANES] = turned[at:at + 8, :]
                copy = pltpu.make_async_copy(
                    out_ref.at[part, where, :], out_hbm.at[0, part, where, :],
                    sems.at[half * 2 + part],
                )
                copy.start()
                copies.append(copy)

    n = 2 * SLOT
    back = flat[pl.ds(RD, NDEV, stride=ROWS_MSG), :].T[:3 * n]
    owner, place = meta_ref[0:1, :], meta_ref[1:2, :]
    own = jnp.where(iota((NDEV, NV), 0) == owner, 1.0, 0.0).astype(BF)
    found = jnp.dot(back.astype(BF), own, preferred_element_type=F32)
    found = found[:n] + found[n:2 * n] + found[2 * n:]
    here = iota((SLOT, NV), 0) == place
    for c in range(2):
        res_ref[c:c + 1, :] = jnp.sum(
            jnp.where(here, found[c * SLOT:(c + 1) * SLOT], 0.0), 0, keepdims=True
        )
    for copy in copies:
        copy.wait()


VMEM = pl.BlockSpec(memory_space=pltpu.VMEM)
HBM = pl.BlockSpec(memory_space=pltpu.MemorySpace.HBM)
TABLES = host_tables()


def in_place(arrays):
    return [pltpu.with_memory_space_constraint(x, pltpu.HBM) for x in arrays]


def exchange(message):
    pairs = message.reshape(NDEV * ROWS_MSG // 2, 2, LANES)
    return lax.all_to_all(pairs, ALL, split_axis=0, concat_axis=0, tiled=True).reshape(message.shape)


def on_device(slab, offsets, position, observed, subgrid_of, clip):
    t = {name: jnp.asarray(value) for name, value in TABLES.items()}
    limit = pltpu.CompilerParams(vmem_limit_bytes=32 << 20)
    message = jax.ShapeDtypeStruct((NDEV * ROWS_MSG, LANES), BF)
    flat = pltpu.VMEM((NDEV * ROWS_MSG, LANES), F32)
    inputs = (
        offsets, slab, position, observed, subgrid_of.reshape(1, NV),
        clip.reshape(1, NV // VIS_BLOCK), t["column"], t["tw_fwd"],
    )
    sent, meta = pl.pallas_call(
        send_kernel,
        out_shape=(message, jax.ShapeDtypeStruct((8, NV), jnp.int32)),
        in_specs=[HBM] * len(inputs),
        out_specs=(VMEM, VMEM),
        scratch_shapes=[pltpu.SMEM((1, 2), jnp.int32)]
        + [pltpu.VMEM(x.shape, x.dtype) for x in inputs[1:]]
        + [
            pltpu.VMEM((2, NA * RD, LANES), F32),
            flat,
            pltpu.SemaphoreType.DMA((len(inputs),)),
        ],
        compiler_params=limit,
        name="send",
    )(*in_place(inputs))
    got = exchange(sent)
    answer = pl.pallas_call(
        owner_kernel,
        out_shape=message,
        in_specs=[VMEM, HBM, HBM],
        out_specs=VMEM,
        scratch_shapes=[
            pltpu.VMEM((4 * SUBG, NQ * RD), BF),
            pltpu.VMEM((NQ * RD, 4 * SUBG), BF),
            flat,
            pltpu.VMEM((2, 2 * SUBG, NV), F32),
            pltpu.VMEM((2, 2 * SUBG, NV), F32),
            pltpu.VMEM((2, 2 * SUBG, NV), BF),
            pltpu.VMEM((2, 2 * SUBG, NV), BF),
            pltpu.SemaphoreType.DMA((2,)),
        ],
        compiler_params=limit,
        name="owner",
    )(got, *in_place((t["row_fwd"], t["row_adj"])))
    back = exchange(answer)
    facet_adjoint, residual = pl.pallas_call(
        facet_kernel,
        out_shape=(
            jax.ShapeDtypeStruct((1, 2, RD, NA * LANES), F32),
            jax.ShapeDtypeStruct((2, NV), F32),
        ),
        in_specs=[VMEM] * 5,
        out_specs=(HBM, VMEM),
        scratch_shapes=[
            flat,
            pltpu.VMEM((4 * NA * 8, LANES), F32),
            pltpu.VMEM((2, RD, NA * LANES), F32),
            pltpu.SemaphoreType.DMA((4,)),
        ],
        compiler_params=limit,
        name="facet",
    )(back, meta, t["coarse_adj"], t["tw_adj"], t["col_adj"])
    return (facet_adjoint, residual)


def solution(mesh):
    placed = (
        P("facet", None, "sub", None),
        P("facet", None),
        P(None, ALL),
        P(None, ALL),
        P(ALL, None),
        P(ALL),
    )
    return jax.shard_map(
        on_device,
        mesh=mesh,
        in_specs=placed,
        out_specs=(P("facet", None, "sub", None), P(None, ALL)),
        check_vma=False,
    )
```

```python
import math

import jax
import jax.numpy as jnp
import numpy as np
from jax import lax
from jax.experimental import pallas as pl
from jax.experimental.pallas import tpu as pltpu
from jax.sharding import PartitionSpec as P

N_IMG = 32768
SUBG = 64
HALF = 32
VIS_BLOCK = 32
LANES = 128
NQ = 32
NF = 4
NDEV = 128
RD = 16
NR2 = 8
NA = 64
NV = 1024
SLOT = 16
MSG = 10
A_HIGH = 3 * 5 * SLOT
TWO_PI = 2.0 * math.pi
BF = jnp.bfloat16
F32 = jnp.float32
ALL = ("facet", "sub")


def unit(index, period):
    angle = TWO_PI * (np.asarray(index, np.int64) % period) / period
    return np.cos(angle), np.sin(angle)


def host_tables():
    block = np.arange(NA)
    lane = np.arange(LANES)
    fine = np.arange(SUBG)
    coarse = np.arange(NQ)
    c, s = unit(fine[:, None] * block[None, :], 256)
    c, s = c / 64.0, s / 64.0
    col_fwd = np.block([[c, s], [-s, c]])
    col_adj = np.block([[c.T, -s.T], [s.T, c.T]])
    tw_c, tw_s = unit(fine[:, None] * lane[None, :], N_IMG)
    twiddle_fwd = np.concatenate([tw_c, -tw_s], 0)
    twiddle_adj = np.stack([np.tile(tw_c.T, (1, 2)), np.tile(tw_s.T, (1, 2))])
    wc, ws = unit(coarse[:, None] * lane[None, :], 32)
    column = np.concatenate([col_fwd, wc, ws, -ws, wc], 0)
    coarse_adj = np.concatenate([wc.T, ws.T], 0)
    k_row = (np.arange(8)[:, None] * 4096 + fine[None, :]).reshape(2, 4 * SUBG)
    r = np.arange(NQ * RD).reshape(NQ, 2, NR2).transpose(1, 2, 0).reshape(-1)
    rc, rs = unit(k_row[:, :, None] * r[None, None, :], N_IMG)
    row_fwd = np.concatenate([rc, -rs], 1) / 64.0
    row_adj = np.ascontiguousarray(row_fwd.transpose(0, 2, 1))
    bf = lambda x: np.asarray(x, np.float32).astype(jnp.bfloat16)
    return dict(
        column=bf(column),
        col_adj=bf(col_adj),
        tw_fwd=np.asarray(twiddle_fwd, np.float32),
        tw_adj=np.asarray(twiddle_adj, np.float32),
        coarse_adj=bf(coarse_adj),
        row_fwd=bf(row_fwd),
        row_adj=bf(row_adj),
    )


def sincos_turn(turn):
    quarter = jnp.floor(turn * 4.0 + 0.5)
    y = (turn - quarter * 0.25) * TWO_PI
    y2 = y * y
    s = y * (1.0 + y2 * (-1.0 / 6 + y2 * (1.0 / 120 + y2 * (-1.0 / 5040 + y2 * (1.0 / 362880)))))
    c = 1.0 + y2 * (-0.5 + y2 * (1.0 / 24 + y2 * (-1.0 / 720 + y2 * (1.0 / 40320))))
    turns = quarter.astype(jnp.int32)
    odd = (turns & 1) == 1
    cos = jnp.where(odd, s, c)
    sin = jnp.where(odd, c, s)
    cos = jnp.where(((turns + 1) & 2) == 2, -cos, cos)
    sin = jnp.where((turns & 2) == 2, -sin, sin)
    return cos, sin


def phase_of(offset, frequency):
    index = (offset * frequency) & (N_IMG - 1)
    return sincos_turn(index.astype(F32) * (1.0 / N_IMG))


def iota(shape, dim):
    return lax.broadcasted_iota(jnp.int32, shape, dim)


def roll(x, shift):
    return pltpu.roll(x, shift, x.ndim - 1)


def lane_sign(rows, width):
    return jnp.where((iota((rows, LANES), 1) & width) == 0, 1.0, -1.0).astype(F32)


def lower(shape):
    return iota(shape, len(shape) - 1) < SUBG


def split3(x):
    high = x.astype(BF)
    rest = x - high.astype(F32)
    middle = rest.astype(BF)
    low = (rest - middle.astype(F32)).astype(BF)
    return high, middle, low


def send_kernel(
    off_hbm, slab_hbm, pos_hbm, obs_hbm, ids_hbm, clip_hbm, table_hbm, tw_hbm, fwd_hbm, adj_hbm,
    msg_ref, meta_ref, fwd_ref, adj_ref, off_ref, slab_ref, pos_ref, obs_ref, ids_ref, clip_ref, table_ref, tw_ref,
    wide, flat, sems,
):
    pairs = [
        (ids_hbm, ids_ref), (clip_hbm, clip_ref), (pos_hbm, pos_ref), (obs_hbm, obs_ref),
        (off_hbm, off_ref), (slab_hbm, slab_ref), (table_hbm, table_ref), (tw_hbm, tw_ref),
    ]
    copies = [pltpu.make_async_copy(a, b, sems.at[i]) for i, (a, b) in enumerate(pairs)]
    four = lax.axis_index("facet") // 2
    later = [
        pltpu.make_async_copy(fwd_hbm.at[four], fwd_ref, sems.at[len(pairs)]),
        pltpu.make_async_copy(adj_hbm.at[four], adj_ref, sems.at[len(pairs) + 1]),
    ]
    for copy in copies + later:
        copy.start()

    copies[0].wait()
    ids = ids_ref[...]
    upper = jnp.where(iota((LANES, LANES), 0) < iota((LANES, LANES), 1), 1.0, 0.0).astype(BF)
    counter = jnp.concatenate([upper, jnp.ones((LANES, LANES), BF)], 1)
    before = jnp.zeros((2 * LANES, LANES), F32)
    ranks = []
    for b in range(NV // LANES):
        hot = iota((2 * LANES, LANES), 0) == ids[:, b * LANES:(b + 1) * LANES]
        hot_f = jnp.where(hot, 1.0, 0.0)
        count = jnp.dot(hot_f.astype(BF), counter, preferred_element_type=F32)
        ranks.append(jnp.sum(hot_f * (count[:, :LANES] + before), 0, keepdims=True))
        before = before + count[:, LANES:]
    rank = jnp.concatenate(ranks, 1).astype(jnp.int32)
    owner = (ids >> 7) * (2 * NQ) + (ids & (NQ - 1)) * 2 + ((ids >> 6) & 1)
    place = ((ids >> 5) & 1) * 8 + rank
    meta_ref[0:1, :] = owner
    meta_ref[1:2, :] = place
    here = iota((SLOT, NV), 0) == place
    copies[1].wait()
    n_block = NV // VIS_BLOCK
    clip = jnp.broadcast_to(clip_ref[...].astype(F32) * 0.25, (n_block, n_block))
    same = iota((n_block, n_block), 0) == iota((n_block, n_block), 1)
    clip = jnp.sum(jnp.where(same, clip, 0.0), 1, keepdims=True)
    block = iota((n_block, NV), 1) // VIS_BLOCK == iota((n_block, NV), 0)
    level = jnp.sum(jnp.where(block, clip, 0.0), 0, keepdims=True)
    copies[2].wait()
    copies[3].wait()
    values = [pos_ref[0:1, :], pos_ref[1:2, :], obs_ref[0:1, :], obs_ref[1:2, :], level]
    pieces = [split3(v) for v in values]
    own = jnp.where(iota((NDEV, NV), 0) == owner, 1.0, 0.0).astype(BF)
    table = jnp.concatenate(
        [jnp.where(here, p[part].astype(F32), 0.0).astype(BF) for part in range(3) for p in pieces]
        + [jnp.zeros((SLOT, NV), BF)], 0
    )
    copies[4].wait()
    meta_ref[2:3, :] = jnp.full((1, NV), off_ref[0, 1], jnp.int32)
    payload = lax.dot_general(own, table, (((1,), (1,)), ((), ())), preferred_element_type=F32)
    lane = iota((NDEV, LANES), 1)
    tail = payload[:, LANES:]
    tail = jnp.where(lane == A_HIGH - LANES, (off_ref[0, 0] >> 8).astype(F32), tail)
    tail = jnp.where(lane == A_HIGH + 1 - LANES, (off_ref[0, 0] & 255).astype(F32), tail)
    flat[pl.ds(NR2, NDEV, stride=MSG), :] = payload[:, :LANES]
    flat[pl.ds(NR2 + 1, NDEV, stride=MSG), :] = tail

    lane1 = iota((NQ, LANES), 1)
    phases = []
    for c in range(2):
        freq = iota((NQ, LANES), 0) * (N_IMG // NQ) + (lane1 & (HALF - 1)) + c * HALF
        phases.append(phase_of(off_ref[0, 1], freq))
    for copy in copies[5:]:
        copy.wait()
    for part in range(2):
        for a in range(NA):
            wide[part, a * RD:(a + 1) * RD, :] = slab_ref[
                0, part, :, a * LANES:(a + 1) * LANES
            ].astype(F32)
    tw_c, tw_s = tw_ref[:SUBG], tw_ref[SUBG:]
    col = table_ref[:LANES]
    coarse = jnp.concatenate(
        [
            jnp.concatenate([table_ref[LANES:LANES + NQ], table_ref[LANES + 2 * NQ:LANES + 3 * NQ]], 1),
            jnp.concatenate([table_ref[LANES + NQ:LANES + 2 * NQ], table_ref[LANES + 3 * NQ:]], 1),
        ], 0
    )
    for base in range(0, NR2, 2):
        which = [base, base + NR2, base + 1, base + 1 + NR2]
        cols = [
            jnp.concatenate(
                [wide[0, pl.ds(r, NA, stride=RD), :], wide[1, pl.ds(r, NA, stride=RD), :]], 0
            ).astype(BF)
            for r in which
        ]
        y = jnp.dot(col, jnp.concatenate(cols, 1), preferred_element_type=F32)
        real, imag = [], []
        for i in range(4):
            yr = y[:SUBG, i * LANES:(i + 1) * LANES]
            yi = y[SUBG:, i * LANES:(i + 1) * LANES]
            zr = yr * tw_c - yi * tw_s
            zi = yr * tw_s + yi * tw_c
            real.append(jnp.concatenate([zr, -zi], 1).astype(BF))
            imag.append(jnp.concatenate([zi, zr], 1).astype(BF))
        stacked = []
        for pair in range(2):
            for c in range(2):
                for i in (2 * pair, 2 * pair + 1):
                    stacked.append(real[i][c * HALF:(c + 1) * HALF])
                    stacked.append(imag[i][c * HALF:(c + 1) * HALF])
        out = lax.dot_general(
            coarse, jnp.concatenate(stacked, 0), (((1,), (1,)), ((), ())),
            preferred_element_type=F32,
        )
        for pair in range(2):
            for c in range(2):
                at = (pair * 2 + c) * LANES
                piece = out[:NQ, at:at + LANES] * phases[c][0] - out[NQ:, at:at + LANES] * phases[c][1]
                for g in range(2):
                    row = (2 * NQ * g + c) * MSG + base + pair
                    flat[pl.ds(row, NQ, stride=2 * MSG), :] = piece
    msg_ref[...] = flat[...].astype(BF)
    for copy in later:
        copy.wait()


def rows_kernel(got_ref, fwd_ref, keep_ref, give_ref, vis_ref, rho_ref, flat, halves):
    flat[...] = got_ref[...].astype(F32)
    got = jnp.concatenate(
        [flat[pl.ds(NR2, NDEV, stride=MSG), :].T, flat[pl.ds(NR2 + 1, NDEV, stride=MSG), :].T], 0
    )
    n = 5 * SLOT
    vis_ref[...] = got[:n] + got[n:2 * n] + got[2 * n:3 * n]
    four = lax.axis_index("facet") // 2
    start = (got[A_HIGH:A_HIGH + 1] * 256.0 + got[A_HIGH + 1:A_HIGH + 2]).astype(jnp.int32)
    low = lower((1, LANES))
    starts = [
        jnp.where(low, start[:, 2 * t * NQ:2 * t * NQ + 1], start[:, (2 * t + 1) * NQ:(2 * t + 1) * NQ + 1])
        for t in range(2)
    ]
    eight = iota((8, LANES), 0)
    turn_c, turn_s = phase_of(
        jnp.where(eight < 4, starts[0], starts[1]), (four * 4 + (eight & 3)) * (N_IMG // 8)
    )
    for t in range(2):
        fine_c, fine_s = phase_of(starts[t], iota((SUBG, LANES), 0))
        for p in range(4):
            tc, ts = turn_c[t * 4 + p:t * 4 + p + 1], turn_s[t * 4 + p:t * 4 + p + 1]
            rho_ref[t, 0, p * SUBG:(p + 1) * SUBG, :] = fine_c * tc - fine_s * ts
            rho_ref[t, 1, p * SUBG:(p + 1) * SUBG, :] = fine_s * tc + fine_c * ts
    low = lower((NQ, LANES))
    first, second = [], []
    for row in range(NR2):
        x = [flat[pl.ds(f * NQ * MSG + row, NQ, stride=MSG), :] for f in range(NF)]
        y = [roll(v, SUBG) for v in x]
        first.append(jnp.concatenate([jnp.where(low, x[0], y[1]), jnp.where(low, x[2], y[3])], 1).astype(BF))
        second.append(jnp.concatenate([jnp.where(low, y[0], x[1]), jnp.where(low, y[2], x[3])], 1).astype(BF))
    both = jnp.dot(fwd_ref[...], jnp.concatenate(first + second, 0), preferred_element_type=F32)
    m = 4 * SUBG
    real, turned = 0.0, 0.0
    for t in range(2):
        rc, rs = rho_ref[t, 0], rho_ref[t, 1]
        a, b = both[:m, t * LANES:(t + 1) * LANES], both[m:, t * LANES:(t + 1) * LANES]
        real = real + (rc * a + rs * b)
        turned = turned + (rc * b - rs * a)
    real = real + roll(real, SUBG)
    turned = turned + roll(turned, SUBG)
    halves[...] = real - roll(turned, HALF) * lane_sign(m, HALF)
    core = lax.axis_index("sub") & 1
    keep_ref[...] = halves[pl.ds(core * LANES, LANES), :].astype(BF)
    give_ref[...] = halves[pl.ds((1 - core) * LANES, LANES), :].astype(BF)


def times(a, b):
    return a[0] * b[0] - a[1] * b[1], a[0] * b[1] + a[1] * b[0]


def tables_kernel(vis_ref, left, basis, small):
    slot = 0
    for l in range(2):
        for which in range(2):
            turn = vis_ref[which * SLOT + l * 8:which * SLOT + l * 8 + 8, :] * (1.0 / SUBG)
            p1 = sincos_turn(turn)
            ones = jnp.ones_like(turn)

            def ladder(p, unit):
                p2 = times(p, p)
                p3 = times(p2, p)
                p4 = times(p2, p2)
                return [unit, p, p2, p3, p4, times(p4, p), times(p3, p3), times(p4, p3)], p4

            low, p4 = ladder(p1, (ones, jnp.zeros_like(turn)))
            high, _ = ladder(times(p4, p4), (ones, jnp.zeros_like(turn)))
            for i in range(8):
                for part in range(2):
                    small[slot, part, i * 8:i * 8 + 8, :] = low[i][part]
                    small[slot, 2 + part, i * 8:i * 8 + 8, :] = high[i][part] * 0.125
            for k in range(8):
                at = slice(k * LANES, (k + 1) * LANES)
                br, bi, ar, ai = [small[slot, part, pl.ds(k, 8, stride=8), :] for part in range(4)]
                re, im = [], []
                for a in range(8):
                    hr, hi = ar[a:a + 1, :], ai[a:a + 1, :]
                    re.append(hr * br - hi * bi)
                    im.append(hr * bi + hi * br)
                if which == 0:
                    left[l, 0:SUBG, at] = jnp.concatenate(re, 0)
                    left[l, SUBG:, at] = jnp.concatenate(im, 0)
                else:
                    for h in range(2):
                        base = h * SUBG
                        basis[l, base:base + HALF, at] = jnp.concatenate(re[h * 4:h * 4 + 4], 0).astype(BF)
                        basis[l, base + HALF:base + SUBG, at] = jnp.concatenate(im[h * 4:h * 4 + 4], 0).astype(BF)
            slot += 1


def swap_half(x):
    return jnp.where((iota(x.shape, 1) & HALF) == 0, roll(x, LANES - HALF), roll(x, HALF))


def visibility_kernel(keep_ref, other_ref, vis_ref, left, basis, corrected_ref, back_ref, inner, phasor):
    upper_core = (lax.axis_index("sub") & 1) == 1
    keep, other = keep_ref[...].astype(F32), other_ref[...].astype(F32)
    halves = jnp.where(upper_core, other, keep), jnp.where(upper_core, keep, other)
    subgrids = jnp.where(lower((LANES, LANES)), halves[0], halves[1])
    sign = lane_sign(SUBG, HALF)
    sums = []
    returned = [[None, None], [None, None]]
    for l in range(2):
        obs_r, obs_i, level = [vis_ref[c * SLOT + l * 8:c * SLOT + l * 8 + 8, :] for c in range(2, 5)]
        sub = subgrids[l * SUBG:(l + 1) * SUBG]
        matrix = jnp.concatenate([sub * sign, swap_half(sub)], 0).astype(BF)
        inner[l] = jnp.dot(matrix, basis[l], preferred_element_type=F32)
        pred_r, pred_i = [], []
        for k in range(8):
            at = slice(k * LANES, (k + 1) * LANES)
            lr, li = left[l, 0:SUBG, at], left[l, SUBG:, at]
            ir, ii = inner[l, 0:SUBG, at], inner[l, SUBG:, at]
            pred_r.append(jnp.sum(lr * ir - li * ii, 0, keepdims=True))
            pred_i.append(jnp.sum(lr * ii + li * ir, 0, keepdims=True))
        mis_r = obs_r - jnp.concatenate(pred_r, 0)
        mis_i = obs_i - jnp.concatenate(pred_i, 0)
        live = level > 0.0
        threshold = jnp.where(live, level, 1.0)
        magnitude = jnp.sqrt(mis_r * mis_r + mis_i * mis_i)
        weight = jnp.where(live, threshold / jnp.maximum(magnitude, threshold), 0.0)
        wr, wi = weight * mis_r, weight * mis_i
        returned[0][l], returned[1][l] = wr, wi
        for k in range(8):
            at = slice(k * LANES, (k + 1) * LANES)
            lr, li = left[l, 0:SUBG, at], left[l, SUBG:, at]
            vr, vi = wr[k:k + 1, :], wi[k:k + 1, :]
            phasor[l, 0:SUBG, at] = (lr * vr + li * vi).astype(BF)
            phasor[l, SUBG:, at] = (lr * vi - li * vr).astype(BF)
        product = lax.dot_general(
            phasor[l], basis[l], (((1,), (1,)), ((), ())), preferred_element_type=F32
        )
        sums.append(product[:SUBG] * sign + swap_half(product[SUBG:]))
    corrected_ref[...] = jnp.concatenate(sums, 0).astype(BF)
    back = jnp.concatenate([returned[0][0], returned[0][1], returned[1][0], returned[1][1]], 0)
    back = [part.astype(F32) for part in split3(back)]
    back_ref[...] = jnp.concatenate(back + [jnp.zeros((2 * SLOT, LANES), F32)], 0)


def images_kernel(mine_ref, other_ref, back_ref, rho_ref, adj_ref, msg_ref, flat):
    upper_core = (lax.axis_index("sub") & 1) == 1
    mine, other = mine_ref[...].astype(F32), other_ref[...].astype(F32)
    low = lower((LANES, LANES))
    rows = []
    for x in (jnp.where(upper_core, other, mine), jnp.where(upper_core, mine, other)):
        y = roll(x, SUBG)
        rows.append(jnp.where(low != upper_core, x, y))
    corrected = jnp.concatenate(rows, 0)
    turned = roll(corrected, HALF) * -lane_sign(4 * SUBG, HALF)
    cols = []
    for t in range(2):
        rc, rs = rho_ref[t, 0], rho_ref[t, 1]
        cols.append(
            jnp.concatenate(
                [(corrected * rc + turned * rs).astype(BF), (corrected * rs - turned * rc).astype(BF)], 0
            )
        )
    images = jnp.dot(adj_ref[...], jnp.concatenate(cols, 1), preferred_element_type=F32)
    low = lower((NQ, LANES))
    for row in range(NR2):
        for t in range(2):
            at = slice(t * LANES, (t + 1) * LANES)
            a = images[row * NQ:(row + 1) * NQ, at]
            b = images[(NR2 + row) * NQ:(NR2 + row + 1) * NQ, at]
            flat[pl.ds(2 * t * NQ * MSG + row, NQ, stride=MSG), :] = jnp.where(low, a, roll(b, SUBG))
            flat[pl.ds((2 * t + 1) * NQ * MSG + row, NQ, stride=MSG), :] = jnp.where(low, roll(a, SUBG), b)
    flat[pl.ds(NR2, NDEV, stride=MSG), :] = back_ref[...].T
    flat[pl.ds(NR2 + 1, NDEV, stride=MSG), :] = jnp.zeros((NDEV, LANES), F32)
    msg_ref[...] = flat[...].astype(BF)


def facet_kernel(
    got_ref, meta_ref, coarse_ref, tw_ref, col_ref, out_hbm, res_hbm, flat, turned, out_ref, res_ref, sems,
):
    flat[...] = got_ref[...].astype(F32)
    n = 2 * SLOT
    back = flat[pl.ds(NR2, NDEV, stride=MSG), :].T[:3 * n]
    owner, place = meta_ref[0:1, :], meta_ref[1:2, :]
    own = jnp.where(iota((NDEV, NV), 0) == owner, 1.0, 0.0).astype(BF)
    found = jnp.dot(back.astype(BF), own, preferred_element_type=F32)
    found = found[:n] + found[n:2 * n] + found[2 * n:]
    here = iota((SLOT, NV), 0) == place
    for c in range(2):
        res_ref[c:c + 1, :] = jnp.sum(
            jnp.where(here, found[c * SLOT:(c + 1) * SLOT], 0.0), 0, keepdims=True
        )
    copies = [pltpu.make_async_copy(res_ref, res_hbm, sems.at[4])]
    copies[0].start()

    freq = iota((NQ, LANES), 0) * (N_IMG // NQ) + (iota((NQ, LANES), 1) & (SUBG - 1))
    ph_c, ph_s = phase_of(meta_ref[2:3, :LANES], freq)
    ph_s = -ph_s * lane_sign(NQ, SUBG)
    tw_c, tw_s = tw_ref[0], tw_ref[1]
    sign = lane_sign(LANES, SUBG)
    quarter = iota((NQ, LANES), 1) // HALF
    images = [None] * RD
    for row in range(NR2):
        x = []
        for c in range(2):
            image = flat[pl.ds(c * MSG + row, NQ, stride=2 * MSG), :]
            x.append(image + flat[pl.ds((2 * NQ + c) * MSG + row, NQ, stride=2 * MSG), :])
        r32, r64, r96 = [[roll(v, k * HALF) for v in x] for k in (1, 2, 3)]
        choose = lambda *v: jnp.where(
            quarter < 2, jnp.where(quarter == 0, v[0], v[1]), jnp.where(quarter == 2, v[2], v[3])
        )
        for h, image in enumerate(
            (choose(x[0], r32[1], r32[0], r64[1]), choose(r64[0], r96[1], r96[0], x[1]))
        ):
            images[row + h * NR2] = (image * ph_c + roll(image, SUBG) * ph_s).astype(BF)
    group = 4
    for base in range(0, RD, group):
        spread = jnp.dot(
            coarse_ref[...], jnp.concatenate(images[base:base + group], 1), preferred_element_type=F32
        )
        stacked = []
        for i in range(group):
            first = spread[:LANES, i * LANES:(i + 1) * LANES]
            second = spread[LANES:, i * LANES:(i + 1) * LANES]
            z = (tw_c * first - tw_s * second) - roll(tw_s * first + tw_c * second, SUBG) * sign
            stacked.append(z.astype(BF))
        out = lax.dot_general(
            col_ref[...], jnp.concatenate(stacked, 0), (((1,), (1,)), ((), ())),
            preferred_element_type=F32,
        )
        for i in range(group):
            r = base + i
            for part in range(2):
                at = (part * 2 + r // 8) * NA * 8 + r % 8
                turned[pl.ds(at, NA, stride=8), :] = out[
                    part * NA:(part + 1) * NA, i * LANES:(i + 1) * LANES
                ]
        if (base + group) % 8 == 0:
            half = base // 8
            for part in range(2):
                where = slice(half * 8, half * 8 + 8)
                for a in range(NA):
                    at = ((part * 2 + half) * NA + a) * 8
                    out_ref[part, where, a * LANES:(a + 1) * LANES] = turned[at:at + 8, :]
                copy = pltpu.make_async_copy(
                    out_ref.at[part, where, :], out_hbm.at[0, part, where, :],
                    sems.at[half * 2 + part],
                )
                copy.start()
                copies.append(copy)
    for copy in copies:
        copy.wait()


VMEM = pl.BlockSpec(memory_space=pltpu.VMEM)
HBM = pl.BlockSpec(memory_space=pltpu.MemorySpace.HBM)
TABLES = host_tables()


def in_place(arrays):
    return [pltpu.with_memory_space_constraint(x, pltpu.HBM) for x in arrays]


def exchange(message):
    pairs = message.reshape(NDEV * MSG // 2, 2, LANES)
    return lax.all_to_all(pairs, ALL, split_axis=0, concat_axis=0, tiled=True).reshape(message.shape)


def other_core(x):
    return lax.ppermute(x, "sub", [(i, i ^ 1) for i in range(NQ)])


def on_device(slab, offsets, position, observed, subgrid_of, clip):
    t = {name: jnp.asarray(value) for name, value in TABLES.items()}
    limit = pltpu.CompilerParams(vmem_limit_bytes=32 << 20)
    shape = jax.ShapeDtypeStruct
    message = shape((NDEV * MSG, LANES), BF)
    table = shape((8 * SUBG, NQ * RD), BF)
    square = shape((LANES, LANES), BF)
    flat = pltpu.VMEM((NDEV * MSG, LANES), F32)

    def call(kernel, name, inputs, outs, scratch, in_specs=None, out_specs=None, flops=1 << 20):
        return pl.pallas_call(
            kernel,
            out_shape=outs,
            in_specs=in_specs or [VMEM] * len(inputs),
            out_specs=out_specs or (VMEM,) * len(outs),
            scratch_shapes=scratch,
            compiler_params=limit,
            cost_estimate=pl.CostEstimate(flops=flops, bytes_accessed=1 << 21, transcendentals=0),
            name=name,
        )(*inputs)

    inputs = (
        offsets, slab, position, observed, subgrid_of.reshape(1, NV),
        clip.reshape(1, NV // VIS_BLOCK), t["column"], t["tw_fwd"],
    )
    sent, meta, fwd, adj = call(
        send_kernel, "send", in_place(inputs + (t["row_fwd"], t["row_adj"])),
        (message, shape((8, NV), jnp.int32), table, table),
        [pltpu.SMEM((1, 2), jnp.int32)]
        + [pltpu.VMEM(x.shape, x.dtype) for x in inputs[1:]]
        + [
            pltpu.VMEM((2, NA * RD, LANES), F32),
            flat,
            pltpu.SemaphoreType.DMA((len(inputs) + 2,)),
        ],
        in_specs=[HBM] * (len(inputs) + 2),
    )
    got = exchange(sent)
    keep, give, vis, rho = call(
        rows_kernel, "rows", (got, fwd),
        (square, square, shape((5 * SLOT, LANES), F32), shape((2, 2, 4 * SUBG, LANES), F32)),
        [flat, pltpu.VMEM((4 * SUBG, LANES), F32)],
    )
    other = other_core(give)
    left, basis = call(
        tables_kernel, "tables", (vis,),
        (shape((2, 2 * SUBG, NV), F32), shape((2, 2 * SUBG, NV), BF)),
        [pltpu.VMEM((4, 4, SUBG, LANES), F32)],
    )
    corrected, back = call(
        visibility_kernel, "visibilities", (keep, other, vis, left, basis),
        (square, shape((LANES, LANES), F32)),
        [pltpu.VMEM((2, 2 * SUBG, NV), F32), pltpu.VMEM((2, 2 * SUBG, NV), BF)],
    )
    (answer,) = call(
        images_kernel, "images", (corrected, other_core(corrected), back, rho, adj), (message,), [flat]
    )
    facet_adjoint, residual = call(
        facet_kernel, "facet",
        (exchange(answer), meta, t["coarse_adj"], t["tw_adj"], t["col_adj"]),
        (shape((1, 2, RD, NA * LANES), F32), shape((2, NV), F32)),
        [
            flat,
            pltpu.VMEM((4 * NA * 8, LANES), F32),
            pltpu.VMEM((2, RD, NA * LANES), F32),
            pltpu.VMEM((2, NV), F32),
            pltpu.SemaphoreType.DMA((5,)),
        ],
        out_specs=(HBM, HBM),
    )
    return (facet_adjoint, residual)


def solution(mesh):
    placed = (
        P("facet", None, "sub", None),
        P("facet", None),
        P(None, ALL),
        P(None, ALL),
        P(ALL, None),
        P(ALL),
    )
    return jax.shard_map(
        on_device,
        mesh=mesh,
        in_specs=placed,
        out_specs=(P("facet", None, "sub", None), P(None, ALL)),
        check_vma=False,
    )
```

```python
import math

import jax
import jax.numpy as jnp
import numpy as np
from jax import lax
from jax.experimental import pallas as pl
from jax.experimental.pallas import tpu as pltpu
from jax.sharding import PartitionSpec as P

N_IMG = 32768
SUBG = 64
HALF = 32
VIS_BLOCK = 32
LANES = 128
NQ = 32
NF = 4
NDEV = 128
RD = 16
NR2 = 8
NA = 64
NV = 1024
SLOT = 16
MSG = 10
A_HIGH = 3 * 5 * SLOT
TWO_PI = 2.0 * math.pi
BF = jnp.bfloat16
F32 = jnp.float32
ALL = ("facet", "sub")


def unit(index, period):
    angle = TWO_PI * (np.asarray(index, np.int64) % period) / period
    return np.cos(angle), np.sin(angle)


def host_tables():
    block = np.arange(NA)
    lane = np.arange(LANES)
    fine = np.arange(SUBG)
    coarse = np.arange(NQ)
    c, s = unit(fine[:, None] * block[None, :], 256)
    c, s = c / 64.0, s / 64.0
    col_fwd = np.block([[c, s], [-s, c]])
    col_adj = np.block([[c.T, -s.T], [s.T, c.T]])
    tw_c, tw_s = unit(fine[:, None] * lane[None, :], N_IMG)
    twiddle_fwd = np.concatenate([tw_c, -tw_s], 0)
    orders = [fine, fine ^ HALF]
    twiddle_adj = np.stack([np.tile(x.T[:, o], (1, 2)) for o in orders for x in (tw_c, tw_s)])
    col_adj = np.concatenate([col_adj[:, np.concatenate([o, o + SUBG])] for o in orders], 0)
    wc, ws = unit(coarse[:, None] * lane[None, :], 32)
    column = np.concatenate([col_fwd, wc, ws, -ws, wc], 0)
    coarse_adj = np.block([[wc.T, ws.T], [-ws.T, wc.T]])
    k_row = (np.arange(8)[:, None] * 4096 + fine[None, :]).reshape(2, 4 * SUBG)
    r = np.arange(NQ * RD).reshape(NQ, 2, NR2).transpose(1, 2, 0).reshape(-1)
    rc, rs = unit(k_row[:, :, None] * r[None, None, :], N_IMG)
    pairs = lambda x: x.reshape(2, 2, 2 * SUBG, NQ * RD) / 64.0
    row_fwd = np.concatenate([pairs(rc), -pairs(rs)], 2)
    row_adj = np.ascontiguousarray(row_fwd.transpose(0, 1, 3, 2))
    bf = lambda x: np.asarray(x, np.float32).astype(jnp.bfloat16)
    return dict(
        column=bf(column),
        col_adj=bf(col_adj),
        tw_fwd=np.asarray(twiddle_fwd, np.float32),
        tw_adj=np.asarray(twiddle_adj, np.float32),
        coarse_adj=bf(coarse_adj),
        row_fwd=bf(row_fwd),
        row_adj=bf(row_adj),
    )


def sincos_turn(turn):
    quarter = jnp.floor(turn * 4.0 + 0.5)
    y = (turn - quarter * 0.25) * TWO_PI
    y2 = y * y
    s = y * (1.0 + y2 * (-1.0 / 6 + y2 * (1.0 / 120 + y2 * (-1.0 / 5040 + y2 * (1.0 / 362880)))))
    c = 1.0 + y2 * (-0.5 + y2 * (1.0 / 24 + y2 * (-1.0 / 720 + y2 * (1.0 / 40320))))
    turns = quarter.astype(jnp.int32)
    odd = (turns & 1) == 1
    cos = jnp.where(odd, s, c)
    sin = jnp.where(odd, c, s)
    cos = jnp.where(((turns + 1) & 2) == 2, -cos, cos)
    sin = jnp.where((turns & 2) == 2, -sin, sin)
    return cos, sin


def phase_of(offset, frequency):
    index = (offset * frequency) & (N_IMG - 1)
    return sincos_turn(index.astype(F32) * (1.0 / N_IMG))


def iota(shape, dim):
    return lax.broadcasted_iota(jnp.int32, shape, dim)


def roll(x, shift):
    return pltpu.roll(x, shift, x.ndim - 1)


def lane_sign(rows, width):
    return jnp.where((iota((rows, LANES), 1) & width) == 0, 1.0, -1.0).astype(F32)


def lower(shape):
    return iota(shape, len(shape) - 1) < SUBG


def split3(x):
    high = x.astype(BF)
    rest = x - high.astype(F32)
    middle = rest.astype(BF)
    low = (rest - middle.astype(F32)).astype(BF)
    return high, middle, low


def send_kernel(
    off_hbm, slab_hbm, pos_hbm, obs_hbm, ids_hbm, clip_hbm, table_hbm, tw_hbm, fwd_hbm, adj_hbm,
    msg_ref, meta_ref, fwd_ref, adj_ref, off_ref, slab_ref, pos_ref, obs_ref, ids_ref, clip_ref, table_ref, tw_ref,
    wide, flat, sems,
):
    pairs = [
        (ids_hbm, ids_ref), (clip_hbm, clip_ref), (pos_hbm, pos_ref), (obs_hbm, obs_ref),
        (off_hbm, off_ref), (slab_hbm, slab_ref), (table_hbm, table_ref), (tw_hbm, tw_ref),
    ]
    copies = [pltpu.make_async_copy(a, b, sems.at[i]) for i, (a, b) in enumerate(pairs)]
    four = lax.axis_index("facet") // 2
    later = [
        pltpu.make_async_copy(fwd_hbm.at[four], fwd_ref, sems.at[len(pairs)]),
        pltpu.make_async_copy(adj_hbm.at[four], adj_ref, sems.at[len(pairs) + 1]),
    ]
    for copy in copies + later:
        copy.start()

    copies[0].wait()
    ids = ids_ref[...]
    upper = jnp.where(iota((LANES, LANES), 0) < iota((LANES, LANES), 1), 1.0, 0.0).astype(BF)
    counter = jnp.concatenate([upper, jnp.ones((LANES, LANES), BF)], 1)
    before = jnp.zeros((2 * LANES, LANES), F32)
    ranks = []
    for b in range(NV // LANES):
        hot = iota((2 * LANES, LANES), 0) == ids[:, b * LANES:(b + 1) * LANES]
        hot_f = jnp.where(hot, 1.0, 0.0)
        count = jnp.dot(hot_f.astype(BF), counter, preferred_element_type=F32)
        ranks.append(jnp.sum(hot_f * (count[:, :LANES] + before), 0, keepdims=True))
        before = before + count[:, LANES:]
    rank = jnp.concatenate(ranks, 1).astype(jnp.int32)
    owner = (ids >> 7) * (2 * NQ) + (ids & (NQ - 1)) * 2 + ((ids >> 6) & 1)
    place = ((ids >> 5) & 1) * 8 + rank
    meta_ref[0:1, :] = owner
    meta_ref[1:2, :] = place
    here = iota((SLOT, NV), 0) == place
    copies[1].wait()
    n_block = NV // VIS_BLOCK
    clip = jnp.broadcast_to(clip_ref[...].astype(F32) * 0.25, (n_block, n_block))
    same = iota((n_block, n_block), 0) == iota((n_block, n_block), 1)
    clip = jnp.sum(jnp.where(same, clip, 0.0), 1, keepdims=True)
    block = iota((n_block, NV), 1) // VIS_BLOCK == iota((n_block, NV), 0)
    level = jnp.sum(jnp.where(block, clip, 0.0), 0, keepdims=True)
    copies[2].wait()
    copies[3].wait()
    values = [pos_ref[0:1, :], pos_ref[1:2, :], obs_ref[0:1, :], obs_ref[1:2, :], level]
    pieces = [split3(v) for v in values]
    own = jnp.where(iota((NDEV, NV), 0) == owner, 1.0, 0.0).astype(BF)
    table = jnp.concatenate(
        [jnp.where(here, p[part].astype(F32), 0.0).astype(BF) for part in range(3) for p in pieces]
        + [jnp.zeros((SLOT, NV), BF)], 0
    )
    copies[4].wait()
    meta_ref[2:3, :] = jnp.full((1, NV), off_ref[0, 1], jnp.int32)
    payload = lax.dot_general(own, table, (((1,), (1,)), ((), ())), preferred_element_type=F32)
    lane = iota((NDEV, LANES), 1)
    tail = payload[:, LANES:]
    tail = jnp.where(lane == A_HIGH - LANES, (off_ref[0, 0] >> 8).astype(F32), tail)
    tail = jnp.where(lane == A_HIGH + 1 - LANES, (off_ref[0, 0] & 255).astype(F32), tail)
    flat[pl.ds(NR2, NDEV, stride=MSG), :] = payload[:, :LANES]
    flat[pl.ds(NR2 + 1, NDEV, stride=MSG), :] = tail

    lane1 = iota((NQ, LANES), 1)
    freq = iota((NQ, LANES), 0) * (N_IMG // NQ) + (lane1 & (HALF - 1)) + lane1 // SUBG * HALF
    ph_c, ph_s = phase_of(off_ref[0, 1], freq)
    for copy in copies[5:]:
        copy.wait()
    for part in range(2):
        for a in range(NA):
            wide[part, a * RD:(a + 1) * RD, :] = slab_ref[
                0, part, :, a * LANES:(a + 1) * LANES
            ].astype(F32)
    tw_c, tw_s = tw_ref[:SUBG], tw_ref[SUBG:]
    col = table_ref[:LANES]
    coarse = jnp.concatenate(
        [
            jnp.concatenate([table_ref[LANES:LANES + NQ], table_ref[LANES + NQ:LANES + 2 * NQ]], 1),
            jnp.concatenate([table_ref[LANES + 2 * NQ:LANES + 3 * NQ], table_ref[LANES + 3 * NQ:]], 1),
        ], 0
    )
    low = lower((NQ, LANES))
    for base in range(0, NR2, 2):
        which = [base, base + NR2, base + 1, base + 1 + NR2]
        cols = [
            jnp.concatenate(
                [wide[0, pl.ds(r, NA, stride=RD), :], wide[1, pl.ds(r, NA, stride=RD), :]], 0
            ).astype(BF)
            for r in which
        ]
        y = jnp.dot(col, jnp.concatenate(cols, 1), preferred_element_type=F32)
        both = []
        for i in range(4):
            yr = y[:SUBG, i * LANES:(i + 1) * LANES]
            yi = y[SUBG:, i * LANES:(i + 1) * LANES]
            zr = yr * tw_c - yi * tw_s
            zi = yr * tw_s + yi * tw_c
            both.append(jnp.concatenate([zr, zi], 1).astype(BF))
        stacked = [
            both[2 * pair + i][c * HALF:(c + 1) * HALF]
            for pair in range(2) for c in range(2) for i in range(2)
        ]
        out = lax.dot_general(
            coarse, jnp.concatenate(stacked, 0), (((1,), (1,)), ((), ())),
            preferred_element_type=F32,
        )
        for pair in range(2):
            at = pair * LANES
            x, y = out[:NQ, at:at + LANES], out[NQ:, at:at + LANES]
            re, im = x * ph_c + y * ph_s, y * ph_c - x * ph_s
            pieces = [jnp.where(low, re, roll(im, SUBG)), jnp.where(low, roll(re, SUBG), im)]
            for c in range(2):
                for g in range(2):
                    row = (2 * NQ * g + c) * MSG + base + pair
                    flat[pl.ds(row, NQ, stride=2 * MSG), :] = pieces[c]
    msg_ref[...] = flat[...].astype(BF)
    for copy in later:
        copy.wait()


def quarter_low(shape):
    return (iota(shape, len(shape) - 1) & HALF) == 0


def combine(both, rho):
    real, turned = 0.0, 0.0
    for t in range(2):
        rc, rs = rho[t, 0], rho[t, 1]
        a, b = both[:LANES, t * LANES:(t + 1) * LANES], both[LANES:, t * LANES:(t + 1) * LANES]
        real = real + (rc * a + rs * b)
        turned = turned + (rc * b - rs * a)
    real = real + roll(real, HALF)
    turned = turned + roll(turned, HALF)
    return (real - roll(turned, SUBG) * lane_sign(LANES, SUBG)).astype(BF)


def rows_kernel(got_ref, fwd_ref, give_ref, rhs_ref, rho_ref, raw_ref, flat):
    flat[...] = got_ref[...].astype(F32)
    core = lax.axis_index("sub") & 1
    four = lax.axis_index("facet") // 2
    low = quarter_low((1, LANES))
    start = []
    for f in range(NF):
        row = f * NQ * MSG + NR2 + 1
        at = A_HIGH - LANES
        start.append((flat[row:row + 1, at:at + 1] * 256.0 + flat[row:row + 1, at + 1:at + 2]).astype(jnp.int32))
    starts = [jnp.where(low, start[2 * t], start[2 * t + 1]) for t in range(2)]
    eight = iota((8, LANES), 0)
    turn_c, turn_s = phase_of(
        jnp.where(eight < 4, starts[0], starts[1]), (four * 4 + (eight & 3)) * (N_IMG // 8)
    )
    for t in range(2):
        fine_c, fine_s = phase_of(starts[t], iota((SUBG, LANES), 0))
        for p in range(4):
            tc, ts = turn_c[t * 4 + p:t * 4 + p + 1], turn_s[t * 4 + p:t * 4 + p + 1]
            at = slice((p & 1) * SUBG, (p & 1) * SUBG + SUBG)
            rho_ref[p // 2, t, 0, at, :] = fine_c * tc - fine_s * ts
            rho_ref[p // 2, t, 1, at, :] = fine_s * tc + fine_c * ts
    low = quarter_low((NQ, LANES))
    for row in range(NR2):
        x = [flat[pl.ds(f * NQ * MSG + row, NQ, stride=MSG), :] for f in range(NF)]
        for t in range(2):
            at = slice(t * LANES, (t + 1) * LANES)
            a, b = x[2 * t], x[2 * t + 1]
            rhs_ref[row * NQ:(row + 1) * NQ, at] = jnp.where(low, a, roll(b, HALF)).astype(BF)
            rhs_ref[(NR2 + row) * NQ:(NR2 + row + 1) * NQ, at] = jnp.where(
                low, roll(a, LANES - HALF), b
            ).astype(BF)
    both = jnp.dot(fwd_ref[1 - core], rhs_ref[...], preferred_element_type=F32)
    give_ref[...] = combine(both, rho_ref.at[1 - core])
    raw_ref[0] = flat[pl.ds(NR2, NDEV, stride=MSG), :]
    raw_ref[1] = flat[pl.ds(NR2 + 1, NDEV, stride=MSG), :]


def times(a, b):
    return a[0] * b[0] - a[1] * b[1], a[0] * b[1] + a[1] * b[0]


def tables_kernel(raw_ref, fwd_ref, rhs_ref, rho_ref, keep_ref, vis_ref, left, basis, small):
    core = lax.axis_index("sub") & 1
    got = jnp.concatenate([raw_ref[0].T, raw_ref[1].T], 0)
    n = 5 * SLOT
    vis_ref[...] = got[:n] + got[n:2 * n] + got[2 * n:3 * n]
    both = jnp.dot(fwd_ref[core], rhs_ref[...], preferred_element_type=F32)
    keep_ref[...] = combine(both, rho_ref.at[core])
    slot = 0
    for l in range(2):
        for which in range(2):
            turn = vis_ref[which * SLOT + l * 8:which * SLOT + l * 8 + 8, :] * (1.0 / SUBG)
            p1 = sincos_turn(turn)
            ones = jnp.ones_like(turn)

            def ladder(p, unit):
                p2 = times(p, p)
                p3 = times(p2, p)
                p4 = times(p2, p2)
                return [unit, p, p2, p3, p4, times(p4, p), times(p3, p3), times(p4, p3)], p4

            low, p4 = ladder(p1, (ones, jnp.zeros_like(turn)))
            high, _ = ladder(times(p4, p4), (ones, jnp.zeros_like(turn)))
            for i in range(8):
                for part in range(2):
                    small[slot, part, i * 8:i * 8 + 8, :] = low[i][part]
                    small[slot, 2 + part, i * 8:i * 8 + 8, :] = high[i][part] * 0.125
            for k in range(8):
                at = slice(k * LANES, (k + 1) * LANES)
                br, bi, ar, ai = [small[slot, part, pl.ds(k, 8, stride=8), :] for part in range(4)]
                re, im = [], []
                for a in range(8):
                    hr, hi = ar[a:a + 1, :], ai[a:a + 1, :]
                    re.append(hr * br - hi * bi)
                    im.append(hr * bi + hi * br)
                if which == 0:
                    left[l, 0:SUBG, at] = jnp.concatenate(re, 0)
                    left[l, SUBG:, at] = jnp.concatenate(im, 0)
                else:
                    basis[l, 0:SUBG, at] = jnp.concatenate(re, 0).astype(BF)
                    basis[l, SUBG:, at] = jnp.concatenate(im, 0).astype(BF)
            slot += 1


def visibility_kernel(keep_ref, other_ref, vis_ref, left, basis, corrected_ref, back_ref, inner, phasor):
    upper_core = (lax.axis_index("sub") & 1) == 1
    keep, other = keep_ref[...].astype(F32), other_ref[...].astype(F32)
    halves = jnp.where(upper_core, other, keep), jnp.where(upper_core, keep, other)
    subgrids = jnp.where(quarter_low((LANES, LANES)), roll(halves[0], LANES - HALF), halves[1])
    sign = lane_sign(SUBG, SUBG)
    sums = []
    returned = [[None, None], [None, None]]
    for l in range(2):
        obs_r, obs_i, level = [vis_ref[c * SLOT + l * 8:c * SLOT + l * 8 + 8, :] for c in range(2, 5)]
        sub = subgrids[l * SUBG:(l + 1) * SUBG]
        matrix = jnp.concatenate([sub * sign, roll(sub, SUBG)], 0).astype(BF)
        inner[l] = jnp.dot(matrix, basis[l], preferred_element_type=F32)
        pred_r, pred_i = [], []
        for k in range(8):
            at = slice(k * LANES, (k + 1) * LANES)
            lr, li = left[l, 0:SUBG, at], left[l, SUBG:, at]
            ir, ii = inner[l, 0:SUBG, at], inner[l, SUBG:, at]
            pred_r.append(jnp.sum(lr * ir - li * ii, 0, keepdims=True))
            pred_i.append(jnp.sum(lr * ii + li * ir, 0, keepdims=True))
        mis_r = obs_r - jnp.concatenate(pred_r, 0)
        mis_i = obs_i - jnp.concatenate(pred_i, 0)
        live = level > 0.0
        threshold = jnp.where(live, level, 1.0)
        magnitude = jnp.sqrt(mis_r * mis_r + mis_i * mis_i)
        weight = jnp.where(live, threshold / jnp.maximum(magnitude, threshold), 0.0)
        wr, wi = weight * mis_r, weight * mis_i
        returned[0][l], returned[1][l] = wr, wi
        for k in range(8):
            at = slice(k * LANES, (k + 1) * LANES)
            lr, li = left[l, 0:SUBG, at], left[l, SUBG:, at]
            vr, vi = wr[k:k + 1, :], wi[k:k + 1, :]
            phasor[l, 0:SUBG, at] = (lr * vr + li * vi).astype(BF)
            phasor[l, SUBG:, at] = (lr * vi - li * vr).astype(BF)
        product = lax.dot_general(
            phasor[l], basis[l], (((1,), (1,)), ((), ())), preferred_element_type=F32
        )
        sums.append(product[:SUBG] * sign + roll(product[SUBG:], SUBG))
    corrected_ref[...] = jnp.concatenate(sums, 0).astype(BF)
    back = jnp.concatenate([returned[0][0], returned[0][1], returned[1][0], returned[1][1]], 0)
    back = [part.astype(F32) for part in split3(back)]
    back_ref[...] = jnp.concatenate(back + [jnp.zeros((2 * SLOT, LANES), F32)], 0)


def partial_images(x, pair, rho_ref, adj_ref):
    core = lax.axis_index("sub") & 1
    x = x.astype(F32)
    moved = jnp.where(core == 1, roll(x, LANES - HALF), roll(x, HALF))
    x = jnp.where(quarter_low(x.shape) != (core == 1), x, moved)
    turned = roll(x, SUBG) * -lane_sign(LANES, SUBG)
    cols = []
    for t in range(2):
        rc, rs = rho_ref[pair, t, 0], rho_ref[pair, t, 1]
        cols.append(
            jnp.concatenate([(x * rc + turned * rs).astype(BF), (x * rs - turned * rc).astype(BF)], 0)
        )
    half = NQ * NR2
    table = jnp.concatenate(
        [
            adj_ref[pair, pl.ds(pl.multiple_of(core * half, half), half), :],
            adj_ref[pair, pl.ds(pl.multiple_of((1 - core) * half, half), half), :],
        ], 0
    )
    return jnp.dot(table, jnp.concatenate(cols, 1), preferred_element_type=F32)


def mine_kernel(corrected_ref, rho_ref, adj_ref, part_ref):
    part_ref[...] = partial_images(corrected_ref[...], lax.axis_index("sub") & 1, rho_ref, adj_ref)


def images_kernel(part_ref, other_ref, back_ref, rho_ref, adj_ref, msg_ref, flat):
    pair = 1 - (lax.axis_index("sub") & 1)
    images = part_ref[...] + partial_images(other_ref[...], pair, rho_ref, adj_ref)
    low = quarter_low((NQ, LANES))
    for row in range(NR2):
        for t in range(2):
            at = slice(t * LANES, (t + 1) * LANES)
            a = images[row * NQ:(row + 1) * NQ, at]
            b = images[(NR2 + row) * NQ:(NR2 + row + 1) * NQ, at]
            flat[pl.ds(2 * t * NQ * MSG + row, NQ, stride=MSG), :] = jnp.where(low, a, roll(b, HALF))
            flat[pl.ds((2 * t + 1) * NQ * MSG + row, NQ, stride=MSG), :] = jnp.where(
                low, roll(a, LANES - HALF), b
            )
    flat[pl.ds(NR2, NDEV, stride=MSG), :] = back_ref[...].T
    flat[pl.ds(NR2 + 1, NDEV, stride=MSG), :] = jnp.zeros((NDEV, LANES), F32)
    msg_ref[...] = flat[...].astype(BF)


def facet_kernel(
    got_ref, meta_ref, coarse_ref, tw_ref, col_ref, out_hbm, res_hbm, flat, turned, out_ref, res_ref, sems,
):
    flat[...] = got_ref[...].astype(F32)
    n = 2 * SLOT
    back = flat[pl.ds(NR2, NDEV, stride=MSG), :].T[:3 * n]
    owner, place = meta_ref[0:1, :], meta_ref[1:2, :]
    own = jnp.where(iota((NDEV, NV), 0) == owner, 1.0, 0.0).astype(BF)
    found = jnp.dot(back.astype(BF), own, preferred_element_type=F32)
    found = found[:n] + found[n:2 * n] + found[2 * n:]
    here = iota((SLOT, NV), 0) == place
    for c in range(2):
        res_ref[c:c + 1, :] = jnp.sum(
            jnp.where(here, found[c * SLOT:(c + 1) * SLOT], 0.0), 0, keepdims=True
        )
    copies = [pltpu.make_async_copy(res_ref, res_hbm, sems.at[8])]
    copies[0].start()

    sign = -lane_sign(NQ, SUBG)
    low = quarter_low((NQ, LANES))
    group = 4
    for base in range(0, RD, group):
        h = base // NR2
        if base % NR2 == 0:
            lane1 = iota((NQ, LANES), 1)
            freq = iota((NQ, LANES), 0) * (N_IMG // NQ) + ((lane1 & (SUBG - 1)) ^ (h * HALF))
            ph_c, ph_s = phase_of(meta_ref[2:3, :LANES], freq)
        images = []
        for i in range(group):
            row = (base + i) % NR2
            x = [
                flat[pl.ds(c * MSG + row, NQ, stride=2 * MSG), :]
                + flat[pl.ds((2 * NQ + c) * MSG + row, NQ, stride=2 * MSG), :]
                for c in range(2)
            ]
            image = jnp.where(low, x[h], x[1 - h])
            turn = roll(image, SUBG) * sign
            images.append(
                jnp.concatenate([image * ph_c + turn * ph_s, turn * ph_c - image * ph_s], 0).astype(BF)
            )
        spread = jnp.dot(coarse_ref[...], jnp.concatenate(images, 1), preferred_element_type=F32)
        tw_c, tw_s = tw_ref[2 * h], tw_ref[2 * h + 1]
        stacked = []
        for i in range(group):
            at = slice(i * LANES, (i + 1) * LANES)
            stacked.append((tw_c * spread[:LANES, at] + tw_s * spread[LANES:, at]).astype(BF))
        out = lax.dot_general(
            col_ref[h * LANES:(h + 1) * LANES], jnp.concatenate(stacked, 0), (((1,), (1,)), ((), ())),
            preferred_element_type=F32,
        )
        for i in range(group):
            r = base + i
            for part in range(2):
                at = (part * 2 + r // 8) * NA * 8 + r % 8
                turned[pl.ds(at, NA, stride=8), :] = out[
                    part * NA:(part + 1) * NA, i * LANES:(i + 1) * LANES
                ]
        if (base + group) % 8 == 0:
            half = base // 8
            for part in range(2):
                where = slice(half * 8, half * 8 + 8)
                for piece in range(2):
                    for a in range(piece * NA // 2, (piece + 1) * NA // 2):
                        at = ((part * 2 + half) * NA + a) * 8
                        out_ref[part, where, a * LANES:(a + 1) * LANES] = turned[at:at + 8, :]
                    wide = slice(piece * NA // 2 * LANES, (piece + 1) * NA // 2 * LANES)
                    copy = pltpu.make_async_copy(
                        out_ref.at[part, where, wide], out_hbm.at[0, part, where, wide],
                        sems.at[(half * 2 + part) * 2 + piece],
                    )
                    copy.start()
                    copies.append(copy)
    for copy in copies:
        copy.wait()


VMEM = pl.BlockSpec(memory_space=pltpu.VMEM)
HBM = pl.BlockSpec(memory_space=pltpu.MemorySpace.HBM)
TABLES = host_tables()


def in_place(arrays):
    return [pltpu.with_memory_space_constraint(x, pltpu.HBM) for x in arrays]


def exchange(message):
    pairs = message.reshape(NDEV * MSG // 2, 2, LANES)
    return lax.all_to_all(pairs, ALL, split_axis=0, concat_axis=0, tiled=True).reshape(message.shape)


def other_core(x):
    return lax.ppermute(x, "sub", [(i, i ^ 1) for i in range(NQ)])


def on_device(slab, offsets, position, observed, subgrid_of, clip):
    t = {name: jnp.asarray(value) for name, value in TABLES.items()}
    limit = pltpu.CompilerParams(vmem_limit_bytes=32 << 20)
    shape = jax.ShapeDtypeStruct
    message = shape((NDEV * MSG, LANES), BF)
    fwd_table = shape((2, 4 * SUBG, NQ * RD), BF)
    adj_table = shape((2, NQ * RD, 4 * SUBG), BF)
    square = shape((LANES, LANES), BF)
    flat = pltpu.VMEM((NDEV * MSG, LANES), F32)

    def call(kernel, name, inputs, outs, scratch, in_specs=None, out_specs=None, flops=1 << 20):
        return pl.pallas_call(
            kernel,
            out_shape=outs,
            in_specs=in_specs or [VMEM] * len(inputs),
            out_specs=out_specs or (VMEM,) * len(outs),
            scratch_shapes=scratch,
            compiler_params=limit,
            cost_estimate=pl.CostEstimate(flops=flops, bytes_accessed=1 << 21, transcendentals=0),
            name=name,
        )(*inputs)

    inputs = (
        offsets, slab, position, observed, subgrid_of.reshape(1, NV),
        clip.reshape(1, NV // VIS_BLOCK), t["column"], t["tw_fwd"],
    )
    sent, meta, fwd, adj = call(
        send_kernel, "send", in_place(inputs + (t["row_fwd"], t["row_adj"])),
        (message, shape((8, NV), jnp.int32), fwd_table, adj_table),
        [pltpu.SMEM((1, 2), jnp.int32)]
        + [pltpu.VMEM(x.shape, x.dtype) for x in inputs[1:]]
        + [
            pltpu.VMEM((2, NA * RD, LANES), F32),
            flat,
            pltpu.SemaphoreType.DMA((len(inputs) + 2,)),
        ],
        in_specs=[HBM] * (len(inputs) + 2),
    )
    got = exchange(sent)
    give, rhs, rho, raw = call(
        rows_kernel, "rows", (got, fwd),
        (
            square, shape((NQ * RD, 2 * LANES), BF), shape((2, 2, 2, LANES, LANES), F32),
            shape((2, NDEV, LANES), F32),
        ),
        [flat],
    )
    other = other_core(give)
    keep, vis, left, basis = call(
        tables_kernel, "tables", (raw, fwd, rhs, rho),
        (
            square, shape((5 * SLOT, LANES), F32), shape((2, 2 * SUBG, NV), F32),
            shape((2, 2 * SUBG, NV), BF),
        ),
        [pltpu.VMEM((4, 4, SUBG, LANES), F32)],
    )
    corrected, back = call(
        visibility_kernel, "visibilities", (keep, other, vis, left, basis),
        (square, shape((LANES, LANES), F32)),
        [pltpu.VMEM((2, 2 * SUBG, NV), F32), pltpu.VMEM((2, 2 * SUBG, NV), BF)],
    )
    other = other_core(corrected)
    (part,) = call(
        mine_kernel, "mine", (corrected, rho, adj), (shape((NQ * RD, 2 * LANES), F32),), []
    )
    (answer,) = call(images_kernel, "images", (part, other, back, rho, adj), (message,), [flat])
    facet_adjoint, residual = call(
        facet_kernel, "facet",
        (exchange(answer), meta, t["coarse_adj"], t["tw_adj"], t["col_adj"]),
        (shape((1, 2, RD, NA * LANES), F32), shape((2, NV), F32)),
        [
            flat,
            pltpu.VMEM((4 * NA * 8, LANES), F32),
            pltpu.VMEM((2, RD, NA * LANES), F32),
            pltpu.VMEM((2, NV), F32),
            pltpu.SemaphoreType.DMA((9,)),
        ],
        out_specs=(HBM, HBM),
    )
    return (facet_adjoint, residual)


def solution(mesh):
    placed = (
        P("facet", None, "sub", None),
        P("facet", None),
        P(None, ALL),
        P(None, ALL),
        P(ALL, None),
        P(ALL),
    )
    return jax.shard_map(
        on_device,
        mesh=mesh,
        in_specs=placed,
        out_specs=(P("facet", None, "sub", None), P(None, ALL)),
        check_vma=False,
    )
```

```python
import math

import jax
import jax.numpy as jnp
import numpy as np
from jax import lax
from jax.experimental import pallas as pl
from jax.experimental.pallas import tpu as pltpu
from jax.sharding import PartitionSpec as P

N_IMG = 32768
SUBG = 64
HALF = 32
VIS_BLOCK = 32
LANES = 128
NQ = 32
NF = 4
NDEV = 128
RD = 16
NR2 = 8
NA = 64
NV = 1024
SLOT = 16
MSG = 10
A_HIGH = 3 * 5 * SLOT
TWO_PI = 2.0 * math.pi
BF = jnp.bfloat16
F32 = jnp.float32
ALL = ("facet", "sub")


def unit(index, period):
    angle = TWO_PI * (np.asarray(index, np.int64) % period) / period
    return np.cos(angle), np.sin(angle)


def host_tables():
    block = np.arange(NA)
    lane = np.arange(LANES)
    fine = np.arange(SUBG)
    coarse = np.arange(NQ)
    c, s = unit(fine[:, None] * block[None, :], 256)
    c, s = c / 64.0, s / 64.0
    col_fwd = np.block([[c, s], [-s, c]])
    col_adj = np.block([[c.T, -s.T], [s.T, c.T]])
    tw_c, tw_s = unit(fine[:, None] * lane[None, :], N_IMG)
    twiddle_fwd = np.concatenate([tw_c, -tw_s], 0)
    orders = [fine, fine ^ HALF]
    twiddle_adj = np.stack([np.tile(x.T[:, o], (1, 2)) for o in orders for x in (tw_c, tw_s)])
    col_adj = np.concatenate([col_adj[:, np.concatenate([o, o + SUBG])] for o in orders], 0)
    wc, ws = unit(coarse[:, None] * lane[None, :], 32)
    column = np.concatenate([col_fwd, wc, ws, -ws, wc], 0)
    coarse_adj = np.block([[wc.T, ws.T], [-ws.T, wc.T]])
    k_row = (np.arange(8)[:, None] * 4096 + fine[None, :]).reshape(2, 4 * SUBG)
    r = np.arange(NQ * RD).reshape(NQ, 2, NR2).transpose(1, 2, 0).reshape(-1)
    rc, rs = unit(k_row[:, :, None] * r[None, None, :], N_IMG)
    pairs = lambda x: x.reshape(2, 2, 2 * SUBG, NQ * RD) / 64.0
    row_fwd = np.concatenate([pairs(rc), -pairs(rs)], 2)
    row_adj = np.ascontiguousarray(row_fwd.transpose(0, 1, 3, 2))
    bf = lambda x: np.asarray(x, np.float32).astype(jnp.bfloat16)
    return dict(
        column=bf(column),
        col_adj=bf(col_adj),
        tw_fwd=np.asarray(twiddle_fwd, np.float32),
        tw_adj=np.asarray(twiddle_adj, np.float32),
        coarse_adj=bf(coarse_adj),
        row_fwd=bf(row_fwd),
        row_adj=bf(row_adj),
    )


def sincos_turn(turn):
    quarter = jnp.floor(turn * 4.0 + 0.5)
    y = (turn - quarter * 0.25) * TWO_PI
    y2 = y * y
    s = y * (1.0 + y2 * (-1.0 / 6 + y2 * (1.0 / 120 + y2 * (-1.0 / 5040 + y2 * (1.0 / 362880)))))
    c = 1.0 + y2 * (-0.5 + y2 * (1.0 / 24 + y2 * (-1.0 / 720 + y2 * (1.0 / 40320))))
    turns = quarter.astype(jnp.int32)
    odd = (turns & 1) == 1
    cos = jnp.where(odd, s, c)
    sin = jnp.where(odd, c, s)
    cos = jnp.where(((turns + 1) & 2) == 2, -cos, cos)
    sin = jnp.where((turns & 2) == 2, -sin, sin)
    return cos, sin


def phase_of(offset, frequency):
    index = (offset * frequency) & (N_IMG - 1)
    return sincos_turn(index.astype(F32) * (1.0 / N_IMG))


def iota(shape, dim):
    return lax.broadcasted_iota(jnp.int32, shape, dim)


def roll(x, shift):
    return pltpu.roll(x, shift, x.ndim - 1)


def lane_sign(rows, width):
    return jnp.where((iota((rows, LANES), 1) & width) == 0, 1.0, -1.0).astype(F32)


def lower(shape):
    return iota(shape, len(shape) - 1) < SUBG


def split3(x):
    high = x.astype(BF)
    rest = x - high.astype(F32)
    middle = rest.astype(BF)
    low = (rest - middle.astype(F32)).astype(BF)
    return high, middle, low


def send_kernel(
    off_hbm, slab_hbm, pos_hbm, obs_hbm, ids_hbm, clip_hbm, table_hbm, tw_hbm, fwd_hbm, adj_hbm,
    msg_ref, meta_ref, fwd_ref, adj_ref, off_ref, slab_ref, pos_ref, obs_ref, ids_ref, clip_ref, table_ref, tw_ref,
    wide, flat, y_ref, z_ref, sems,
):
    pairs = [
        (ids_hbm, ids_ref), (clip_hbm, clip_ref), (pos_hbm, pos_ref), (obs_hbm, obs_ref),
        (off_hbm, off_ref), (slab_hbm, slab_ref), (table_hbm, table_ref), (tw_hbm, tw_ref),
    ]
    copies = [pltpu.make_async_copy(a, b, sems.at[i]) for i, (a, b) in enumerate(pairs)]
    four = lax.axis_index("facet") // 2
    later = [
        pltpu.make_async_copy(fwd_hbm.at[four], fwd_ref, sems.at[len(pairs)]),
        pltpu.make_async_copy(adj_hbm.at[four], adj_ref, sems.at[len(pairs) + 1]),
    ]
    for copy in copies + later:
        copy.start()

    copies[0].wait()
    ids = ids_ref[...]
    upper = jnp.where(iota((LANES, LANES), 0) < iota((LANES, LANES), 1), 1.0, 0.0).astype(BF)
    counter = jnp.concatenate([upper, jnp.ones((LANES, LANES), BF)], 1)
    before = jnp.zeros((2 * LANES, LANES), F32)
    ranks = []
    for b in range(NV // LANES):
        hot = iota((2 * LANES, LANES), 0) == ids[:, b * LANES:(b + 1) * LANES]
        hot_f = jnp.where(hot, 1.0, 0.0)
        count = jnp.dot(hot_f.astype(BF), counter, preferred_element_type=F32)
        ranks.append(jnp.sum(hot_f * (count[:, :LANES] + before), 0, keepdims=True))
        before = before + count[:, LANES:]
    rank = jnp.concatenate(ranks, 1).astype(jnp.int32)
    owner = (ids >> 7) * (2 * NQ) + (ids & (NQ - 1)) * 2 + ((ids >> 6) & 1)
    place = ((ids >> 5) & 1) * 8 + rank
    meta_ref[0:1, :] = owner
    meta_ref[1:2, :] = place
    here = iota((SLOT, NV), 0) == place
    copies[1].wait()
    n_block = NV // VIS_BLOCK
    clip = jnp.broadcast_to(clip_ref[...].astype(F32) * 0.25, (n_block, n_block))
    same = iota((n_block, n_block), 0) == iota((n_block, n_block), 1)
    clip = jnp.sum(jnp.where(same, clip, 0.0), 1, keepdims=True)
    block = iota((n_block, NV), 1) // VIS_BLOCK == iota((n_block, NV), 0)
    level = jnp.sum(jnp.where(block, clip, 0.0), 0, keepdims=True)
    copies[2].wait()
    copies[3].wait()
    values = [pos_ref[0:1, :], pos_ref[1:2, :], obs_ref[0:1, :], obs_ref[1:2, :], level]
    pieces = [split3(v) for v in values]
    own = jnp.where(iota((NDEV, NV), 0) == owner, 1.0, 0.0).astype(BF)
    table = jnp.concatenate(
        [jnp.where(here, p[part].astype(F32), 0.0).astype(BF) for part in range(3) for p in pieces]
        + [jnp.zeros((SLOT, NV), BF)], 0
    )
    copies[4].wait()
    meta_ref[2:3, :] = jnp.full((1, NV), off_ref[0, 1], jnp.int32)
    payload = lax.dot_general(own, table, (((1,), (1,)), ((), ())), preferred_element_type=F32)
    lane = iota((NDEV, LANES), 1)
    tail = payload[:, LANES:]
    tail = jnp.where(lane == A_HIGH - LANES, (off_ref[0, 0] >> 8).astype(F32), tail)
    tail = jnp.where(lane == A_HIGH + 1 - LANES, (off_ref[0, 0] & 255).astype(F32), tail)
    flat[pl.ds(NR2, NDEV, stride=MSG), :] = payload[:, :LANES]
    flat[pl.ds(NR2 + 1, NDEV, stride=MSG), :] = tail

    lane1 = iota((NQ, LANES), 1)
    freq = iota((NQ, LANES), 0) * (N_IMG // NQ) + (lane1 & (HALF - 1)) + lane1 // SUBG * HALF
    ph_c, ph_s = phase_of(off_ref[0, 1], freq)
    for copy in copies[5:]:
        copy.wait()
    for part in range(2):
        for a in range(NA):
            wide[part, a * RD:(a + 1) * RD, :] = slab_ref[
                0, part, :, a * LANES:(a + 1) * LANES
            ].astype(F32)
    tw_c, tw_s = tw_ref[:SUBG], tw_ref[SUBG:]
    col = table_ref[:LANES]
    coarse = jnp.concatenate(
        [
            jnp.concatenate([table_ref[LANES:LANES + NQ], table_ref[LANES + NQ:LANES + 2 * NQ]], 1),
            jnp.concatenate([table_ref[LANES + 2 * NQ:LANES + 3 * NQ], table_ref[LANES + 3 * NQ:]], 1),
        ], 0
    )
    low = lower((NQ, LANES))
    cols = [
        jnp.concatenate(
            [wide[0, pl.ds(r, NA, stride=RD), :], wide[1, pl.ds(r, NA, stride=RD), :]], 0
        ).astype(BF)
        for r in range(RD)
    ]
    y_ref[...] = jnp.dot(col, jnp.concatenate(cols, 1), preferred_element_type=F32)
    for row in range(NR2):
        both = []
        for r in (row, row + NR2):
            at = slice(r * LANES, (r + 1) * LANES)
            yr, yi = y_ref[:SUBG, at], y_ref[SUBG:, at]
            zr = yr * tw_c - yi * tw_s
            zi = yr * tw_s + yi * tw_c
            both.append(jnp.concatenate([zr, zi], 1).astype(BF))
        for i, (c, h) in enumerate(((0, 0), (0, 1), (1, 0), (1, 1))):
            at = row * LANES + i * HALF
            z_ref[at:at + HALF, :] = both[h][c * HALF:(c + 1) * HALF]
    out = lax.dot_general(
        coarse, z_ref[...], (((1,), (1,)), ((), ())), preferred_element_type=F32
    )
    for row in range(NR2):
        at = slice(row * LANES, (row + 1) * LANES)
        x, y = out[:NQ, at], out[NQ:, at]
        re, im = x * ph_c + y * ph_s, y * ph_c - x * ph_s
        pieces = [jnp.where(low, re, roll(im, SUBG)), jnp.where(low, roll(re, SUBG), im)]
        for c in range(2):
            for g in range(2):
                flat[pl.ds((2 * NQ * g + c) * MSG + row, NQ, stride=2 * MSG), :] = pieces[c]
    msg_ref[...] = flat[...].astype(BF)
    for copy in later:
        copy.wait()


def quarter_low(shape):
    return (iota(shape, len(shape) - 1) & HALF) == 0


def combine(both, rho):
    real, turned = 0.0, 0.0
    for t in range(2):
        rc, rs = rho[t, 0], rho[t, 1]
        a, b = both[:LANES, t * LANES:(t + 1) * LANES], both[LANES:, t * LANES:(t + 1) * LANES]
        real = real + (rc * a + rs * b)
        turned = turned + (rc * b - rs * a)
    real = real + roll(real, HALF)
    turned = turned + roll(turned, HALF)
    return (real - roll(turned, SUBG) * lane_sign(LANES, SUBG)).astype(BF)


def row_phases(tails, pair, rho_ref):
    first = (lax.axis_index("facet") // 2) * 4 + pair * 2
    low = quarter_low((1, LANES))
    start = [(v[:, 0:1] * 256.0 + v[:, 1:2]).astype(jnp.int32) for v in tails]
    starts = [jnp.where(low, start[2 * t], start[2 * t + 1]) for t in range(2)]
    eight = iota((8, LANES), 0)
    turn_c, turn_s = phase_of(
        jnp.where(eight < 4, starts[0], starts[1]), (first + (eight & 1)) * (N_IMG // 8)
    )
    for t in range(2):
        fine_c, fine_s = phase_of(starts[t], iota((SUBG, LANES), 0))
        for p in range(2):
            tc, ts = turn_c[t * 4 + p:t * 4 + p + 1], turn_s[t * 4 + p:t * 4 + p + 1]
            at = slice(p * SUBG, (p + 1) * SUBG)
            rho_ref[t, 0, at, :] = fine_c * tc - fine_s * ts
            rho_ref[t, 1, at, :] = fine_s * tc + fine_c * ts


def rows_kernel(got_ref, fwd_ref, give_ref, rhs_ref, rho_ref, raw_ref, flat):
    flat[...] = got_ref[...].astype(F32)
    core = lax.axis_index("sub") & 1
    at = A_HIGH - LANES
    tails = [flat[f * NQ * MSG + NR2 + 1:f * NQ * MSG + NR2 + 2, at:at + 2] for f in range(NF)]
    row_phases(tails, 1 - core, rho_ref)
    low = quarter_low((NQ, LANES))
    for row in range(NR2):
        x = [flat[pl.ds(f * NQ * MSG + row, NQ, stride=MSG), :] for f in range(NF)]
        for t in range(2):
            at = slice(t * LANES, (t + 1) * LANES)
            a, b = x[2 * t], x[2 * t + 1]
            rhs_ref[row * NQ:(row + 1) * NQ, at] = jnp.where(low, a, roll(b, HALF)).astype(BF)
            rhs_ref[(NR2 + row) * NQ:(NR2 + row + 1) * NQ, at] = jnp.where(
                low, roll(a, LANES - HALF), b
            ).astype(BF)
    both = jnp.dot(fwd_ref[1 - core], rhs_ref[...], preferred_element_type=F32)
    give_ref[...] = combine(both, rho_ref)
    raw_ref[0] = flat[pl.ds(NR2, NDEV, stride=MSG), :]
    raw_ref[1] = flat[pl.ds(NR2 + 1, NDEV, stride=MSG), :]


def times(a, b):
    return a[0] * b[0] - a[1] * b[1], a[0] * b[1] + a[1] * b[0]


def tables_kernel(raw_ref, fwd_ref, rhs_ref, keep_ref, vis_ref, rho_ref, left, basis, small):
    core = lax.axis_index("sub") & 1
    at = A_HIGH - LANES
    row_phases([raw_ref[1, f * NQ:f * NQ + 1, at:at + 2] for f in range(NF)], core, rho_ref)
    got = jnp.concatenate([raw_ref[0].T, raw_ref[1].T], 0)
    n = 5 * SLOT
    vis_ref[...] = got[:n] + got[n:2 * n] + got[2 * n:3 * n]
    both = jnp.dot(fwd_ref[core], rhs_ref[...], preferred_element_type=F32)
    keep_ref[...] = combine(both, rho_ref)
    slot = 0
    for l in range(2):
        for which in range(2):
            turn = vis_ref[which * SLOT + l * 8:which * SLOT + l * 8 + 8, :] * (1.0 / SUBG)
            p1 = sincos_turn(turn)
            ones = jnp.ones_like(turn)

            def ladder(p, unit):
                p2 = times(p, p)
                p3 = times(p2, p)
                p4 = times(p2, p2)
                return [unit, p, p2, p3, p4, times(p4, p), times(p3, p3), times(p4, p3)], p4

            low, p4 = ladder(p1, (ones, jnp.zeros_like(turn)))
            high, _ = ladder(times(p4, p4), (ones, jnp.zeros_like(turn)))
            for i in range(8):
                for part in range(2):
                    small[slot, part, i * 8:i * 8 + 8, :] = low[i][part]
                    small[slot, 2 + part, i * 8:i * 8 + 8, :] = high[i][part] * 0.125
            for k in range(8):
                at = slice(k * LANES, (k + 1) * LANES)
                br, bi, ar, ai = [small[slot, part, pl.ds(k, 8, stride=8), :] for part in range(4)]
                re, im = [], []
                for a in range(8):
                    hr, hi = ar[a:a + 1, :], ai[a:a + 1, :]
                    re.append(hr * br - hi * bi)
                    im.append(hr * bi + hi * br)
                if which == 0:
                    left[l, 0:SUBG, at] = jnp.concatenate(re, 0)
                    left[l, SUBG:, at] = jnp.concatenate(im, 0)
                else:
                    basis[l, 0:SUBG, at] = jnp.concatenate(re, 0).astype(BF)
                    basis[l, SUBG:, at] = jnp.concatenate(im, 0).astype(BF)
            slot += 1


def visibility_kernel(keep_ref, other_ref, vis_ref, left, basis, corrected_ref, back_ref, inner, phasor):
    upper_core = (lax.axis_index("sub") & 1) == 1
    keep, other = keep_ref[...].astype(F32), other_ref[...].astype(F32)
    halves = jnp.where(upper_core, other, keep), jnp.where(upper_core, keep, other)
    subgrids = jnp.where(quarter_low((LANES, LANES)), roll(halves[0], LANES - HALF), halves[1])
    sign = lane_sign(SUBG, SUBG)
    for l in range(2):
        sub = subgrids[l * SUBG:(l + 1) * SUBG]
        matrix = jnp.concatenate([sub * sign, roll(sub, SUBG)], 0).astype(BF)
        inner[l] = jnp.dot(matrix, basis[l], preferred_element_type=F32)
    predicted = [[], [], [], []]
    for l in range(2):
        for k in range(8):
            at = slice(k * LANES, (k + 1) * LANES)
            lr, li = left[l, 0:SUBG, at], left[l, SUBG:, at]
            ir, ii = inner[l, 0:SUBG, at], inner[l, SUBG:, at]
            predicted[l].append(jnp.sum(lr * ir - li * ii, 0, keepdims=True))
            predicted[2 + l].append(jnp.sum(lr * ii + li * ir, 0, keepdims=True))
    rows_of = lambda c: vis_ref[c * SLOT:(c + 1) * SLOT, :]
    mis_r = rows_of(2) - jnp.concatenate(predicted[0] + predicted[1], 0)
    mis_i = rows_of(3) - jnp.concatenate(predicted[2] + predicted[3], 0)
    level = rows_of(4)
    live = level > 0.0
    threshold = jnp.where(live, level, 1.0)
    magnitude = jnp.sqrt(mis_r * mis_r + mis_i * mis_i)
    weight = jnp.where(live, threshold / jnp.maximum(magnitude, threshold), 0.0)
    wr, wi = weight * mis_r, weight * mis_i
    for l in range(2):
        for k in range(8):
            at = slice(k * LANES, (k + 1) * LANES)
            lr, li = left[l, 0:SUBG, at], left[l, SUBG:, at]
            vr, vi = wr[l * 8 + k:l * 8 + k + 1, :], wi[l * 8 + k:l * 8 + k + 1, :]
            phasor[l, 0:SUBG, at] = (lr * vr + li * vi).astype(BF)
            phasor[l, SUBG:, at] = (lr * vi - li * vr).astype(BF)
    sums = []
    for l in range(2):
        product = lax.dot_general(
            phasor[l], basis[l], (((1,), (1,)), ((), ())), preferred_element_type=F32
        )
        sums.append(product[:SUBG] * sign + roll(product[SUBG:], SUBG))
    corrected_ref[...] = jnp.concatenate(sums, 0).astype(BF)
    back = jnp.concatenate([wr, wi], 0)
    back = [part.astype(F32) for part in split3(back)]
    back_ref[...] = jnp.concatenate(back + [jnp.zeros((2 * SLOT, LANES), F32)], 0)


def partial_images(x, pair, rho_ref, adj_ref):
    core = lax.axis_index("sub") & 1
    x = x.astype(F32)
    moved = jnp.where(core == 1, roll(x, LANES - HALF), roll(x, HALF))
    x = jnp.where(quarter_low(x.shape) != (core == 1), x, moved)
    turned = roll(x, SUBG) * -lane_sign(LANES, SUBG)
    cols = []
    for t in range(2):
        rc, rs = rho_ref[t, 0], rho_ref[t, 1]
        cols.append(
            jnp.concatenate([(x * rc + turned * rs).astype(BF), (x * rs - turned * rc).astype(BF)], 0)
        )
    half = NQ * NR2
    table = jnp.concatenate(
        [
            adj_ref[pair, pl.ds(pl.multiple_of(core * half, half), half), :],
            adj_ref[pair, pl.ds(pl.multiple_of((1 - core) * half, half), half), :],
        ], 0
    )
    return jnp.dot(table, jnp.concatenate(cols, 1), preferred_element_type=F32)


def mine_kernel(corrected_ref, rho_ref, adj_ref, part_ref):
    part_ref[...] = partial_images(corrected_ref[...], lax.axis_index("sub") & 1, rho_ref, adj_ref)


def images_kernel(part_ref, other_ref, back_ref, rho_ref, adj_ref, msg_ref, flat):
    pair = 1 - (lax.axis_index("sub") & 1)
    images = part_ref[...] + partial_images(other_ref[...], pair, rho_ref, adj_ref)
    low = quarter_low((NQ, LANES))
    for row in range(NR2):
        for t in range(2):
            at = slice(t * LANES, (t + 1) * LANES)
            a = images[row * NQ:(row + 1) * NQ, at]
            b = images[(NR2 + row) * NQ:(NR2 + row + 1) * NQ, at]
            flat[pl.ds(2 * t * NQ * MSG + row, NQ, stride=MSG), :] = jnp.where(low, a, roll(b, HALF))
            flat[pl.ds((2 * t + 1) * NQ * MSG + row, NQ, stride=MSG), :] = jnp.where(
                low, roll(a, LANES - HALF), b
            )
    flat[pl.ds(NR2, NDEV, stride=MSG), :] = back_ref[...].T
    flat[pl.ds(NR2 + 1, NDEV, stride=MSG), :] = jnp.zeros((NDEV, LANES), F32)
    msg_ref[...] = flat[...].astype(BF)


def facet_kernel(
    got_ref, meta_ref, coarse_ref, tw_ref, col_ref, out_hbm, res_hbm, flat, spread, z_ref, turned, out_ref, res_ref, sems,
):
    flat[...] = got_ref[...].astype(F32)
    n = 2 * SLOT
    back = flat[pl.ds(NR2, NDEV, stride=MSG), :].T[:3 * n]
    owner, place = meta_ref[0:1, :], meta_ref[1:2, :]
    own = jnp.where(iota((NDEV, NV), 0) == owner, 1.0, 0.0).astype(BF)
    found = jnp.dot(back.astype(BF), own, preferred_element_type=F32)
    found = found[:n] + found[n:2 * n] + found[2 * n:]
    here = iota((SLOT, NV), 0) == place
    for c in range(2):
        res_ref[c:c + 1, :] = jnp.sum(
            jnp.where(here, found[c * SLOT:(c + 1) * SLOT], 0.0), 0, keepdims=True
        )
    copies = [pltpu.make_async_copy(res_ref, res_hbm, sems.at[8])]
    copies[0].start()

    sign = -lane_sign(NQ, SUBG)
    low = quarter_low((NQ, LANES))
    for h in range(2):
        lane1 = iota((NQ, LANES), 1)
        freq = iota((NQ, LANES), 0) * (N_IMG // NQ) + ((lane1 & (SUBG - 1)) ^ (h * HALF))
        ph_c, ph_s = phase_of(meta_ref[2:3, :LANES], freq)
        images = []
        for row in range(NR2):
            x = [
                flat[pl.ds(c * MSG + row, NQ, stride=2 * MSG), :]
                + flat[pl.ds((2 * NQ + c) * MSG + row, NQ, stride=2 * MSG), :]
                for c in range(2)
            ]
            image = jnp.where(low, x[h], x[1 - h])
            turn = roll(image, SUBG) * sign
            images.append(
                jnp.concatenate([image * ph_c + turn * ph_s, turn * ph_c - image * ph_s], 0).astype(BF)
            )
        spread[h] = jnp.dot(coarse_ref[...], jnp.concatenate(images, 1), preferred_element_type=F32)
    for h in range(2):
        tw_c, tw_s = tw_ref[2 * h], tw_ref[2 * h + 1]
        for row in range(NR2):
            at = slice(row * LANES, (row + 1) * LANES)
            z_ref[h, at, :] = (tw_c * spread[h, :LANES, at] + tw_s * spread[h, LANES:, at]).astype(BF)
        out = lax.dot_general(
            col_ref[h * LANES:(h + 1) * LANES], z_ref[h], (((1,), (1,)), ((), ())),
            preferred_element_type=F32,
        )
        for part in range(2):
            for row in range(NR2):
                turned[h, part, pl.ds(row, NA, stride=NR2), :] = out[
                    part * NA:(part + 1) * NA, row * LANES:(row + 1) * LANES
                ]
            where = slice(h * NR2, (h + 1) * NR2)
            for piece in range(2):
                for a in range(piece * NA // 2, (piece + 1) * NA // 2):
                    out_ref[part, where, a * LANES:(a + 1) * LANES] = turned[
                        h, part, a * NR2:(a + 1) * NR2, :
                    ]
                wide = slice(piece * NA // 2 * LANES, (piece + 1) * NA // 2 * LANES)
                copy = pltpu.make_async_copy(
                    out_ref.at[part, where, wide], out_hbm.at[0, part, where, wide],
                    sems.at[(h * 2 + part) * 2 + piece],
                )
                copy.start()
                copies.append(copy)
    for copy in copies:
        copy.wait()


VMEM = pl.BlockSpec(memory_space=pltpu.VMEM)
HBM = pl.BlockSpec(memory_space=pltpu.MemorySpace.HBM)
TABLES = host_tables()


def in_place(arrays):
    return [pltpu.with_memory_space_constraint(x, pltpu.HBM) for x in arrays]


def exchange(message):
    pairs = message.reshape(NDEV * MSG // 2, 2, LANES)
    return lax.all_to_all(pairs, ALL, split_axis=0, concat_axis=0, tiled=True).reshape(message.shape)


def other_core(x):
    return lax.ppermute(x, "sub", [(i, i ^ 1) for i in range(NQ)])


def on_device(slab, offsets, position, observed, subgrid_of, clip):
    t = {name: jnp.asarray(value) for name, value in TABLES.items()}
    limit = pltpu.CompilerParams(vmem_limit_bytes=32 << 20)
    shape = jax.ShapeDtypeStruct
    message = shape((NDEV * MSG, LANES), BF)
    fwd_table = shape((2, 4 * SUBG, NQ * RD), BF)
    adj_table = shape((2, NQ * RD, 4 * SUBG), BF)
    square = shape((LANES, LANES), BF)
    phases = shape((2, 2, LANES, LANES), F32)
    flat = pltpu.VMEM((NDEV * MSG, LANES), F32)

    def call(kernel, name, inputs, outs, scratch, in_specs=None, out_specs=None, flops=1 << 20):
        return pl.pallas_call(
            kernel,
            out_shape=outs,
            in_specs=in_specs or [VMEM] * len(inputs),
            out_specs=out_specs or (VMEM,) * len(outs),
            scratch_shapes=scratch,
            compiler_params=limit,
            cost_estimate=pl.CostEstimate(flops=flops, bytes_accessed=1 << 21, transcendentals=0),
            name=name,
        )(*inputs)

    inputs = (
        offsets, slab, position, observed, subgrid_of.reshape(1, NV),
        clip.reshape(1, NV // VIS_BLOCK), t["column"], t["tw_fwd"],
    )
    sent, meta, fwd, adj = call(
        send_kernel, "send", in_place(inputs + (t["row_fwd"], t["row_adj"])),
        (message, shape((8, NV), jnp.int32), fwd_table, adj_table),
        [pltpu.SMEM((1, 2), jnp.int32)]
        + [pltpu.VMEM(x.shape, x.dtype) for x in inputs[1:]]
        + [
            pltpu.VMEM((2, NA * RD, LANES), F32),
            flat,
            pltpu.VMEM((LANES, RD * LANES), F32),
            pltpu.VMEM((NR2 * LANES, 2 * LANES), BF),
            pltpu.SemaphoreType.DMA((len(inputs) + 2,)),
        ],
        in_specs=[HBM] * (len(inputs) + 2),
    )
    got = exchange(sent)
    give, rhs, other_rho, raw = call(
        rows_kernel, "rows", (got, fwd),
        (
            square, shape((NQ * RD, 2 * LANES), BF), phases, shape((2, NDEV, LANES), F32),
        ),
        [flat],
    )
    other = other_core(give)
    keep, vis, rho, left, basis = call(
        tables_kernel, "tables", (raw, fwd, rhs),
        (
            square, shape((5 * SLOT, LANES), F32), phases, shape((2, 2 * SUBG, NV), F32),
            shape((2, 2 * SUBG, NV), BF),
        ),
        [pltpu.VMEM((4, 4, SUBG, LANES), F32)],
    )
    corrected, back = call(
        visibility_kernel, "visibilities", (keep, other, vis, left, basis),
        (square, shape((LANES, LANES), F32)),
        [pltpu.VMEM((2, 2 * SUBG, NV), F32), pltpu.VMEM((2, 2 * SUBG, NV), BF)],
    )
    other = other_core(corrected)
    (part,) = call(
        mine_kernel, "mine", (corrected, rho, adj), (shape((NQ * RD, 2 * LANES), F32),), []
    )
    (answer,) = call(images_kernel, "images", (part, other, back, other_rho, adj), (message,), [flat])
    facet_adjoint, residual = call(
        facet_kernel, "facet",
        (exchange(answer), meta, t["coarse_adj"], t["tw_adj"], t["col_adj"]),
        (shape((1, 2, RD, NA * LANES), F32), shape((2, NV), F32)),
        [
            flat,
            pltpu.VMEM((2, 2 * LANES, NR2 * LANES), F32),
            pltpu.VMEM((2, NR2 * LANES, LANES), BF),
            pltpu.VMEM((2, 2, NA * NR2, LANES), F32),
            pltpu.VMEM((2, RD, NA * LANES), F32),
            pltpu.VMEM((2, NV), F32),
            pltpu.SemaphoreType.DMA((9,)),
        ],
        out_specs=(HBM, HBM),
    )
    return (facet_adjoint, residual)


def solution(mesh):
    placed = (
        P("facet", None, "sub", None),
        P("facet", None),
        P(None, ALL),
        P(None, ALL),
        P(ALL, None),
        P(ALL),
    )
    return jax.shard_map(
        on_device,
        mesh=mesh,
        in_specs=placed,
        out_specs=(P("facet", None, "sub", None), P(None, ALL)),
        check_vma=False,
    )
```

```python
import math

import jax
import jax.numpy as jnp
import numpy as np
from jax import lax
from jax.experimental import pallas as pl
from jax.experimental.pallas import tpu as pltpu
from jax.sharding import PartitionSpec as P

N_IMG = 32768
SUBG = 64
HALF = 32
VIS_BLOCK = 32
LANES = 128
NQ = 32
NF = 4
NDEV = 128
RD = 16
NR2 = 8
NA = 64
NV = 1024
SLOT = 16
MSG = 10
A_HIGH = 3 * 5 * SLOT
TWO_PI = 2.0 * math.pi
BF = jnp.bfloat16
F32 = jnp.float32
ALL = ("facet", "sub")


def unit(index, period):
    angle = TWO_PI * (np.asarray(index, np.int64) % period) / period
    return np.cos(angle), np.sin(angle)


def host_tables():
    block = np.arange(NA)
    lane = np.arange(LANES)
    fine = np.arange(SUBG)
    coarse = np.arange(NQ)
    c, s = unit(fine[:, None] * block[None, :], 256)
    c, s = c / 64.0, s / 64.0
    col_fwd = np.block([[c, s], [-s, c]])
    col_adj = np.block([[c.T, -s.T], [s.T, c.T]])
    tw_c, tw_s = unit(fine[:, None] * lane[None, :], N_IMG)
    twiddle_fwd = np.concatenate([tw_c, -tw_s], 0)
    orders = [fine, fine ^ HALF]
    twiddle_adj = np.stack([np.tile(x.T[:, o], (1, 2)) for o in orders for x in (tw_c, tw_s)])
    col_adj = np.concatenate([col_adj[:, np.concatenate([o, o + SUBG])] for o in orders], 0)
    wc, ws = unit(coarse[:, None] * lane[None, :], 32)
    column = np.concatenate([col_fwd, wc, ws, -ws, wc], 0)
    coarse_adj = np.block([[wc.T, ws.T], [-ws.T, wc.T]])
    k_row = (np.arange(8)[:, None] * 4096 + fine[None, :]).reshape(2, 4 * SUBG)
    r = np.arange(NQ * RD).reshape(NQ, 2, NR2).transpose(1, 2, 0).reshape(-1)
    rc, rs = unit(k_row[:, :, None] * r[None, None, :], N_IMG)
    pairs = lambda x: x.reshape(2, 2, 2 * SUBG, NQ * RD) / 64.0
    row_fwd = np.concatenate([pairs(rc), -pairs(rs)], 2)
    row_adj = np.ascontiguousarray(row_fwd.transpose(0, 1, 3, 2))
    bf = lambda x: np.asarray(x, np.float32).astype(jnp.bfloat16)
    return dict(
        column=bf(column),
        col_adj=bf(col_adj),
        tw_fwd=np.asarray(twiddle_fwd, np.float32),
        tw_adj=np.asarray(twiddle_adj, np.float32),
        coarse_adj=bf(coarse_adj),
        row_fwd=bf(row_fwd),
        row_adj=bf(row_adj),
    )


def sincos_turn(turn):
    quarter = jnp.floor(turn * 4.0 + 0.5)
    y = (turn - quarter * 0.25) * TWO_PI
    y2 = y * y
    s = y * (1.0 + y2 * (-1.0 / 6 + y2 * (1.0 / 120 + y2 * (-1.0 / 5040 + y2 * (1.0 / 362880)))))
    c = 1.0 + y2 * (-0.5 + y2 * (1.0 / 24 + y2 * (-1.0 / 720 + y2 * (1.0 / 40320))))
    turns = quarter.astype(jnp.int32)
    odd = (turns & 1) == 1
    cos = jnp.where(odd, s, c)
    sin = jnp.where(odd, c, s)
    cos = jnp.where(((turns + 1) & 2) == 2, -cos, cos)
    sin = jnp.where((turns & 2) == 2, -sin, sin)
    return cos, sin


def phase_of(offset, frequency):
    index = (offset * frequency) & (N_IMG - 1)
    return sincos_turn(index.astype(F32) * (1.0 / N_IMG))


def iota(shape, dim):
    return lax.broadcasted_iota(jnp.int32, shape, dim)


def roll(x, shift):
    return pltpu.roll(x, shift, x.ndim - 1)


def lane_sign(rows, width):
    return jnp.where((iota((rows, LANES), 1) & width) == 0, 1.0, -1.0).astype(F32)


def lower(shape):
    return iota(shape, len(shape) - 1) < SUBG


def split3(x):
    high = x.astype(BF)
    rest = x - high.astype(F32)
    middle = rest.astype(BF)
    low = (rest - middle.astype(F32)).astype(BF)
    return high, middle, low


def send_kernel(
    off_hbm, slab_hbm, pos_hbm, obs_hbm, ids_hbm, ids8_hbm, clip_hbm, table_hbm, tw_hbm, fwd_hbm, adj_hbm,
    msg_ref, meta_ref, fwd_ref, adj_ref, off_ref, slab_ref, pos_ref, obs_ref, ids_ref, ids8_ref, clip_ref, table_ref, tw_ref,
    wide, flat, y_ref, z_ref, sems,
):
    pairs = [
        (ids_hbm, ids_ref), (ids8_hbm, ids8_ref), (clip_hbm, clip_ref), (pos_hbm, pos_ref), (obs_hbm, obs_ref),
        (off_hbm, off_ref), (slab_hbm, slab_ref), (table_hbm, table_ref), (tw_hbm, tw_ref),
    ]
    copies = [pltpu.make_async_copy(a, b, sems.at[i]) for i, (a, b) in enumerate(pairs)]
    four = lax.axis_index("facet") // 2
    later = [
        pltpu.make_async_copy(fwd_hbm.at[four], fwd_ref, sems.at[len(pairs)]),
        pltpu.make_async_copy(adj_hbm.at[four], adj_ref, sems.at[len(pairs) + 1]),
    ]
    for copy in copies + later:
        copy.start()

    copies[0].wait()
    copies[1].wait()
    ids = ids_ref[...]
    n_tile = NV // LANES
    column = ids8_ref[...].astype(F32).T
    row_ids = ids.astype(F32).astype(BF)
    zero, one = jnp.zeros((), BF), jnp.ones((), BF)
    above = iota((LANES, LANES), 0) < iota((LANES, LANES), 1)
    above = jnp.where(above, 1.0, 0.0).astype(BF)
    counts = [None] * n_tile
    for b in range(n_tile):
        mine = jnp.broadcast_to(column[:, b:b + 1], (LANES, LANES)).astype(BF)
        for c in range(b, n_tile):
            other = jnp.broadcast_to(row_ids[:, c * LANES:(c + 1) * LANES], (LANES, LANES))
            same = jnp.where(mine == other, above if b == c else one, zero)
            counts[c] = same if b == 0 else counts[c] + same
    ranks = []
    for c in range(n_tile):
        part = counts[c]
        while part.shape[0] > 16:
            half = part.shape[0] // 2
            part = part[:half] + part[half:]
        ranks.append(jnp.sum(part.astype(F32), 0, keepdims=True))
    rank = jnp.concatenate(ranks, 1).astype(jnp.int32)
    owner = (ids >> 7) * (2 * NQ) + (ids & (NQ - 1)) * 2 + ((ids >> 6) & 1)
    place = ((ids >> 5) & 1) * 8 + rank
    meta_ref[0:1, :] = owner
    meta_ref[1:2, :] = place
    here = iota((SLOT, NV), 0).astype(F32).astype(BF) == place.astype(F32).astype(BF)
    copies[2].wait()
    n_block = NV // VIS_BLOCK
    clip = jnp.broadcast_to(clip_ref[...].astype(F32) * 0.25, (n_block, n_block))
    same = iota((n_block, n_block), 0) == iota((n_block, n_block), 1)
    clip = jnp.sum(jnp.where(same, clip, 0.0), 1, keepdims=True)
    block = iota((n_block, NV), 1) // VIS_BLOCK == iota((n_block, NV), 0)
    level = jnp.sum(jnp.where(block, clip, 0.0), 0, keepdims=True)
    copies[3].wait()
    copies[4].wait()
    values = [pos_ref[0:1, :], pos_ref[1:2, :], obs_ref[0:1, :], obs_ref[1:2, :], level]
    pieces = [split3(v) for v in values]
    own = jnp.where(
        iota((NDEV, NV), 0).astype(F32).astype(BF) == owner.astype(F32).astype(BF), one, zero
    )
    table = jnp.concatenate(
        [
            jnp.where(here, jnp.broadcast_to(p[part], (SLOT, NV)), zero)
            for part in range(3) for p in pieces
        ]
        + [jnp.zeros((SLOT, NV), BF)], 0
    )
    copies[5].wait()
    meta_ref[2:3, :] = jnp.full((1, NV), off_ref[0, 1], jnp.int32)
    payload = lax.dot_general(own, table, (((1,), (1,)), ((), ())), preferred_element_type=F32)
    lane = iota((NDEV, LANES), 1)
    tail = payload[:, LANES:]
    tail = jnp.where(lane == A_HIGH - LANES, (off_ref[0, 0] >> 8).astype(F32), tail)
    tail = jnp.where(lane == A_HIGH + 1 - LANES, (off_ref[0, 0] & 255).astype(F32), tail)
    flat[pl.ds(NR2, NDEV, stride=MSG), :] = payload[:, :LANES]
    flat[pl.ds(NR2 + 1, NDEV, stride=MSG), :] = tail

    lane1 = iota((NQ, LANES), 1)
    freq = iota((NQ, LANES), 0) * (N_IMG // NQ) + (lane1 & (HALF - 1)) + lane1 // SUBG * HALF
    ph_c, ph_s = phase_of(off_ref[0, 1], freq)
    for copy in copies[6:]:
        copy.wait()
    for part in range(2):
        for a in range(NA):
            wide[part, a * RD:(a + 1) * RD, :] = slab_ref[
                0, part, :, a * LANES:(a + 1) * LANES
            ].astype(F32)
    tw_c, tw_s = tw_ref[:SUBG], tw_ref[SUBG:]
    col = table_ref[:LANES]
    coarse = jnp.concatenate(
        [
            jnp.concatenate([table_ref[LANES:LANES + NQ], table_ref[LANES + NQ:LANES + 2 * NQ]], 1),
            jnp.concatenate([table_ref[LANES + 2 * NQ:LANES + 3 * NQ], table_ref[LANES + 3 * NQ:]], 1),
        ], 0
    )
    low = lower((NQ, LANES))
    cols = [
        jnp.concatenate(
            [wide[0, pl.ds(r, NA, stride=RD), :], wide[1, pl.ds(r, NA, stride=RD), :]], 0
        ).astype(BF)
        for r in range(RD)
    ]
    y_ref[...] = jnp.dot(col, jnp.concatenate(cols, 1), preferred_element_type=F32)
    for row in range(NR2):
        both = []
        for r in (row, row + NR2):
            at = slice(r * LANES, (r + 1) * LANES)
            yr, yi = y_ref[:SUBG, at], y_ref[SUBG:, at]
            zr = yr * tw_c - yi * tw_s
            zi = yr * tw_s + yi * tw_c
            both.append(jnp.concatenate([zr, zi], 1).astype(BF))
        for i, (c, h) in enumerate(((0, 0), (0, 1), (1, 0), (1, 1))):
            at = row * LANES + i * HALF
            z_ref[at:at + HALF, :] = both[h][c * HALF:(c + 1) * HALF]
    out = lax.dot_general(
        coarse, z_ref[...], (((1,), (1,)), ((), ())), preferred_element_type=F32
    )
    for row in range(NR2):
        at = slice(row * LANES, (row + 1) * LANES)
        x, y = out[:NQ, at], out[NQ:, at]
        re, im = x * ph_c + y * ph_s, y * ph_c - x * ph_s
        pieces = [jnp.where(low, re, roll(im, SUBG)), jnp.where(low, roll(re, SUBG), im)]
        for c in range(2):
            for g in range(2):
                flat[pl.ds((2 * NQ * g + c) * MSG + row, NQ, stride=2 * MSG), :] = pieces[c]
    msg_ref[...] = flat[...].astype(BF)
    for copy in later:
        copy.wait()


def quarter_low(shape):
    return (iota(shape, len(shape) - 1) & HALF) == 0


def combine(both, rho):
    real, turned = 0.0, 0.0
    for t in range(2):
        rc, rs = rho[t, 0], rho[t, 1]
        a, b = both[:LANES, t * LANES:(t + 1) * LANES], both[LANES:, t * LANES:(t + 1) * LANES]
        real = real + (rc * a + rs * b)
        turned = turned + (rc * b - rs * a)
    real = real + roll(real, HALF)
    turned = turned + roll(turned, HALF)
    return (real - roll(turned, SUBG) * lane_sign(LANES, SUBG)).astype(BF)


def row_phases(tails, pair, rho_ref):
    first = (lax.axis_index("facet") // 2) * 4 + pair * 2
    low = quarter_low((1, LANES))
    start = [(v[:, 0:1] * 256.0 + v[:, 1:2]).astype(jnp.int32) for v in tails]
    starts = [jnp.where(low, start[2 * t], start[2 * t + 1]) for t in range(2)]
    eight = iota((8, LANES), 0)
    turn_c, turn_s = phase_of(
        jnp.where(eight < 4, starts[0], starts[1]), (first + (eight & 1)) * (N_IMG // 8)
    )
    for t in range(2):
        low_c, low_s = phase_of(starts[t], eight)
        high_c, high_s = phase_of(starts[t], eight * 8)
        for p in range(2):
            tc, ts = turn_c[t * 4 + p:t * 4 + p + 1], turn_s[t * 4 + p:t * 4 + p + 1]
            hc, hs = high_c * tc - high_s * ts, high_s * tc + high_c * ts
            for a in range(8):
                at = slice(p * SUBG + a * 8, p * SUBG + a * 8 + 8)
                ac, asin = hc[a:a + 1], hs[a:a + 1]
                rho_ref[t, 0, at, :] = low_c * ac - low_s * asin
                rho_ref[t, 1, at, :] = low_s * ac + low_c * asin


def rows_kernel(got_ref, fwd_ref, give_ref, rhs_ref, rho_ref, raw_ref, flat):
    flat[...] = got_ref[...].astype(F32)
    core = lax.axis_index("sub") & 1
    at = A_HIGH - LANES
    tails = [flat[f * NQ * MSG + NR2 + 1:f * NQ * MSG + NR2 + 2, at:at + 2] for f in range(NF)]
    row_phases(tails, 1 - core, rho_ref)
    low = quarter_low((NQ, LANES))
    for row in range(NR2):
        x = [flat[pl.ds(f * NQ * MSG + row, NQ, stride=MSG), :] for f in range(NF)]
        for t in range(2):
            at = slice(t * LANES, (t + 1) * LANES)
            a, b = x[2 * t], x[2 * t + 1]
            rhs_ref[row * NQ:(row + 1) * NQ, at] = jnp.where(low, a, roll(b, HALF)).astype(BF)
            rhs_ref[(NR2 + row) * NQ:(NR2 + row + 1) * NQ, at] = jnp.where(
                low, roll(a, LANES - HALF), b
            ).astype(BF)
    both = jnp.dot(fwd_ref[1 - core], rhs_ref[...], preferred_element_type=F32)
    give_ref[...] = combine(both, rho_ref)
    raw_ref[0] = flat[pl.ds(NR2, NDEV, stride=MSG), :]
    raw_ref[1] = flat[pl.ds(NR2 + 1, NDEV, stride=MSG), :]


def times(a, b):
    return a[0] * b[0] - a[1] * b[1], a[0] * b[1] + a[1] * b[0]


def tables_kernel(raw_ref, fwd_ref, rhs_ref, keep_ref, vis_ref, rho_ref, left, basis, small):
    core = lax.axis_index("sub") & 1
    at = A_HIGH - LANES
    row_phases([raw_ref[1, f * NQ:f * NQ + 1, at:at + 2] for f in range(NF)], core, rho_ref)
    got = jnp.concatenate([raw_ref[0].T, raw_ref[1].T], 0)
    n = 5 * SLOT
    vis_ref[...] = got[:n] + got[n:2 * n] + got[2 * n:3 * n]
    both = jnp.dot(fwd_ref[core], rhs_ref[...], preferred_element_type=F32)
    keep_ref[...] = combine(both, rho_ref)
    slot = 0
    for l in range(2):
        for which in range(2):
            turn = vis_ref[which * SLOT + l * 8:which * SLOT + l * 8 + 8, :] * (1.0 / SUBG)
            p1 = sincos_turn(turn)
            ones = jnp.ones_like(turn)

            def ladder(p, unit):
                p2 = times(p, p)
                p3 = times(p2, p)
                p4 = times(p2, p2)
                return [unit, p, p2, p3, p4, times(p4, p), times(p3, p3), times(p4, p3)], p4

            low, p4 = ladder(p1, (ones, jnp.zeros_like(turn)))
            high, _ = ladder(times(p4, p4), (ones, jnp.zeros_like(turn)))
            for i in range(8):
                for part in range(2):
                    small[slot, part, i * 8:i * 8 + 8, :] = low[i][part]
                    small[slot, 2 + part, i * 8:i * 8 + 8, :] = high[i][part] * 0.125
            for k in range(8):
                at = slice(k * LANES, (k + 1) * LANES)
                br, bi, ar, ai = [small[slot, part, pl.ds(k, 8, stride=8), :] for part in range(4)]
                re, im = [], []
                for a in range(8):
                    hr, hi = ar[a:a + 1, :], ai[a:a + 1, :]
                    re.append(hr * br - hi * bi)
                    im.append(hr * bi + hi * br)
                if which == 0:
                    left[l, 0:SUBG, at] = jnp.concatenate(re, 0)
                    left[l, SUBG:, at] = jnp.concatenate(im, 0)
                else:
                    basis[l, 0:SUBG, at] = jnp.concatenate(re, 0).astype(BF)
                    basis[l, SUBG:, at] = jnp.concatenate(im, 0).astype(BF)
            slot += 1


def visibility_kernel(keep_ref, other_ref, vis_ref, left, basis, corrected_ref, back_ref, inner, phasor):
    upper_core = (lax.axis_index("sub") & 1) == 1
    keep, other = keep_ref[...].astype(F32), other_ref[...].astype(F32)
    halves = jnp.where(upper_core, other, keep), jnp.where(upper_core, keep, other)
    subgrids = jnp.where(quarter_low((LANES, LANES)), roll(halves[0], LANES - HALF), halves[1])
    sign = lane_sign(SUBG, SUBG)
    for l in range(2):
        sub = subgrids[l * SUBG:(l + 1) * SUBG]
        matrix = jnp.concatenate([sub * sign, roll(sub, SUBG)], 0).astype(BF)
        inner[l] = jnp.dot(matrix, basis[l], preferred_element_type=F32)
    predicted = [[], [], [], []]
    for l in range(2):
        for k in range(8):
            at = slice(k * LANES, (k + 1) * LANES)
            lr, li = left[l, 0:SUBG, at], left[l, SUBG:, at]
            ir, ii = inner[l, 0:SUBG, at], inner[l, SUBG:, at]
            predicted[l].append(jnp.sum(lr * ir - li * ii, 0, keepdims=True))
            predicted[2 + l].append(jnp.sum(lr * ii + li * ir, 0, keepdims=True))
    rows_of = lambda c: vis_ref[c * SLOT:(c + 1) * SLOT, :]
    mis_r = rows_of(2) - jnp.concatenate(predicted[0] + predicted[1], 0)
    mis_i = rows_of(3) - jnp.concatenate(predicted[2] + predicted[3], 0)
    level = rows_of(4)
    live = level > 0.0
    threshold = jnp.where(live, level, 1.0)
    magnitude = jnp.sqrt(mis_r * mis_r + mis_i * mis_i)
    weight = jnp.where(live, threshold / jnp.maximum(magnitude, threshold), 0.0)
    wr, wi = weight * mis_r, weight * mis_i
    for l in range(2):
        for k in range(8):
            at = slice(k * LANES, (k + 1) * LANES)
            lr, li = left[l, 0:SUBG, at], left[l, SUBG:, at]
            vr, vi = wr[l * 8 + k:l * 8 + k + 1, :], wi[l * 8 + k:l * 8 + k + 1, :]
            phasor[l, 0:SUBG, at] = (lr * vr + li * vi).astype(BF)
            phasor[l, SUBG:, at] = (lr * vi - li * vr).astype(BF)
    sums = []
    for l in range(2):
        product = lax.dot_general(
            phasor[l], basis[l], (((1,), (1,)), ((), ())), preferred_element_type=F32
        )
        sums.append(product[:SUBG] * sign + roll(product[SUBG:], SUBG))
    corrected_ref[...] = jnp.concatenate(sums, 0).astype(BF)
    back_ref[...] = jnp.concatenate([wr, wi], 0)


def partial_images(x, pair, rho_ref, adj_ref):
    core = lax.axis_index("sub") & 1
    x = x.astype(F32)
    moved = jnp.where(core == 1, roll(x, LANES - HALF), roll(x, HALF))
    x = jnp.where(quarter_low(x.shape) != (core == 1), x, moved)
    turned = roll(x, SUBG) * -lane_sign(LANES, SUBG)
    cols = []
    for t in range(2):
        rc, rs = rho_ref[t, 0], rho_ref[t, 1]
        cols.append(
            jnp.concatenate([(x * rc + turned * rs).astype(BF), (x * rs - turned * rc).astype(BF)], 0)
        )
    half = NQ * NR2
    table = jnp.concatenate(
        [
            adj_ref[pair, pl.ds(pl.multiple_of(core * half, half), half), :],
            adj_ref[pair, pl.ds(pl.multiple_of((1 - core) * half, half), half), :],
        ], 0
    )
    return jnp.dot(table, jnp.concatenate(cols, 1), preferred_element_type=F32)


def mine_kernel(corrected_ref, back_ref, rho_ref, adj_ref, part_ref, tail_ref):
    back = [part.astype(F32) for part in split3(back_ref[...])]
    tail_ref[...] = jnp.concatenate(back + [jnp.zeros((2 * SLOT, LANES), F32)], 0).T
    part_ref[...] = partial_images(corrected_ref[...], lax.axis_index("sub") & 1, rho_ref, adj_ref)


def images_kernel(part_ref, other_ref, tail_ref, rho_ref, adj_ref, msg_ref, flat):
    pair = 1 - (lax.axis_index("sub") & 1)
    images = part_ref[...] + partial_images(other_ref[...], pair, rho_ref, adj_ref)
    low = quarter_low((NQ, LANES))
    for row in range(NR2):
        for t in range(2):
            at = slice(t * LANES, (t + 1) * LANES)
            a = images[row * NQ:(row + 1) * NQ, at]
            b = images[(NR2 + row) * NQ:(NR2 + row + 1) * NQ, at]
            flat[pl.ds(2 * t * NQ * MSG + row, NQ, stride=MSG), :] = jnp.where(low, a, roll(b, HALF))
            flat[pl.ds((2 * t + 1) * NQ * MSG + row, NQ, stride=MSG), :] = jnp.where(
                low, roll(a, LANES - HALF), b
            )
    flat[pl.ds(NR2, NDEV, stride=MSG), :] = tail_ref[...]
    flat[pl.ds(NR2 + 1, NDEV, stride=MSG), :] = jnp.zeros((NDEV, LANES), F32)
    msg_ref[...] = flat[...].astype(BF)


def facet_kernel(
    got_ref, meta_ref, coarse_ref, tw_ref, col_ref, out_hbm, res_hbm, flat, spread, z_ref, turned, out_ref, res_ref, sems,
):
    flat[...] = got_ref[...].astype(F32)
    n = 2 * SLOT
    back = flat[pl.ds(NR2, NDEV, stride=MSG), :].T[:3 * n]
    owner, place = meta_ref[0:1, :], meta_ref[1:2, :]
    own = jnp.where(iota((NDEV, NV), 0) == owner, 1.0, 0.0).astype(BF)
    found = jnp.dot(back.astype(BF), own, preferred_element_type=F32)
    found = found[:n] + found[n:2 * n] + found[2 * n:]
    here = iota((SLOT, NV), 0) == place
    for c in range(2):
        res_ref[c:c + 1, :] = jnp.sum(
            jnp.where(here, found[c * SLOT:(c + 1) * SLOT], 0.0), 0, keepdims=True
        )
    copies = [pltpu.make_async_copy(res_ref, res_hbm, sems.at[8])]
    copies[0].start()

    sign = -lane_sign(NQ, SUBG)
    low = quarter_low((NQ, LANES))
    for h in range(2):
        lane1 = iota((NQ, LANES), 1)
        freq = iota((NQ, LANES), 0) * (N_IMG // NQ) + ((lane1 & (SUBG - 1)) ^ (h * HALF))
        ph_c, ph_s = phase_of(meta_ref[2:3, :LANES], freq)
        images = []
        for row in range(NR2):
            x = [
                flat[pl.ds(c * MSG + row, NQ, stride=2 * MSG), :]
                + flat[pl.ds((2 * NQ + c) * MSG + row, NQ, stride=2 * MSG), :]
                for c in range(2)
            ]
            image = jnp.where(low, x[h], x[1 - h])
            turn = roll(image, SUBG) * sign
            images.append(
                jnp.concatenate([image * ph_c + turn * ph_s, turn * ph_c - image * ph_s], 0).astype(BF)
            )
        spread[h] = jnp.dot(coarse_ref[...], jnp.concatenate(images, 1), preferred_element_type=F32)
    for h in range(2):
        tw_c, tw_s = tw_ref[2 * h], tw_ref[2 * h + 1]
        for row in range(NR2):
            at = slice(row * LANES, (row + 1) * LANES)
            z_ref[h, at, :] = (tw_c * spread[h, :LANES, at] + tw_s * spread[h, LANES:, at]).astype(BF)
        out = lax.dot_general(
            col_ref[h * LANES:(h + 1) * LANES], z_ref[h], (((1,), (1,)), ((), ())),
            preferred_element_type=F32,
        )
        for part in range(2):
            for row in range(NR2):
                turned[h, part, pl.ds(row, NA, stride=NR2), :] = out[
                    part * NA:(part + 1) * NA, row * LANES:(row + 1) * LANES
                ]
            where = slice(h * NR2, (h + 1) * NR2)
            for piece in range(2):
                for a in range(piece * NA // 2, (piece + 1) * NA // 2):
                    out_ref[part, where, a * LANES:(a + 1) * LANES] = turned[
                        h, part, a * NR2:(a + 1) * NR2, :
                    ]
                wide = slice(piece * NA // 2 * LANES, (piece + 1) * NA // 2 * LANES)
                copy = pltpu.make_async_copy(
                    out_ref.at[part, where, wide], out_hbm.at[0, part, where, wide],
                    sems.at[(h * 2 + part) * 2 + piece],
                )
                copy.start()
                copies.append(copy)
    for copy in copies:
        copy.wait()


VMEM = pl.BlockSpec(memory_space=pltpu.VMEM)
HBM = pl.BlockSpec(memory_space=pltpu.MemorySpace.HBM)
TABLES = host_tables()


def in_place(arrays):
    return [pltpu.with_memory_space_constraint(x, pltpu.HBM) for x in arrays]


def exchange(message):
    pairs = message.reshape(NDEV * MSG // 2, 2, LANES)
    return lax.all_to_all(pairs, ALL, split_axis=0, concat_axis=0, tiled=True).reshape(message.shape)


def other_core(x):
    return lax.ppermute(x, "sub", [(i, i ^ 1) for i in range(NQ)])


def on_device(slab, offsets, position, observed, subgrid_of, clip):
    t = {name: jnp.asarray(value) for name, value in TABLES.items()}
    limit = pltpu.CompilerParams(vmem_limit_bytes=32 << 20)
    shape = jax.ShapeDtypeStruct
    message = shape((NDEV * MSG, LANES), BF)
    fwd_table = shape((2, 4 * SUBG, NQ * RD), BF)
    adj_table = shape((2, NQ * RD, 4 * SUBG), BF)
    square = shape((LANES, LANES), BF)
    phases = shape((2, 2, LANES, LANES), F32)
    flat = pltpu.VMEM((NDEV * MSG, LANES), F32)

    def call(kernel, name, inputs, outs, scratch, in_specs=None, out_specs=None, flops=1 << 20):
        return pl.pallas_call(
            kernel,
            out_shape=outs,
            in_specs=in_specs or [VMEM] * len(inputs),
            out_specs=out_specs or (VMEM,) * len(outs),
            scratch_shapes=scratch,
            compiler_params=limit,
            cost_estimate=pl.CostEstimate(flops=flops, bytes_accessed=1 << 21, transcendentals=0),
            name=name,
        )(*inputs)

    inputs = (
        offsets, slab, position, observed, subgrid_of.reshape(1, NV), subgrid_of.reshape(8, LANES),
        clip.reshape(1, NV // VIS_BLOCK), t["column"], t["tw_fwd"],
    )
    sent, meta, fwd, adj = call(
        send_kernel, "send", in_place(inputs + (t["row_fwd"], t["row_adj"])),
        (message, shape((8, NV), jnp.int32), fwd_table, adj_table),
        [pltpu.SMEM((1, 2), jnp.int32)]
        + [pltpu.VMEM(x.shape, x.dtype) for x in inputs[1:]]
        + [
            pltpu.VMEM((2, NA * RD, LANES), F32),
            flat,
            pltpu.VMEM((LANES, RD * LANES), F32),
            pltpu.VMEM((NR2 * LANES, 2 * LANES), BF),
            pltpu.SemaphoreType.DMA((len(inputs) + 2,)),
        ],
        in_specs=[HBM] * (len(inputs) + 2),
    )
    got = exchange(sent)
    give, rhs, other_rho, raw = call(
        rows_kernel, "rows", (got, fwd),
        (
            square, shape((NQ * RD, 2 * LANES), BF), phases, shape((2, NDEV, LANES), F32),
        ),
        [flat],
    )
    other = other_core(give)
    keep, vis, rho, left, basis = call(
        tables_kernel, "tables", (raw, fwd, rhs),
        (
            square, shape((5 * SLOT, LANES), F32), phases, shape((2, 2 * SUBG, NV), F32),
            shape((2, 2 * SUBG, NV), BF),
        ),
        [pltpu.VMEM((4, 4, SUBG, LANES), F32)],
    )
    corrected, back = call(
        visibility_kernel, "visibilities", (keep, other, vis, left, basis),
        (square, shape((2 * SLOT, LANES), F32)),
        [pltpu.VMEM((2, 2 * SUBG, NV), F32), pltpu.VMEM((2, 2 * SUBG, NV), BF)],
    )
    other = other_core(corrected)
    part, tail = call(
        mine_kernel, "mine", (corrected, back, rho, adj),
        (shape((NQ * RD, 2 * LANES), F32), shape((LANES, LANES), F32)), [],
    )
    (answer,) = call(images_kernel, "images", (part, other, tail, other_rho, adj), (message,), [flat])
    facet_adjoint, residual = call(
        facet_kernel, "facet",
        (exchange(answer), meta, t["coarse_adj"], t["tw_adj"], t["col_adj"]),
        (shape((1, 2, RD, NA * LANES), F32), shape((2, NV), F32)),
        [
            flat,
            pltpu.VMEM((2, 2 * LANES, NR2 * LANES), F32),
            pltpu.VMEM((2, NR2 * LANES, LANES), BF),
            pltpu.VMEM((2, 2, NA * NR2, LANES), F32),
            pltpu.VMEM((2, RD, NA * LANES), F32),
            pltpu.VMEM((2, NV), F32),
            pltpu.SemaphoreType.DMA((9,)),
        ],
        out_specs=(HBM, HBM),
    )
    return (facet_adjoint, residual)


def solution(mesh):
    placed = (
        P("facet", None, "sub", None),
        P("facet", None),
        P(None, ALL),
        P(None, ALL),
        P(ALL, None),
        P(ALL),
    )
    return jax.shard_map(
        on_device,
        mesh=mesh,
        in_specs=placed,
        out_specs=(P("facet", None, "sub", None), P(None, ALL)),
        check_vma=False,
    )
```

```python
import math

import jax
import jax.numpy as jnp
import numpy as np
from jax import lax
from jax.experimental import pallas as pl
from jax.experimental.pallas import tpu as pltpu
from jax.sharding import PartitionSpec as P

N_IMG = 32768
SUBG = 64
HALF = 32
VIS_BLOCK = 32
LANES = 128
NQ = 32
NF = 4
NDEV = 128
RD = 16
NR2 = 8
NA = 64
NV = 1024
SLOT = 16
MSG = 10
A_HIGH = 3 * 5 * SLOT
TWO_PI = 2.0 * math.pi
BF = jnp.bfloat16
F32 = jnp.float32
ALL = ("facet", "sub")


def unit(index, period):
    angle = TWO_PI * (np.asarray(index, np.int64) % period) / period
    return np.cos(angle), np.sin(angle)


def host_tables():
    block = np.arange(NA)
    lane = np.arange(LANES)
    fine = np.arange(SUBG)
    coarse = np.arange(NQ)
    c, s = unit(fine[:, None] * block[None, :], 256)
    c, s = c / 64.0, s / 64.0
    col_fwd = np.block([[c, s], [-s, c]])
    col_adj = np.block([[c.T, -s.T], [s.T, c.T]])
    tw_c, tw_s = unit(fine[:, None] * lane[None, :], N_IMG)
    twiddle_fwd = np.concatenate([tw_c, -tw_s], 0)
    orders = [fine, fine ^ HALF]
    twiddle_adj = np.stack([np.tile(x.T[:, o], (1, 2)) for o in orders for x in (tw_c, tw_s)])
    col_adj = np.concatenate([col_adj[:, np.concatenate([o, o + SUBG])] for o in orders], 0)
    wc, ws = unit(coarse[:, None] * lane[None, :], 32)
    column = np.concatenate([col_fwd, wc, ws, -ws, wc], 0)
    coarse_adj = np.block([[wc.T, ws.T], [-ws.T, wc.T]])
    k_row = (np.arange(8)[:, None] * 4096 + fine[None, :]).reshape(2, 4 * SUBG)
    r = np.arange(NQ * RD).reshape(NQ, 2, NR2).transpose(1, 2, 0).reshape(-1)
    rc, rs = unit(k_row[:, :, None] * r[None, None, :], N_IMG)
    pairs = lambda x: x.reshape(2, 2, 2 * SUBG, NQ * RD) / 64.0
    row_fwd = np.concatenate([pairs(rc), -pairs(rs)], 2)
    row_adj = np.ascontiguousarray(row_fwd.transpose(0, 1, 3, 2))
    bf = lambda x: np.asarray(x, np.float32).astype(jnp.bfloat16)
    return dict(
        column=bf(column),
        col_adj=bf(col_adj),
        tw_fwd=np.asarray(twiddle_fwd, np.float32),
        tw_adj=np.asarray(twiddle_adj, np.float32),
        coarse_adj=bf(coarse_adj),
        row_fwd=bf(row_fwd),
        row_adj=bf(row_adj),
    )


def sincos_turn(turn):
    quarter = jnp.floor(turn * 4.0 + 0.5)
    y = (turn - quarter * 0.25) * TWO_PI
    y2 = y * y
    s = y * (1.0 + y2 * (-1.0 / 6 + y2 * (1.0 / 120 + y2 * (-1.0 / 5040 + y2 * (1.0 / 362880)))))
    c = 1.0 + y2 * (-0.5 + y2 * (1.0 / 24 + y2 * (-1.0 / 720 + y2 * (1.0 / 40320))))
    turns = quarter.astype(jnp.int32)
    odd = (turns & 1) == 1
    cos = jnp.where(odd, s, c)
    sin = jnp.where(odd, c, s)
    cos = jnp.where(((turns + 1) & 2) == 2, -cos, cos)
    sin = jnp.where((turns & 2) == 2, -sin, sin)
    return cos, sin


def phase_of(offset, frequency):
    index = (offset * frequency) & (N_IMG - 1)
    return sincos_turn(index.astype(F32) * (1.0 / N_IMG))


def iota(shape, dim):
    return lax.broadcasted_iota(jnp.int32, shape, dim)


def roll(x, shift):
    return pltpu.roll(x, shift, x.ndim - 1)


def lane_sign(rows, width):
    return jnp.where((iota((rows, LANES), 1) & width) == 0, 1.0, -1.0).astype(F32)


def lower(shape):
    return iota(shape, len(shape) - 1) < SUBG


def split3(x):
    high = x.astype(BF)
    rest = x - high.astype(F32)
    middle = rest.astype(BF)
    low = (rest - middle.astype(F32)).astype(BF)
    return high, middle, low


def send_kernel(
    off_hbm, slab_hbm, pos_hbm, obs_hbm, ids_hbm, ids8_hbm, clip_hbm, table_hbm, tw_hbm, fwd_hbm, adj_hbm,
    msg_ref, meta_ref, fwd_ref, adj_ref, off_ref, slab_ref, pos_ref, obs_ref, ids_ref, ids8_ref, clip_ref, table_ref, tw_ref,
    wide, flat, y_ref, z_ref, sems,
):
    pairs = [
        (ids_hbm, ids_ref), (ids8_hbm, ids8_ref), (clip_hbm, clip_ref), (pos_hbm, pos_ref), (obs_hbm, obs_ref),
        (off_hbm, off_ref), (slab_hbm, slab_ref), (table_hbm, table_ref), (tw_hbm, tw_ref),
    ]
    copies = [pltpu.make_async_copy(a, b, sems.at[i]) for i, (a, b) in enumerate(pairs)]
    four = lax.axis_index("facet") // 2
    later = [
        pltpu.make_async_copy(fwd_hbm.at[four], fwd_ref, sems.at[len(pairs)]),
        pltpu.make_async_copy(adj_hbm.at[four], adj_ref, sems.at[len(pairs) + 1]),
    ]
    for copy in copies + later:
        copy.start()

    copies[0].wait()
    copies[1].wait()
    ids = ids_ref[...]
    n_tile = NV // LANES
    column = ids8_ref[...].astype(F32).T
    row_ids = ids.astype(F32).astype(BF)
    zero, one = jnp.zeros((), BF), jnp.ones((), BF)
    above = iota((LANES, LANES), 0) < iota((LANES, LANES), 1)
    above = jnp.where(above, 1.0, 0.0).astype(BF)
    counts = [None] * n_tile
    for b in range(n_tile):
        mine = jnp.broadcast_to(column[:, b:b + 1], (LANES, LANES)).astype(BF)
        for c in range(b, n_tile):
            other = jnp.broadcast_to(row_ids[:, c * LANES:(c + 1) * LANES], (LANES, LANES))
            same = jnp.where(mine == other, above if b == c else one, zero)
            counts[c] = same if b == 0 else counts[c] + same
    ranks = []
    for c in range(n_tile):
        part = counts[c]
        while part.shape[0] > 16:
            half = part.shape[0] // 2
            part = part[:half] + part[half:]
        ranks.append(jnp.sum(part.astype(F32), 0, keepdims=True))
    rank = jnp.concatenate(ranks, 1).astype(jnp.int32)
    owner = (ids >> 7) * (2 * NQ) + (ids & (NQ - 1)) * 2 + ((ids >> 6) & 1)
    place = ((ids >> 5) & 1) * 8 + rank
    meta_ref[0:1, :] = owner
    meta_ref[1:2, :] = place
    here = iota((SLOT, NV), 0).astype(F32).astype(BF) == place.astype(F32).astype(BF)
    copies[2].wait()
    n_block = NV // VIS_BLOCK
    clip = jnp.broadcast_to(clip_ref[...].astype(F32) * 0.25, (n_block, n_block))
    same = iota((n_block, n_block), 0) == iota((n_block, n_block), 1)
    clip = jnp.sum(jnp.where(same, clip, 0.0), 1, keepdims=True)
    block = iota((n_block, NV), 1) // VIS_BLOCK == iota((n_block, NV), 0)
    level = jnp.sum(jnp.where(block, clip, 0.0), 0, keepdims=True)
    copies[3].wait()
    copies[4].wait()
    values = [pos_ref[0:1, :], pos_ref[1:2, :], obs_ref[0:1, :], obs_ref[1:2, :], level]
    pieces = [split3(v) for v in values]
    own = jnp.where(
        iota((NDEV, NV), 0).astype(F32).astype(BF) == owner.astype(F32).astype(BF), one, zero
    )
    table = jnp.concatenate(
        [
            jnp.where(here, jnp.broadcast_to(p[part], (SLOT, NV)), zero)
            for part in range(3) for p in pieces
        ]
        + [jnp.zeros((SLOT, NV), BF)], 0
    )
    copies[5].wait()
    meta_ref[2:3, :] = jnp.full((1, NV), off_ref[0, 1], jnp.int32)
    payload = lax.dot_general(own, table, (((1,), (1,)), ((), ())), preferred_element_type=F32)
    lane = iota((NDEV, LANES), 1)
    tail = payload[:, LANES:]
    tail = jnp.where(lane == A_HIGH - LANES, (off_ref[0, 0] >> 8).astype(F32), tail)
    tail = jnp.where(lane == A_HIGH + 1 - LANES, (off_ref[0, 0] & 255).astype(F32), tail)
    flat[pl.ds(NR2, NDEV, stride=MSG), :] = payload[:, :LANES]
    flat[pl.ds(NR2 + 1, NDEV, stride=MSG), :] = tail

    lane1 = iota((NQ, LANES), 1)
    freq = iota((NQ, LANES), 0) * (N_IMG // NQ) + (lane1 & (HALF - 1)) + lane1 // SUBG * HALF
    ph_c, ph_s = phase_of(off_ref[0, 1], freq)
    for copy in copies[6:]:
        copy.wait()
    for part in range(2):
        for a in range(NA):
            wide[part, a * RD:(a + 1) * RD, :] = slab_ref[
                0, part, :, a * LANES:(a + 1) * LANES
            ].astype(F32)
    tw_c, tw_s = tw_ref[:SUBG], tw_ref[SUBG:]
    col = table_ref[:LANES]
    coarse = jnp.concatenate(
        [
            jnp.concatenate([table_ref[LANES:LANES + NQ], table_ref[LANES + NQ:LANES + 2 * NQ]], 1),
            jnp.concatenate([table_ref[LANES + 2 * NQ:LANES + 3 * NQ], table_ref[LANES + 3 * NQ:]], 1),
        ], 0
    )
    low = lower((NQ, LANES))
    cols = [
        jnp.concatenate(
            [wide[0, pl.ds(r, NA, stride=RD), :], wide[1, pl.ds(r, NA, stride=RD), :]], 0
        ).astype(BF)
        for r in range(RD)
    ]
    y_ref[...] = jnp.dot(col, jnp.concatenate(cols, 1), preferred_element_type=F32)
    for row in range(NR2):
        both = []
        for r in (row, row + NR2):
            at = slice(r * LANES, (r + 1) * LANES)
            yr, yi = y_ref[:SUBG, at], y_ref[SUBG:, at]
            zr = yr * tw_c - yi * tw_s
            zi = yr * tw_s + yi * tw_c
            both.append(jnp.concatenate([zr, zi], 1).astype(BF))
        for i, (c, h) in enumerate(((0, 0), (0, 1), (1, 0), (1, 1))):
            at = row * LANES + i * HALF
            z_ref[at:at + HALF, :] = both[h][c * HALF:(c + 1) * HALF]
    out = lax.dot_general(
        coarse, z_ref[...], (((1,), (1,)), ((), ())), preferred_element_type=F32
    )
    for row in range(NR2):
        at = slice(row * LANES, (row + 1) * LANES)
        x, y = out[:NQ, at], out[NQ:, at]
        re, im = x * ph_c + y * ph_s, y * ph_c - x * ph_s
        pieces = [jnp.where(low, re, roll(im, SUBG)), jnp.where(low, roll(re, SUBG), im)]
        for c in range(2):
            for g in range(2):
                flat[pl.ds((2 * NQ * g + c) * MSG + row, NQ, stride=2 * MSG), :] = pieces[c]
    msg_ref[...] = flat[...].astype(BF)
    for copy in later:
        copy.wait()


def quarter_low(shape):
    return (iota(shape, len(shape) - 1) & HALF) == 0


def combine(both, rho):
    real, turned = 0.0, 0.0
    for t in range(2):
        rc, rs = rho[t, 0], rho[t, 1]
        a, b = both[:LANES, t * LANES:(t + 1) * LANES], both[LANES:, t * LANES:(t + 1) * LANES]
        real = real + (rc * a + rs * b)
        turned = turned + (rc * b - rs * a)
    real = real + roll(real, HALF)
    turned = turned + roll(turned, HALF)
    return (real - roll(turned, SUBG) * lane_sign(LANES, SUBG)).astype(BF)


def row_phases(tails, pair, rho_ref):
    first = (lax.axis_index("facet") // 2) * 4 + pair * 2
    low = quarter_low((1, LANES))
    start = [(v[:, 0:1] * 256.0 + v[:, 1:2]).astype(jnp.int32) for v in tails]
    starts = [jnp.where(low, start[2 * t], start[2 * t + 1]) for t in range(2)]
    eight = iota((8, LANES), 0)
    turn_c, turn_s = phase_of(
        jnp.where(eight < 4, starts[0], starts[1]), (first + (eight & 1)) * (N_IMG // 8)
    )
    for t in range(2):
        low_c, low_s = phase_of(starts[t], eight)
        high_c, high_s = phase_of(starts[t], eight * 8)
        for p in range(2):
            tc, ts = turn_c[t * 4 + p:t * 4 + p + 1], turn_s[t * 4 + p:t * 4 + p + 1]
            hc, hs = high_c * tc - high_s * ts, high_s * tc + high_c * ts
            for a in range(8):
                at = slice(p * SUBG + a * 8, p * SUBG + a * 8 + 8)
                ac, asin = hc[a:a + 1], hs[a:a + 1]
                rho_ref[t, 0, at, :] = low_c * ac - low_s * asin
                rho_ref[t, 1, at, :] = low_s * ac + low_c * asin


def rows_kernel(got_ref, fwd_ref, give_ref, rhs_ref, rho_ref, raw_ref, flat):
    flat[...] = got_ref[...].astype(F32)
    core = lax.axis_index("sub") & 1
    at = A_HIGH - LANES
    tails = [flat[f * NQ * MSG + NR2 + 1:f * NQ * MSG + NR2 + 2, at:at + 2] for f in range(NF)]
    row_phases(tails, 1 - core, rho_ref)
    low = quarter_low((NQ, LANES))
    for row in range(NR2):
        x = [flat[pl.ds(f * NQ * MSG + row, NQ, stride=MSG), :] for f in range(NF)]
        for t in range(2):
            at = slice(t * LANES, (t + 1) * LANES)
            a, b = x[2 * t], x[2 * t + 1]
            rhs_ref[row * NQ:(row + 1) * NQ, at] = jnp.where(low, a, roll(b, HALF)).astype(BF)
            rhs_ref[(NR2 + row) * NQ:(NR2 + row + 1) * NQ, at] = jnp.where(
                low, roll(a, LANES - HALF), b
            ).astype(BF)
    both = jnp.dot(fwd_ref[1 - core], rhs_ref[...], preferred_element_type=F32)
    give_ref[...] = combine(both, rho_ref)
    raw_ref[0] = flat[pl.ds(NR2, NDEV, stride=MSG), :]
    raw_ref[1] = flat[pl.ds(NR2 + 1, NDEV, stride=MSG), :]


def times(a, b):
    return a[0] * b[0] - a[1] * b[1], a[0] * b[1] + a[1] * b[0]


def tables_kernel(raw_ref, fwd_ref, rhs_ref, keep_ref, vis_ref, rho_ref, left, basis, small):
    core = lax.axis_index("sub") & 1
    at = A_HIGH - LANES
    row_phases([raw_ref[1, f * NQ:f * NQ + 1, at:at + 2] for f in range(NF)], core, rho_ref)
    got = jnp.concatenate([raw_ref[0].T, raw_ref[1].T], 0)
    n = 5 * SLOT
    vis_ref[...] = got[:n] + got[n:2 * n] + got[2 * n:3 * n]
    both = jnp.dot(fwd_ref[core], rhs_ref[...], preferred_element_type=F32)
    keep_ref[...] = combine(both, rho_ref)
    slot = 0
    for l in range(2):
        for which in range(2):
            turn = vis_ref[which * SLOT + l * 8:which * SLOT + l * 8 + 8, :] * (1.0 / SUBG)
            p1 = sincos_turn(turn)
            ones = jnp.ones_like(turn)

            def ladder(p, unit):
                p2 = times(p, p)
                p3 = times(p2, p)
                p4 = times(p2, p2)
                return [unit, p, p2, p3, p4, times(p4, p), times(p3, p3), times(p4, p3)], p4

            low, p4 = ladder(p1, (ones, jnp.zeros_like(turn)))
            high, _ = ladder(times(p4, p4), (ones, jnp.zeros_like(turn)))
            for i in range(8):
                for part in range(2):
                    small[slot, part, i * 8:i * 8 + 8, :] = low[i][part]
                    small[slot, 2 + part, i * 8:i * 8 + 8, :] = high[i][part] * 0.125
            for k in range(8):
                at = slice(k * LANES, (k + 1) * LANES)
                br, bi, ar, ai = [small[slot, part, pl.ds(k, 8, stride=8), :] for part in range(4)]
                re, im = [], []
                for a in range(8):
                    hr, hi = ar[a:a + 1, :], ai[a:a + 1, :]
                    re.append(hr * br - hi * bi)
                    im.append(hr * bi + hi * br)
                if which == 0:
                    left[l, 0:SUBG, at] = jnp.concatenate(re, 0)
                    left[l, SUBG:, at] = jnp.concatenate(im, 0)
                else:
                    basis[l, 0:SUBG, at] = jnp.concatenate(re, 0).astype(BF)
                    basis[l, SUBG:, at] = jnp.concatenate(im, 0).astype(BF)
            slot += 1


def visibility_kernel(keep_ref, other_ref, vis_ref, left, basis, corrected_ref, back_ref, inner, phasor):
    upper_core = (lax.axis_index("sub") & 1) == 1
    keep, other = keep_ref[...].astype(F32), other_ref[...].astype(F32)
    halves = jnp.where(upper_core, other, keep), jnp.where(upper_core, keep, other)
    subgrids = jnp.where(quarter_low((LANES, LANES)), roll(halves[0], LANES - HALF), halves[1])
    sign = lane_sign(SUBG, SUBG)
    for l in range(2):
        sub = subgrids[l * SUBG:(l + 1) * SUBG]
        matrix = jnp.concatenate([sub * sign, roll(sub, SUBG)], 0).astype(BF)
        inner[l] = jnp.dot(matrix, basis[l], preferred_element_type=F32)
    predicted = [[], [], [], []]
    for l in range(2):
        for k in range(8):
            at = slice(k * LANES, (k + 1) * LANES)
            lr, li = left[l, 0:SUBG, at], left[l, SUBG:, at]
            ir, ii = inner[l, 0:SUBG, at], inner[l, SUBG:, at]
            predicted[l].append(jnp.sum(lr * ir - li * ii, 0, keepdims=True))
            predicted[2 + l].append(jnp.sum(lr * ii + li * ir, 0, keepdims=True))
    rows_of = lambda c: vis_ref[c * SLOT:(c + 1) * SLOT, :]
    mis_r = rows_of(2) - jnp.concatenate(predicted[0] + predicted[1], 0)
    mis_i = rows_of(3) - jnp.concatenate(predicted[2] + predicted[3], 0)
    level = rows_of(4)
    live = level > 0.0
    threshold = jnp.where(live, level, 1.0)
    magnitude = jnp.sqrt(mis_r * mis_r + mis_i * mis_i)
    weight = jnp.where(live, threshold / jnp.maximum(magnitude, threshold), 0.0)
    wr, wi = weight * mis_r, weight * mis_i
    for l in range(2):
        for k in range(8):
            at = slice(k * LANES, (k + 1) * LANES)
            lr, li = left[l, 0:SUBG, at], left[l, SUBG:, at]
            vr, vi = wr[l * 8 + k:l * 8 + k + 1, :], wi[l * 8 + k:l * 8 + k + 1, :]
            phasor[l, 0:SUBG, at] = (lr * vr + li * vi).astype(BF)
            phasor[l, SUBG:, at] = (lr * vi - li * vr).astype(BF)
    sums = []
    for l in range(2):
        product = lax.dot_general(
            phasor[l], basis[l], (((1,), (1,)), ((), ())), preferred_element_type=F32
        )
        sums.append(product[:SUBG] * sign + roll(product[SUBG:], SUBG))
    corrected_ref[...] = jnp.concatenate(sums, 0).astype(BF)
    back_ref[...] = jnp.concatenate([wr, wi], 0)


def partial_images(x, pair, rho_ref, adj_ref):
    core = lax.axis_index("sub") & 1
    x = x.astype(F32)
    moved = jnp.where(core == 1, roll(x, LANES - HALF), roll(x, HALF))
    x = jnp.where(quarter_low(x.shape) != (core == 1), x, moved)
    turned = roll(x, SUBG) * -lane_sign(LANES, SUBG)
    cols = []
    for t in range(2):
        rc, rs = rho_ref[t, 0], rho_ref[t, 1]
        cols.append(
            jnp.concatenate([(x * rc + turned * rs).astype(BF), (x * rs - turned * rc).astype(BF)], 0)
        )
    half = NQ * NR2
    table = jnp.concatenate(
        [
            adj_ref[pair, pl.ds(pl.multiple_of(core * half, half), half), :],
            adj_ref[pair, pl.ds(pl.multiple_of((1 - core) * half, half), half), :],
        ], 0
    )
    return jnp.dot(table, jnp.concatenate(cols, 1), preferred_element_type=F32)


def mine_kernel(corrected_ref, back_ref, rho_ref, adj_ref, part_ref, tail_ref):
    back = [part.astype(F32) for part in split3(back_ref[...])]
    tail_ref[...] = jnp.concatenate(back + [jnp.zeros((2 * SLOT, LANES), F32)], 0).T
    part_ref[...] = partial_images(corrected_ref[...], lax.axis_index("sub") & 1, rho_ref, adj_ref)


def images_kernel(part_ref, other_ref, tail_ref, rho_ref, adj_ref, msg_ref, flat):
    pair = 1 - (lax.axis_index("sub") & 1)
    images = part_ref[...] + partial_images(other_ref[...], pair, rho_ref, adj_ref)
    low = quarter_low((NQ, LANES))
    for row in range(NR2):
        for t in range(2):
            at = slice(t * LANES, (t + 1) * LANES)
            a = images[row * NQ:(row + 1) * NQ, at]
            b = images[(NR2 + row) * NQ:(NR2 + row + 1) * NQ, at]
            flat[pl.ds(2 * t * NQ * MSG + row, NQ, stride=MSG), :] = jnp.where(low, a, roll(b, HALF))
            flat[pl.ds((2 * t + 1) * NQ * MSG + row, NQ, stride=MSG), :] = jnp.where(
                low, roll(a, LANES - HALF), b
            )
    flat[pl.ds(NR2, NDEV, stride=MSG), :] = tail_ref[...]
    flat[pl.ds(NR2 + 1, NDEV, stride=MSG), :] = jnp.zeros((NDEV, LANES), F32)
    msg_ref[...] = flat[...].astype(BF)


def facet_kernel(
    got_ref, meta_ref, coarse_ref, tw_ref, col_ref, out_hbm, res_hbm, flat, spread, z_ref, turned, out_ref, res_ref, sems,
):
    flat[...] = got_ref[...].astype(F32)
    copies = []
    sign = -lane_sign(NQ, SUBG)
    low = quarter_low((NQ, LANES))
    for h in range(2):
        lane1 = iota((NQ, LANES), 1)
        freq = iota((NQ, LANES), 0) * (N_IMG // NQ) + ((lane1 & (SUBG - 1)) ^ (h * HALF))
        ph_c, ph_s = phase_of(meta_ref[2:3, :LANES], freq)
        images = []
        for row in range(NR2):
            x = [
                flat[pl.ds(c * MSG + row, NQ, stride=2 * MSG), :]
                + flat[pl.ds((2 * NQ + c) * MSG + row, NQ, stride=2 * MSG), :]
                for c in range(2)
            ]
            image = jnp.where(low, x[h], x[1 - h])
            turn = roll(image, SUBG) * sign
            images.append(
                jnp.concatenate([image * ph_c + turn * ph_s, turn * ph_c - image * ph_s], 0).astype(BF)
            )
        spread[h] = jnp.dot(coarse_ref[...], jnp.concatenate(images, 1), preferred_element_type=F32)
    for h in range(2):
        tw_c, tw_s = tw_ref[2 * h], tw_ref[2 * h + 1]
        for row in range(NR2):
            at = slice(row * LANES, (row + 1) * LANES)
            z_ref[h, at, :] = (tw_c * spread[h, :LANES, at] + tw_s * spread[h, LANES:, at]).astype(BF)
        out = lax.dot_general(
            col_ref[h * LANES:(h + 1) * LANES], z_ref[h], (((1,), (1,)), ((), ())),
            preferred_element_type=F32,
        )
        for part in range(2):
            for row in range(NR2):
                turned[h, part, pl.ds(row, NA, stride=NR2), :] = out[
                    part * NA:(part + 1) * NA, row * LANES:(row + 1) * LANES
                ]
            where = slice(h * NR2, (h + 1) * NR2)
            for piece in range(2):
                for a in range(piece * NA // 2, (piece + 1) * NA // 2):
                    out_ref[part, where, a * LANES:(a + 1) * LANES] = turned[
                        h, part, a * NR2:(a + 1) * NR2, :
                    ]
                wide = slice(piece * NA // 2 * LANES, (piece + 1) * NA // 2 * LANES)
                copy = pltpu.make_async_copy(
                    out_ref.at[part, where, wide], out_hbm.at[0, part, where, wide],
                    sems.at[(h * 2 + part) * 2 + piece],
                )
                copy.start()
                copies.append(copy)
    n = 2 * SLOT
    back = flat[pl.ds(NR2, NDEV, stride=MSG), :].T[:3 * n]
    owner, place = meta_ref[0:1, :], meta_ref[1:2, :]
    own = jnp.where(iota((NDEV, NV), 0) == owner, 1.0, 0.0).astype(BF)
    found = jnp.dot(back.astype(BF), own, preferred_element_type=F32)
    found = found[:n] + found[n:2 * n] + found[2 * n:]
    here = iota((SLOT, NV), 0) == place
    for c in range(2):
        res_ref[c:c + 1, :] = jnp.sum(
            jnp.where(here, found[c * SLOT:(c + 1) * SLOT], 0.0), 0, keepdims=True
        )
    copies.append(pltpu.make_async_copy(res_ref, res_hbm, sems.at[8]))
    copies[-1].start()

    for copy in copies:
        copy.wait()


VMEM = pl.BlockSpec(memory_space=pltpu.VMEM)
HBM = pl.BlockSpec(memory_space=pltpu.MemorySpace.HBM)
TABLES = host_tables()


def in_place(arrays):
    return [pltpu.with_memory_space_constraint(x, pltpu.HBM) for x in arrays]


def exchange(message):
    pairs = message.reshape(NDEV * MSG // 2, 2, LANES)
    return lax.all_to_all(pairs, ALL, split_axis=0, concat_axis=0, tiled=True).reshape(message.shape)


def other_core(x):
    return lax.ppermute(x, "sub", [(i, i ^ 1) for i in range(NQ)])


def on_device(slab, offsets, position, observed, subgrid_of, clip):
    t = {name: jnp.asarray(value) for name, value in TABLES.items()}
    limit = pltpu.CompilerParams(vmem_limit_bytes=32 << 20)
    shape = jax.ShapeDtypeStruct
    message = shape((NDEV * MSG, LANES), BF)
    fwd_table = shape((2, 4 * SUBG, NQ * RD), BF)
    adj_table = shape((2, NQ * RD, 4 * SUBG), BF)
    square = shape((LANES, LANES), BF)
    phases = shape((2, 2, LANES, LANES), F32)
    flat = pltpu.VMEM((NDEV * MSG, LANES), F32)

    def call(kernel, name, inputs, outs, scratch, in_specs=None, out_specs=None, flops=1 << 20):
        return pl.pallas_call(
            kernel,
            out_shape=outs,
            in_specs=in_specs or [VMEM] * len(inputs),
            out_specs=out_specs or (VMEM,) * len(outs),
            scratch_shapes=scratch,
            compiler_params=limit,
            cost_estimate=pl.CostEstimate(flops=flops, bytes_accessed=1 << 21, transcendentals=0),
            name=name,
        )(*inputs)

    inputs = (
        offsets, slab, position, observed, subgrid_of.reshape(1, NV), subgrid_of.reshape(8, LANES),
        clip.reshape(1, NV // VIS_BLOCK), t["column"], t["tw_fwd"],
    )
    sent, meta, fwd, adj = call(
        send_kernel, "send", in_place(inputs + (t["row_fwd"], t["row_adj"])),
        (message, shape((8, NV), jnp.int32), fwd_table, adj_table),
        [pltpu.SMEM((1, 2), jnp.int32)]
        + [pltpu.VMEM(x.shape, x.dtype) for x in inputs[1:]]
        + [
            pltpu.VMEM((2, NA * RD, LANES), F32),
            flat,
            pltpu.VMEM((LANES, RD * LANES), F32),
            pltpu.VMEM((NR2 * LANES, 2 * LANES), BF),
            pltpu.SemaphoreType.DMA((len(inputs) + 2,)),
        ],
        in_specs=[HBM] * (len(inputs) + 2),
    )
    got = exchange(sent)
    give, rhs, other_rho, raw = call(
        rows_kernel, "rows", (got, fwd),
        (
            square, shape((NQ * RD, 2 * LANES), BF), phases, shape((2, NDEV, LANES), F32),
        ),
        [flat],
    )
    other = other_core(give)
    keep, vis, rho, left, basis = call(
        tables_kernel, "tables", (raw, fwd, rhs),
        (
            square, shape((5 * SLOT, LANES), F32), phases, shape((2, 2 * SUBG, NV), F32),
            shape((2, 2 * SUBG, NV), BF),
        ),
        [pltpu.VMEM((4, 4, SUBG, LANES), F32)],
    )
    corrected, back = call(
        visibility_kernel, "visibilities", (keep, other, vis, left, basis),
        (square, shape((2 * SLOT, LANES), F32)),
        [pltpu.VMEM((2, 2 * SUBG, NV), F32), pltpu.VMEM((2, 2 * SUBG, NV), BF)],
    )
    other = other_core(corrected)
    part, tail = call(
        mine_kernel, "mine", (corrected, back, rho, adj),
        (shape((NQ * RD, 2 * LANES), F32), shape((LANES, LANES), F32)), [],
    )
    (answer,) = call(images_kernel, "images", (part, other, tail, other_rho, adj), (message,), [flat])
    facet_adjoint, residual = call(
        facet_kernel, "facet",
        (exchange(answer), meta, t["coarse_adj"], t["tw_adj"], t["col_adj"]),
        (shape((1, 2, RD, NA * LANES), F32), shape((2, NV), F32)),
        [
            flat,
            pltpu.VMEM((2, 2 * LANES, NR2 * LANES), F32),
            pltpu.VMEM((2, NR2 * LANES, LANES), BF),
            pltpu.VMEM((2, 2, NA * NR2, LANES), F32),
            pltpu.VMEM((2, RD, NA * LANES), F32),
            pltpu.VMEM((2, NV), F32),
            pltpu.SemaphoreType.DMA((9,)),
        ],
        out_specs=(HBM, HBM),
    )
    return (facet_adjoint, residual)


def solution(mesh):
    placed = (
        P("facet", None, "sub", None),
        P("facet", None),
        P(None, ALL),
        P(None, ALL),
        P(ALL, None),
        P(ALL),
    )
    return jax.shard_map(
        on_device,
        mesh=mesh,
        in_specs=placed,
        out_specs=(P("facet", None, "sub", None), P(None, ALL)),
        check_vma=False,
    )
```

```python
import math

import jax
import jax.numpy as jnp
import numpy as np
from jax import lax
from jax.experimental import pallas as pl
from jax.experimental.pallas import tpu as pltpu
from jax.sharding import PartitionSpec as P

N_IMG = 32768
SUBG = 64
HALF = 32
VIS_BLOCK = 32
LANES = 128
NQ = 32
NF = 4
NDEV = 128
RD = 16
NR2 = 8
NA = 64
NV = 1024
SLOT = 16
MSG = 10
A_HIGH = 3 * 5 * SLOT
TWO_PI = 2.0 * math.pi
BF = jnp.bfloat16
F32 = jnp.float32
ALL = ("facet", "sub")


def unit(index, period):
    angle = TWO_PI * (np.asarray(index, np.int64) % period) / period
    return np.cos(angle), np.sin(angle)


def host_tables():
    block = np.arange(NA)
    lane = np.arange(LANES)
    fine = np.arange(SUBG)
    coarse = np.arange(NQ)
    c, s = unit(fine[:, None] * block[None, :], 256)
    c, s = c / 64.0, s / 64.0
    col_fwd = np.block([[c, s], [-s, c]])
    col_adj = np.block([[c.T, -s.T], [s.T, c.T]])
    tw_c, tw_s = unit(fine[:, None] * lane[None, :], N_IMG)
    twiddle_fwd = np.concatenate([tw_c, -tw_s], 0)
    orders = [fine, fine ^ HALF]
    twiddle_adj = np.stack([np.tile(x.T[:, o], (1, 2)) for o in orders for x in (tw_c, tw_s)])
    col_adj = np.concatenate([col_adj[:, np.concatenate([o, o + SUBG])] for o in orders], 0)
    wc, ws = unit(coarse[:, None] * lane[None, :], 32)
    column = np.concatenate([col_fwd, wc, ws, -ws, wc], 0)
    coarse_adj = np.block([[wc.T, ws.T], [-ws.T, wc.T]])
    k_row = (np.arange(8)[:, None] * 4096 + fine[None, :]).reshape(2, 4 * SUBG)
    r = np.arange(NQ * RD).reshape(NQ, 2, NR2).transpose(1, 2, 0).reshape(-1)
    rc, rs = unit(k_row[:, :, None] * r[None, None, :], N_IMG)
    pairs = lambda x: x.reshape(2, 2, 2 * SUBG, NQ * RD) / 64.0
    row_fwd = np.concatenate([pairs(rc), -pairs(rs)], 2)
    row_adj = np.ascontiguousarray(row_fwd.transpose(0, 1, 3, 2))
    bf = lambda x: np.asarray(x, np.float32).astype(jnp.bfloat16)
    return dict(
        column=bf(column),
        col_adj=bf(col_adj),
        tw_fwd=np.asarray(twiddle_fwd, np.float32),
        tw_adj=np.asarray(twiddle_adj, np.float32),
        coarse_adj=bf(coarse_adj),
        row_fwd=bf(row_fwd),
        row_adj=bf(row_adj),
    )


def sincos_turn(turn):
    quarter = jnp.floor(turn * 4.0 + 0.5)
    y = (turn - quarter * 0.25) * TWO_PI
    y2 = y * y
    s = y * (1.0 + y2 * (-1.0 / 6 + y2 * (1.0 / 120 + y2 * (-1.0 / 5040 + y2 * (1.0 / 362880)))))
    c = 1.0 + y2 * (-0.5 + y2 * (1.0 / 24 + y2 * (-1.0 / 720 + y2 * (1.0 / 40320))))
    turns = quarter.astype(jnp.int32)
    odd = (turns & 1) == 1
    cos = jnp.where(odd, s, c)
    sin = jnp.where(odd, c, s)
    cos = jnp.where(((turns + 1) & 2) == 2, -cos, cos)
    sin = jnp.where((turns & 2) == 2, -sin, sin)
    return cos, sin


def phase_of(offset, frequency):
    index = (offset * frequency) & (N_IMG - 1)
    return sincos_turn(index.astype(F32) * (1.0 / N_IMG))


def iota(shape, dim):
    return lax.broadcasted_iota(jnp.int32, shape, dim)


def roll(x, shift):
    return pltpu.roll(x, shift, x.ndim - 1)


def lane_sign(rows, width):
    return jnp.where((iota((rows, LANES), 1) & width) == 0, 1.0, -1.0).astype(F32)


def lower(shape):
    return iota(shape, len(shape) - 1) < SUBG


def split3(x):
    high = x.astype(BF)
    rest = x - high.astype(F32)
    middle = rest.astype(BF)
    low = (rest - middle.astype(F32)).astype(BF)
    return high, middle, low


def send_kernel(
    off_hbm, slab_hbm, pos_hbm, obs_hbm, ids_hbm, ids8_hbm, clip_hbm, table_hbm, tw_hbm, fwd_hbm, adj_hbm,
    msg_ref, meta_ref, fwd_ref, adj_ref, off_ref, slab_ref, pos_ref, obs_ref, ids_ref, ids8_ref, clip_ref, table_ref, tw_ref,
    wide, flat, y_ref, z_ref, sems,
):
    pairs = [
        (ids_hbm, ids_ref), (ids8_hbm, ids8_ref), (clip_hbm, clip_ref), (pos_hbm, pos_ref), (obs_hbm, obs_ref),
        (off_hbm, off_ref), (slab_hbm, slab_ref), (table_hbm, table_ref), (tw_hbm, tw_ref),
    ]
    copies = [pltpu.make_async_copy(a, b, sems.at[i]) for i, (a, b) in enumerate(pairs)]
    four = lax.axis_index("facet") // 2
    later = [
        pltpu.make_async_copy(fwd_hbm.at[four], fwd_ref, sems.at[len(pairs)]),
        pltpu.make_async_copy(adj_hbm.at[four], adj_ref, sems.at[len(pairs) + 1]),
    ]
    for copy in copies + later:
        copy.start()

    copies[0].wait()
    copies[1].wait()
    ids = ids_ref[...]
    n_tile = NV // LANES
    column = ids8_ref[...].astype(F32).T
    row_ids = ids.astype(F32).astype(BF)
    zero, one = jnp.zeros((), BF), jnp.ones((), BF)
    above = iota((LANES, LANES), 0) < iota((LANES, LANES), 1)
    above = jnp.where(above, 1.0, 0.0).astype(BF)
    counts = [None] * n_tile
    for b in range(n_tile):
        mine = jnp.broadcast_to(column[:, b:b + 1], (LANES, LANES)).astype(BF)
        for c in range(b, n_tile):
            other = jnp.broadcast_to(row_ids[:, c * LANES:(c + 1) * LANES], (LANES, LANES))
            same = jnp.where(mine == other, above if b == c else one, zero)
            counts[c] = same if b == 0 else counts[c] + same
    ranks = []
    for c in range(n_tile):
        part = counts[c]
        while part.shape[0] > 16:
            half = part.shape[0] // 2
            part = part[:half] + part[half:]
        ranks.append(jnp.sum(part.astype(F32), 0, keepdims=True))
    rank = jnp.concatenate(ranks, 1).astype(jnp.int32)
    owner = (ids >> 7) * (2 * NQ) + (ids & (NQ - 1)) * 2 + ((ids >> 6) & 1)
    place = ((ids >> 5) & 1) * 8 + rank
    meta_ref[0:1, :] = owner
    meta_ref[1:2, :] = place
    here = iota((SLOT, NV), 0).astype(F32).astype(BF) == place.astype(F32).astype(BF)
    copies[2].wait()
    n_block = NV // VIS_BLOCK
    clip = jnp.broadcast_to(clip_ref[...].astype(F32) * 0.25, (n_block, n_block))
    same = iota((n_block, n_block), 0) == iota((n_block, n_block), 1)
    clip = jnp.sum(jnp.where(same, clip, 0.0), 1, keepdims=True)
    block = iota((n_block, NV), 1) // VIS_BLOCK == iota((n_block, NV), 0)
    level = jnp.sum(jnp.where(block, clip, 0.0), 0, keepdims=True)
    copies[3].wait()
    copies[4].wait()
    values = [pos_ref[0:1, :], pos_ref[1:2, :], obs_ref[0:1, :], obs_ref[1:2, :], level]
    pieces = [split3(v) for v in values]
    own = jnp.where(
        iota((NDEV, NV), 0).astype(F32).astype(BF) == owner.astype(F32).astype(BF), one, zero
    )
    table = jnp.concatenate(
        [
            jnp.where(here, jnp.broadcast_to(p[part], (SLOT, NV)), zero)
            for part in range(3) for p in pieces
        ]
        + [jnp.zeros((SLOT, NV), BF)], 0
    )
    copies[5].wait()
    meta_ref[2:3, :] = jnp.full((1, NV), off_ref[0, 1], jnp.int32)
    payload = lax.dot_general(own, table, (((1,), (1,)), ((), ())), preferred_element_type=F32)
    lane = iota((NDEV, LANES), 1)
    tail = payload[:, LANES:]
    tail = jnp.where(lane == A_HIGH - LANES, (off_ref[0, 0] >> 8).astype(F32), tail)
    tail = jnp.where(lane == A_HIGH + 1 - LANES, (off_ref[0, 0] & 255).astype(F32), tail)
    flat[pl.ds(NR2, NDEV, stride=MSG), :] = payload[:, :LANES]
    flat[pl.ds(NR2 + 1, NDEV, stride=MSG), :] = tail

    lane1 = iota((NQ, LANES), 1)
    freq = iota((NQ, LANES), 0) * (N_IMG // NQ) + (lane1 & (HALF - 1)) + lane1 // SUBG * HALF
    ph_c, ph_s = phase_of(off_ref[0, 1], freq)
    for copy in copies[6:]:
        copy.wait()
    for part in range(2):
        for a in range(NA):
            wide[part, a * RD:(a + 1) * RD, :] = slab_ref[
                0, part, :, a * LANES:(a + 1) * LANES
            ].astype(F32)
    tw_c, tw_s = tw_ref[:SUBG], tw_ref[SUBG:]
    col = table_ref[:LANES]
    coarse = jnp.concatenate(
        [
            jnp.concatenate([table_ref[LANES:LANES + NQ], table_ref[LANES + NQ:LANES + 2 * NQ]], 1),
            jnp.concatenate([table_ref[LANES + 2 * NQ:LANES + 3 * NQ], table_ref[LANES + 3 * NQ:]], 1),
        ], 0
    )
    low = lower((NQ, LANES))
    cols = [
        jnp.concatenate(
            [wide[0, pl.ds(r, NA, stride=RD), :], wide[1, pl.ds(r, NA, stride=RD), :]], 0
        ).astype(BF)
        for r in range(RD)
    ]
    y_ref[...] = jnp.dot(col, jnp.concatenate(cols, 1), preferred_element_type=F32)
    for row in range(NR2):
        both = []
        for r in (row, row + NR2):
            at = slice(r * LANES, (r + 1) * LANES)
            yr, yi = y_ref[:SUBG, at], y_ref[SUBG:, at]
            zr = yr * tw_c - yi * tw_s
            zi = yr * tw_s + yi * tw_c
            both.append(jnp.concatenate([zr, zi], 1).astype(BF))
        for i, (c, h) in enumerate(((0, 0), (0, 1), (1, 0), (1, 1))):
            at = row * LANES + i * HALF
            z_ref[at:at + HALF, :] = both[h][c * HALF:(c + 1) * HALF]
    out = lax.dot_general(
        coarse, z_ref[...], (((1,), (1,)), ((), ())), preferred_element_type=F32
    )
    for row in range(NR2):
        at = slice(row * LANES, (row + 1) * LANES)
        x, y = out[:NQ, at], out[NQ:, at]
        re, im = x * ph_c + y * ph_s, y * ph_c - x * ph_s
        pieces = [jnp.where(low, re, roll(im, SUBG)), jnp.where(low, roll(re, SUBG), im)]
        for c in range(2):
            for g in range(2):
                flat[pl.ds((2 * NQ * g + c) * MSG + row, NQ, stride=2 * MSG), :] = pieces[c]
    msg_ref[...] = flat[...].astype(BF)
    for copy in later:
        copy.wait()


def quarter_low(shape):
    return (iota(shape, len(shape) - 1) & HALF) == 0


def combine(both, rho):
    real, turned = 0.0, 0.0
    for t in range(2):
        rc, rs = rho[t, 0], rho[t, 1]
        a, b = both[:LANES, t * LANES:(t + 1) * LANES], both[LANES:, t * LANES:(t + 1) * LANES]
        real = real + (rc * a + rs * b)
        turned = turned + (rc * b - rs * a)
    real = real + roll(real, HALF)
    turned = turned + roll(turned, HALF)
    return (real - roll(turned, SUBG) * lane_sign(LANES, SUBG)).astype(BF)


def row_phases(tails, pair, rho_ref):
    first = (lax.axis_index("facet") // 2) * 4 + pair * 2
    low = quarter_low((1, LANES))
    start = [(v[:, 0:1] * 256.0 + v[:, 1:2]).astype(jnp.int32) for v in tails]
    starts = [jnp.where(low, start[2 * t], start[2 * t + 1]) for t in range(2)]
    eight = iota((8, LANES), 0)
    turn_c, turn_s = phase_of(
        jnp.where(eight < 4, starts[0], starts[1]), (first + (eight & 1)) * (N_IMG // 8)
    )
    for t in range(2):
        low_c, low_s = phase_of(starts[t], eight)
        high_c, high_s = phase_of(starts[t], eight * 8)
        for p in range(2):
            tc, ts = turn_c[t * 4 + p:t * 4 + p + 1], turn_s[t * 4 + p:t * 4 + p + 1]
            hc, hs = high_c * tc - high_s * ts, high_s * tc + high_c * ts
            for a in range(8):
                at = slice(p * SUBG + a * 8, p * SUBG + a * 8 + 8)
                ac, asin = hc[a:a + 1], hs[a:a + 1]
                rho_ref[t, 0, at, :] = low_c * ac - low_s * asin
                rho_ref[t, 1, at, :] = low_s * ac + low_c * asin


def rows_kernel(got_ref, fwd_ref, give_ref, rhs_ref, rho_ref, raw_ref, flat):
    flat[...] = got_ref[...].astype(F32)
    core = lax.axis_index("sub") & 1
    at = A_HIGH - LANES
    tails = [flat[f * NQ * MSG + NR2 + 1:f * NQ * MSG + NR2 + 2, at:at + 2] for f in range(NF)]
    row_phases(tails, 1 - core, rho_ref)
    low = quarter_low((NQ, LANES))
    for row in range(NR2):
        x = [flat[pl.ds(f * NQ * MSG + row, NQ, stride=MSG), :] for f in range(NF)]
        for t in range(2):
            at = slice(t * LANES, (t + 1) * LANES)
            a, b = x[2 * t], x[2 * t + 1]
            rhs_ref[row * NQ:(row + 1) * NQ, at] = jnp.where(low, a, roll(b, HALF)).astype(BF)
            rhs_ref[(NR2 + row) * NQ:(NR2 + row + 1) * NQ, at] = jnp.where(
                low, roll(a, LANES - HALF), b
            ).astype(BF)
    both = jnp.dot(fwd_ref[1 - core], rhs_ref[...], preferred_element_type=F32)
    give_ref[...] = combine(both, rho_ref)
    raw_ref[0] = flat[pl.ds(NR2, NDEV, stride=MSG), :]
    raw_ref[1] = flat[pl.ds(NR2 + 1, NDEV, stride=MSG), :]


def times(a, b):
    return a[0] * b[0] - a[1] * b[1], a[0] * b[1] + a[1] * b[0]


def tables_kernel(raw_ref, fwd_ref, rhs_ref, keep_ref, vis_ref, rho_ref, left, basis, small):
    core = lax.axis_index("sub") & 1
    at = A_HIGH - LANES
    row_phases([raw_ref[1, f * NQ:f * NQ + 1, at:at + 2] for f in range(NF)], core, rho_ref)
    got = jnp.concatenate([raw_ref[0].T, raw_ref[1].T], 0)
    n = 5 * SLOT
    vis_ref[...] = got[:n] + got[n:2 * n] + got[2 * n:3 * n]
    both = jnp.dot(fwd_ref[core], rhs_ref[...], preferred_element_type=F32)
    keep_ref[...] = combine(both, rho_ref)
    slot = 0
    for l in range(2):
        for which in range(2):
            turn = vis_ref[which * SLOT + l * 8:which * SLOT + l * 8 + 8, :] * (1.0 / SUBG)
            p1 = sincos_turn(turn)
            ones = jnp.ones_like(turn)

            def ladder(p, unit):
                p2 = times(p, p)
                p3 = times(p2, p)
                p4 = times(p2, p2)
                return [unit, p, p2, p3, p4, times(p4, p), times(p3, p3), times(p4, p3)], p4

            low, p4 = ladder(p1, (ones, jnp.zeros_like(turn)))
            high, _ = ladder(times(p4, p4), (ones, jnp.zeros_like(turn)))
            for i in range(8):
                for part in range(2):
                    small[slot, part, i * 8:i * 8 + 8, :] = low[i][part]
                    small[slot, 2 + part, i * 8:i * 8 + 8, :] = high[i][part] * 0.125
            for k in range(8):
                at = slice(k * LANES, (k + 1) * LANES)
                br, bi, ar, ai = [small[slot, part, pl.ds(k, 8, stride=8), :] for part in range(4)]
                re, im = [], []
                for a in range(8):
                    hr, hi = ar[a:a + 1, :], ai[a:a + 1, :]
                    re.append(hr * br - hi * bi)
                    im.append(hr * bi + hi * br)
                if which == 0:
                    left[l, 0:SUBG, at] = jnp.concatenate(re, 0)
                    left[l, SUBG:, at] = jnp.concatenate(im, 0)
                else:
                    basis[l, 0:SUBG, at] = jnp.concatenate(re, 0).astype(BF)
                    basis[l, SUBG:, at] = jnp.concatenate(im, 0).astype(BF)
            slot += 1


def visibility_kernel(keep_ref, other_ref, vis_ref, left, basis, corrected_ref, back_ref, inner, phasor):
    upper_core = (lax.axis_index("sub") & 1) == 1
    keep, other = keep_ref[...].astype(F32), other_ref[...].astype(F32)
    halves = jnp.where(upper_core, other, keep), jnp.where(upper_core, keep, other)
    subgrids = jnp.where(quarter_low((LANES, LANES)), roll(halves[0], LANES - HALF), halves[1])
    sign = lane_sign(SUBG, SUBG)
    for l in range(2):
        sub = subgrids[l * SUBG:(l + 1) * SUBG]
        matrix = jnp.concatenate([sub * sign, roll(sub, SUBG)], 0).astype(BF)
        inner[l] = jnp.dot(matrix, basis[l], preferred_element_type=F32)
    predicted = [[], [], [], []]
    for l in range(2):
        for k in range(8):
            at = slice(k * LANES, (k + 1) * LANES)
            lr, li = left[l, 0:SUBG, at], left[l, SUBG:, at]
            ir, ii = inner[l, 0:SUBG, at], inner[l, SUBG:, at]
            predicted[l].append(jnp.sum(lr * ir - li * ii, 0, keepdims=True))
            predicted[2 + l].append(jnp.sum(lr * ii + li * ir, 0, keepdims=True))
    rows_of = lambda c: vis_ref[c * SLOT:(c + 1) * SLOT, :]
    mis_r = rows_of(2) - jnp.concatenate(predicted[0] + predicted[1], 0)
    mis_i = rows_of(3) - jnp.concatenate(predicted[2] + predicted[3], 0)
    level = rows_of(4)
    live = level > 0.0
    threshold = jnp.where(live, level, 1.0)
    magnitude = jnp.sqrt(mis_r * mis_r + mis_i * mis_i)
    weight = jnp.where(live, threshold / jnp.maximum(magnitude, threshold), 0.0)
    wr, wi = weight * mis_r, weight * mis_i
    for l in range(2):
        for k in range(8):
            at = slice(k * LANES, (k + 1) * LANES)
            lr, li = left[l, 0:SUBG, at], left[l, SUBG:, at]
            vr, vi = wr[l * 8 + k:l * 8 + k + 1, :], wi[l * 8 + k:l * 8 + k + 1, :]
            phasor[l, 0:SUBG, at] = (lr * vr + li * vi).astype(BF)
            phasor[l, SUBG:, at] = (lr * vi - li * vr).astype(BF)
    sums = []
    for l in range(2):
        product = lax.dot_general(
            phasor[l], basis[l], (((1,), (1,)), ((), ())), preferred_element_type=F32
        )
        sums.append(product[:SUBG] * sign + roll(product[SUBG:], SUBG))
    corrected_ref[...] = jnp.concatenate(sums, 0).astype(BF)
    back_ref[...] = jnp.concatenate([wr, wi], 0)


def partial_images(x, pair, rho_ref, adj_ref):
    core = lax.axis_index("sub") & 1
    x = x.astype(F32)
    moved = jnp.where(core == 1, roll(x, LANES - HALF), roll(x, HALF))
    x = jnp.where(quarter_low(x.shape) != (core == 1), x, moved)
    turned = roll(x, SUBG) * -lane_sign(LANES, SUBG)
    cols = []
    for t in range(2):
        rc, rs = rho_ref[t, 0], rho_ref[t, 1]
        cols.append(
            jnp.concatenate([(x * rc + turned * rs).astype(BF), (x * rs - turned * rc).astype(BF)], 0)
        )
    half = NQ * NR2
    table = jnp.concatenate(
        [
            adj_ref[pair, pl.ds(pl.multiple_of(core * half, half), half), :],
            adj_ref[pair, pl.ds(pl.multiple_of((1 - core) * half, half), half), :],
        ], 0
    )
    return jnp.dot(table, jnp.concatenate(cols, 1), preferred_element_type=F32)


def mine_kernel(corrected_ref, back_ref, rho_ref, adj_ref, part_ref, tail_ref):
    back = [part.astype(F32) for part in split3(back_ref[...])]
    tail_ref[...] = jnp.concatenate(back + [jnp.zeros((2 * SLOT, LANES), F32)], 0).T
    part_ref[...] = partial_images(corrected_ref[...], lax.axis_index("sub") & 1, rho_ref, adj_ref)


def images_kernel(part_ref, other_ref, tail_ref, rho_ref, adj_ref, msg_ref, flat):
    pair = 1 - (lax.axis_index("sub") & 1)
    images = part_ref[...] + partial_images(other_ref[...], pair, rho_ref, adj_ref)
    low = quarter_low((NQ, LANES))
    for row in range(NR2):
        for t in range(2):
            at = slice(t * LANES, (t + 1) * LANES)
            a = images[row * NQ:(row + 1) * NQ, at]
            b = images[(NR2 + row) * NQ:(NR2 + row + 1) * NQ, at]
            flat[pl.ds(2 * t * NQ * MSG + row, NQ, stride=MSG), :] = jnp.where(low, a, roll(b, HALF))
            flat[pl.ds((2 * t + 1) * NQ * MSG + row, NQ, stride=MSG), :] = jnp.where(
                low, roll(a, LANES - HALF), b
            )
    flat[pl.ds(NR2, NDEV, stride=MSG), :] = tail_ref[...]
    flat[pl.ds(NR2 + 1, NDEV, stride=MSG), :] = jnp.zeros((NDEV, LANES), F32)
    msg_ref[...] = flat[...].astype(BF)


def facet_kernel(
    got_ref, meta_ref, coarse_ref, tw_ref, col_ref, out_hbm, res_hbm, flat, spread, z_ref, turned, out_ref, res_ref, sems,
):
    flat[...] = got_ref[...].astype(F32)
    copies = []
    sign = -lane_sign(NQ, SUBG)
    low = quarter_low((NQ, LANES))
    for h in range(2):
        lane1 = iota((NQ, LANES), 1)
        freq = iota((NQ, LANES), 0) * (N_IMG // NQ) + ((lane1 & (SUBG - 1)) ^ (h * HALF))
        ph_c, ph_s = phase_of(meta_ref[2:3, :LANES], freq)
        images = []
        for row in range(NR2):
            x = [
                flat[pl.ds(c * MSG + row, NQ, stride=2 * MSG), :]
                + flat[pl.ds((2 * NQ + c) * MSG + row, NQ, stride=2 * MSG), :]
                for c in range(2)
            ]
            image = jnp.where(low, x[h], x[1 - h])
            turn = roll(image, SUBG) * sign
            images.append(
                jnp.concatenate([image * ph_c + turn * ph_s, turn * ph_c - image * ph_s], 0).astype(BF)
            )
        spread[h] = jnp.dot(coarse_ref[...], jnp.concatenate(images, 1), preferred_element_type=F32)
    for h in range(2):
        tw_c, tw_s = tw_ref[2 * h], tw_ref[2 * h + 1]
        for row in range(NR2):
            at = slice(row * LANES, (row + 1) * LANES)
            z_ref[h, at, :] = (tw_c * spread[h, :LANES, at] + tw_s * spread[h, LANES:, at]).astype(BF)
        out = lax.dot_general(
            col_ref[h * LANES:(h + 1) * LANES], z_ref[h], (((1,), (1,)), ((), ())),
            preferred_element_type=F32,
        )
        for part in range(2):
            for row in range(NR2):
                turned[h, part, pl.ds(row, NA, stride=NR2), :] = out[
                    part * NA:(part + 1) * NA, row * LANES:(row + 1) * LANES
                ]
            where = slice(h * NR2, (h + 1) * NR2)
            for piece in range(2):
                for a in range(piece * NA // 2, (piece + 1) * NA // 2):
                    out_ref[part, where, a * LANES:(a + 1) * LANES] = turned[
                        h, part, a * NR2:(a + 1) * NR2, :
                    ]
                wide = slice(piece * NA // 2 * LANES, (piece + 1) * NA // 2 * LANES)
                copy = pltpu.make_async_copy(
                    out_ref.at[part, where, wide], out_hbm.at[0, part, where, wide],
                    sems.at[(h * 2 + part) * 2 + piece],
                )
                copy.start()
                copies.append(copy)
    n = 2 * SLOT
    back = flat[pl.ds(NR2, NDEV, stride=MSG), :].T[:3 * n]
    owner, place = meta_ref[0:1, :], meta_ref[1:2, :]
    one, zero = jnp.ones((), BF), jnp.zeros((), BF)
    own = jnp.where(
        iota((NDEV, NV), 0).astype(F32).astype(BF) == owner.astype(F32).astype(BF), one, zero
    )
    found = jnp.dot(back.astype(BF), own, preferred_element_type=F32)
    found = found[:n] + found[n:2 * n] + found[2 * n:]
    here = iota((SLOT, NV), 0) == place
    for c in range(2):
        res_ref[c:c + 1, :] = jnp.sum(
            jnp.where(here, found[c * SLOT:(c + 1) * SLOT], 0.0), 0, keepdims=True
        )
    copies.append(pltpu.make_async_copy(res_ref, res_hbm, sems.at[8]))
    copies[-1].start()

    for copy in copies:
        copy.wait()


VMEM = pl.BlockSpec(memory_space=pltpu.VMEM)
HBM = pl.BlockSpec(memory_space=pltpu.MemorySpace.HBM)
TABLES = host_tables()


def in_place(arrays):
    return [pltpu.with_memory_space_constraint(x, pltpu.HBM) for x in arrays]


def exchange(message):
    pairs = message.reshape(NDEV * MSG // 2, 2, LANES)
    return lax.all_to_all(pairs, ALL, split_axis=0, concat_axis=0, tiled=True).reshape(message.shape)


def other_core(x):
    return lax.ppermute(x, "sub", [(i, i ^ 1) for i in range(NQ)])


def on_device(slab, offsets, position, observed, subgrid_of, clip):
    t = {name: jnp.asarray(value) for name, value in TABLES.items()}
    limit = pltpu.CompilerParams(vmem_limit_bytes=20 << 20)
    shape = jax.ShapeDtypeStruct
    message = shape((NDEV * MSG, LANES), BF)
    fwd_table = shape((2, 4 * SUBG, NQ * RD), BF)
    adj_table = shape((2, NQ * RD, 4 * SUBG), BF)
    square = shape((LANES, LANES), BF)
    phases = shape((2, 2, LANES, LANES), F32)
    flat = pltpu.VMEM((NDEV * MSG, LANES), F32)

    def call(kernel, name, inputs, outs, scratch, in_specs=None, out_specs=None, flops=1 << 20):
        return pl.pallas_call(
            kernel,
            out_shape=outs,
            in_specs=in_specs or [VMEM] * len(inputs),
            out_specs=out_specs or (VMEM,) * len(outs),
            scratch_shapes=scratch,
            compiler_params=limit,
            cost_estimate=pl.CostEstimate(flops=flops, bytes_accessed=1 << 21, transcendentals=0),
            name=name,
        )(*inputs)

    inputs = (
        offsets, slab, position, observed, subgrid_of.reshape(1, NV), subgrid_of.reshape(8, LANES),
        clip.reshape(1, NV // VIS_BLOCK), t["column"], t["tw_fwd"],
    )
    sent, meta, fwd, adj = call(
        send_kernel, "send", in_place(inputs + (t["row_fwd"], t["row_adj"])),
        (message, shape((8, NV), jnp.int32), fwd_table, adj_table),
        [pltpu.SMEM((1, 2), jnp.int32)]
        + [pltpu.VMEM(x.shape, x.dtype) for x in inputs[1:]]
        + [
            pltpu.VMEM((2, NA * RD, LANES), F32),
            flat,
            pltpu.VMEM((LANES, RD * LANES), F32),
            pltpu.VMEM((NR2 * LANES, 2 * LANES), BF),
            pltpu.SemaphoreType.DMA((len(inputs) + 2,)),
        ],
        in_specs=[HBM] * (len(inputs) + 2),
    )
    got = exchange(sent)
    give, rhs, other_rho, raw = call(
        rows_kernel, "rows", (got, fwd),
        (
            square, shape((NQ * RD, 2 * LANES), BF), phases, shape((2, NDEV, LANES), F32),
        ),
        [flat],
    )
    other = other_core(give)
    keep, vis, rho, left, basis = call(
        tables_kernel, "tables", (raw, fwd, rhs),
        (
            square, shape((5 * SLOT, LANES), F32), phases, shape((2, 2 * SUBG, NV), F32),
            shape((2, 2 * SUBG, NV), BF),
        ),
        [pltpu.VMEM((4, 4, SUBG, LANES), F32)],
    )
    corrected, back = call(
        visibility_kernel, "visibilities", (keep, other, vis, left, basis),
        (square, shape((2 * SLOT, LANES), F32)),
        [pltpu.VMEM((2, 2 * SUBG, NV), F32), pltpu.VMEM((2, 2 * SUBG, NV), BF)],
    )
    other = other_core(corrected)
    part, tail = call(
        mine_kernel, "mine", (corrected, back, rho, adj),
        (shape((NQ * RD, 2 * LANES), F32), shape((LANES, LANES), F32)), [],
    )
    (answer,) = call(images_kernel, "images", (part, other, tail, other_rho, adj), (message,), [flat])
    facet_adjoint, residual = call(
        facet_kernel, "facet",
        (exchange(answer), meta, t["coarse_adj"], t["tw_adj"], t["col_adj"]),
        (shape((1, 2, RD, NA * LANES), F32), shape((2, NV), F32)),
        [
            flat,
            pltpu.VMEM((2, 2 * LANES, NR2 * LANES), F32),
            pltpu.VMEM((2, NR2 * LANES, LANES), BF),
            pltpu.VMEM((2, 2, NA * NR2, LANES), F32),
            pltpu.VMEM((2, RD, NA * LANES), F32),
            pltpu.VMEM((2, NV), F32),
            pltpu.SemaphoreType.DMA((9,)),
        ],
        out_specs=(HBM, HBM),
    )
    return (facet_adjoint, residual)


def solution(mesh):
    placed = (
        P("facet", None, "sub", None),
        P("facet", None),
        P(None, ALL),
        P(None, ALL),
        P(ALL, None),
        P(ALL),
    )
    return jax.shard_map(
        on_device,
        mesh=mesh,
        in_specs=placed,
        out_specs=(P("facet", None, "sub", None), P(None, ALL)),
        check_vma=False,
    )
```

```python
import math

import jax
import jax.numpy as jnp
import numpy as np
from jax import lax
from jax.experimental import pallas as pl
from jax.experimental.pallas import tpu as pltpu
from jax.sharding import PartitionSpec as P

N_IMG = 32768
SUBG = 64
HALF = 32
VIS_BLOCK = 32
LANES = 128
NQ = 32
NF = 4
NDEV = 128
RD = 16
NR2 = 8
NA = 64
NV = 1024
SLOT = 16
MSG = 10
A_HIGH = 3 * 5 * SLOT
TWO_PI = 2.0 * math.pi
BF = jnp.bfloat16
F32 = jnp.float32
ALL = ("facet", "sub")


def unit(index, period):
    angle = TWO_PI * (np.asarray(index, np.int64) % period) / period
    return np.cos(angle), np.sin(angle)


def host_tables():
    block = np.arange(NA)
    lane = np.arange(LANES)
    fine = np.arange(SUBG)
    coarse = np.arange(NQ)
    c, s = unit(fine[:, None] * block[None, :], 256)
    c, s = c / 64.0, s / 64.0
    col_fwd = np.block([[c, s], [-s, c]])
    col_adj = np.block([[c.T, -s.T], [s.T, c.T]])
    tw_c, tw_s = unit(fine[:, None] * lane[None, :], N_IMG)
    twiddle_fwd = np.concatenate([tw_c, -tw_s], 0)
    orders = [fine, fine ^ HALF]
    twiddle_adj = np.stack([np.tile(x.T[:, o], (1, 2)) for o in orders for x in (tw_c, tw_s)])
    col_adj = np.concatenate([col_adj[:, np.concatenate([o, o + SUBG])] for o in orders], 0)
    wc, ws = unit(coarse[:, None] * lane[None, :], 32)
    column = np.concatenate([col_fwd, wc, ws, -ws, wc], 0)
    coarse_adj = np.block([[wc.T, ws.T], [-ws.T, wc.T]])
    k_row = (np.arange(8)[:, None] * 4096 + fine[None, :]).reshape(2, 4 * SUBG)
    r = np.arange(NQ * RD).reshape(NQ, 2, NR2).transpose(1, 2, 0).reshape(-1)
    rc, rs = unit(k_row[:, :, None] * r[None, None, :], N_IMG)
    pairs = lambda x: x.reshape(2, 2, 2 * SUBG, NQ * RD) / 64.0
    row_fwd = np.concatenate([pairs(rc), -pairs(rs)], 2)
    row_adj = np.ascontiguousarray(row_fwd.transpose(0, 1, 3, 2))
    bf = lambda x: np.asarray(x, np.float32).astype(jnp.bfloat16)
    return dict(
        column=bf(column),
        col_adj=bf(col_adj),
        tw_fwd=np.asarray(twiddle_fwd, np.float32),
        tw_adj=np.asarray(twiddle_adj, np.float32),
        coarse_adj=bf(coarse_adj),
        row_fwd=bf(row_fwd),
        row_adj=bf(row_adj),
    )


def sincos_turn(turn):
    quarter = jnp.floor(turn * 4.0 + 0.5)
    y = (turn - quarter * 0.25) * TWO_PI
    y2 = y * y
    s = y * (1.0 + y2 * (-1.0 / 6 + y2 * (1.0 / 120 + y2 * (-1.0 / 5040 + y2 * (1.0 / 362880)))))
    c = 1.0 + y2 * (-0.5 + y2 * (1.0 / 24 + y2 * (-1.0 / 720 + y2 * (1.0 / 40320))))
    turns = quarter.astype(jnp.int32)
    odd = (turns & 1) == 1
    cos = jnp.where(odd, s, c)
    sin = jnp.where(odd, c, s)
    cos = jnp.where(((turns + 1) & 2) == 2, -cos, cos)
    sin = jnp.where((turns & 2) == 2, -sin, sin)
    return cos, sin


def phase_of(offset, frequency):
    index = (offset * frequency) & (N_IMG - 1)
    return sincos_turn(index.astype(F32) * (1.0 / N_IMG))


def iota(shape, dim):
    return lax.broadcasted_iota(jnp.int32, shape, dim)


def roll(x, shift):
    return pltpu.roll(x, shift, x.ndim - 1)


def lane_sign(rows, width):
    return jnp.where((iota((rows, LANES), 1) & width) == 0, 1.0, -1.0).astype(F32)


def lower(shape):
    return iota(shape, len(shape) - 1) < SUBG


def split3(x):
    high = x.astype(BF)
    rest = x - high.astype(F32)
    middle = rest.astype(BF)
    low = (rest - middle.astype(F32)).astype(BF)
    return high, middle, low


def send_kernel(
    off_hbm, slab_hbm, pos_hbm, obs_hbm, ids_hbm, ids8_hbm, clip_hbm, table_hbm, tw_hbm, fwd_hbm,
    msg_ref, meta_ref, fwd_ref, off_ref, slab_ref, pos_ref, obs_ref, ids_ref, ids8_ref, clip_ref, table_ref, tw_ref,
    wide, flat, y_ref, z_ref, sems,
):
    pairs = [
        (ids_hbm, ids_ref), (ids8_hbm, ids8_ref), (clip_hbm, clip_ref), (pos_hbm, pos_ref), (obs_hbm, obs_ref),
        (off_hbm, off_ref), (slab_hbm, slab_ref), (table_hbm, table_ref), (tw_hbm, tw_ref),
    ]
    copies = [pltpu.make_async_copy(a, b, sems.at[i]) for i, (a, b) in enumerate(pairs)]
    four = lax.axis_index("facet") // 2
    later = [
        pltpu.make_async_copy(fwd_hbm.at[four], fwd_ref, sems.at[len(pairs)]),
    ]
    for copy in copies + later:
        copy.start()

    copies[0].wait()
    copies[1].wait()
    ids = ids_ref[...]
    n_tile = NV // LANES
    column = ids8_ref[...].astype(F32).T
    row_ids = ids.astype(F32).astype(BF)
    zero, one = jnp.zeros((), BF), jnp.ones((), BF)
    above = iota((LANES, LANES), 0) < iota((LANES, LANES), 1)
    above = jnp.where(above, 1.0, 0.0).astype(BF)
    counts = [None] * n_tile
    for b in range(n_tile):
        mine = jnp.broadcast_to(column[:, b:b + 1], (LANES, LANES)).astype(BF)
        for c in range(b, n_tile):
            other = jnp.broadcast_to(row_ids[:, c * LANES:(c + 1) * LANES], (LANES, LANES))
            same = jnp.where(mine == other, above if b == c else one, zero)
            counts[c] = same if b == 0 else counts[c] + same
    ranks = []
    for c in range(n_tile):
        part = counts[c]
        while part.shape[0] > 16:
            half = part.shape[0] // 2
            part = part[:half] + part[half:]
        ranks.append(jnp.sum(part.astype(F32), 0, keepdims=True))
    rank = jnp.concatenate(ranks, 1).astype(jnp.int32)
    owner = (ids >> 7) * (2 * NQ) + (ids & (NQ - 1)) * 2 + ((ids >> 6) & 1)
    place = ((ids >> 5) & 1) * 8 + rank
    meta_ref[0:1, :] = owner
    meta_ref[1:2, :] = place
    here = iota((SLOT, NV), 0).astype(F32).astype(BF) == place.astype(F32).astype(BF)
    copies[2].wait()
    n_block = NV // VIS_BLOCK
    clip = jnp.broadcast_to(clip_ref[...].astype(F32) * 0.25, (n_block, n_block))
    same = iota((n_block, n_block), 0) == iota((n_block, n_block), 1)
    clip = jnp.sum(jnp.where(same, clip, 0.0), 1, keepdims=True)
    block = iota((n_block, NV), 1) // VIS_BLOCK == iota((n_block, NV), 0)
    level = jnp.sum(jnp.where(block, clip, 0.0), 0, keepdims=True)
    copies[3].wait()
    copies[4].wait()
    values = [pos_ref[0:1, :], pos_ref[1:2, :], obs_ref[0:1, :], obs_ref[1:2, :], level]
    pieces = [split3(v) for v in values]
    own = jnp.where(
        iota((NDEV, NV), 0).astype(F32).astype(BF) == owner.astype(F32).astype(BF), one, zero
    )
    table = jnp.concatenate(
        [
            jnp.where(here, jnp.broadcast_to(p[part], (SLOT, NV)), zero)
            for part in range(3) for p in pieces
        ]
        + [jnp.zeros((SLOT, NV), BF)], 0
    )
    copies[5].wait()
    meta_ref[2:3, :] = jnp.full((1, NV), off_ref[0, 1], jnp.int32)
    payload = lax.dot_general(own, table, (((1,), (1,)), ((), ())), preferred_element_type=F32)
    lane = iota((NDEV, LANES), 1)
    tail = payload[:, LANES:]
    tail = jnp.where(lane == A_HIGH - LANES, (off_ref[0, 0] >> 8).astype(F32), tail)
    tail = jnp.where(lane == A_HIGH + 1 - LANES, (off_ref[0, 0] & 255).astype(F32), tail)
    flat[pl.ds(NR2, NDEV, stride=MSG), :] = payload[:, :LANES]
    flat[pl.ds(NR2 + 1, NDEV, stride=MSG), :] = tail

    lane1 = iota((NQ, LANES), 1)
    freq = iota((NQ, LANES), 0) * (N_IMG // NQ) + (lane1 & (HALF - 1)) + lane1 // SUBG * HALF
    ph_c, ph_s = phase_of(off_ref[0, 1], freq)
    for copy in copies[6:]:
        copy.wait()
    for part in range(2):
        for a in range(NA):
            wide[part, a * RD:(a + 1) * RD, :] = slab_ref[
                0, part, :, a * LANES:(a + 1) * LANES
            ].astype(F32)
    tw_c, tw_s = tw_ref[:SUBG], tw_ref[SUBG:]
    col = table_ref[:LANES]
    coarse = jnp.concatenate(
        [
            jnp.concatenate([table_ref[LANES:LANES + NQ], table_ref[LANES + NQ:LANES + 2 * NQ]], 1),
            jnp.concatenate([table_ref[LANES + 2 * NQ:LANES + 3 * NQ], table_ref[LANES + 3 * NQ:]], 1),
        ], 0
    )
    low = lower((NQ, LANES))
    cols = [
        jnp.concatenate(
            [wide[0, pl.ds(r, NA, stride=RD), :], wide[1, pl.ds(r, NA, stride=RD), :]], 0
        ).astype(BF)
        for r in range(RD)
    ]
    y_ref[...] = jnp.dot(col, jnp.concatenate(cols, 1), preferred_element_type=F32)
    for row in range(NR2):
        both = []
        for r in (row, row + NR2):
            at = slice(r * LANES, (r + 1) * LANES)
            yr, yi = y_ref[:SUBG, at], y_ref[SUBG:, at]
            zr = yr * tw_c - yi * tw_s
            zi = yr * tw_s + yi * tw_c
            both.append(jnp.concatenate([zr, zi], 1).astype(BF))
        for i, (c, h) in enumerate(((0, 0), (0, 1), (1, 0), (1, 1))):
            at = row * LANES + i * HALF
            z_ref[at:at + HALF, :] = both[h][c * HALF:(c + 1) * HALF]
    out = lax.dot_general(
        coarse, z_ref[...], (((1,), (1,)), ((), ())), preferred_element_type=F32
    )
    for row in range(NR2):
        at = slice(row * LANES, (row + 1) * LANES)
        x, y = out[:NQ, at], out[NQ:, at]
        re, im = x * ph_c + y * ph_s, y * ph_c - x * ph_s
        pieces = [jnp.where(low, re, roll(im, SUBG)), jnp.where(low, roll(re, SUBG), im)]
        for c in range(2):
            for g in range(2):
                flat[pl.ds((2 * NQ * g + c) * MSG + row, NQ, stride=2 * MSG), :] = pieces[c]
    msg_ref[...] = flat[...].astype(BF)
    for copy in later:
        copy.wait()


def quarter_low(shape):
    return (iota(shape, len(shape) - 1) & HALF) == 0


def combine(both, rho):
    real, turned = 0.0, 0.0
    for t in range(2):
        rc, rs = rho[t, 0], rho[t, 1]
        a, b = both[:LANES, t * LANES:(t + 1) * LANES], both[LANES:, t * LANES:(t + 1) * LANES]
        real = real + (rc * a + rs * b)
        turned = turned + (rc * b - rs * a)
    real = real + roll(real, HALF)
    turned = turned + roll(turned, HALF)
    return (real - roll(turned, SUBG) * lane_sign(LANES, SUBG)).astype(BF)


def row_phases(tails, pair, rho_ref):
    first = (lax.axis_index("facet") // 2) * 4 + pair * 2
    low = quarter_low((1, LANES))
    start = [(v[:, 0:1] * 256.0 + v[:, 1:2]).astype(jnp.int32) for v in tails]
    starts = [jnp.where(low, start[2 * t], start[2 * t + 1]) for t in range(2)]
    eight = iota((8, LANES), 0)
    turn_c, turn_s = phase_of(
        jnp.where(eight < 4, starts[0], starts[1]), (first + (eight & 1)) * (N_IMG // 8)
    )
    for t in range(2):
        low_c, low_s = phase_of(starts[t], eight)
        high_c, high_s = phase_of(starts[t], eight * 8)
        for p in range(2):
            tc, ts = turn_c[t * 4 + p:t * 4 + p + 1], turn_s[t * 4 + p:t * 4 + p + 1]
            hc, hs = high_c * tc - high_s * ts, high_s * tc + high_c * ts
            for a in range(8):
                at = slice(p * SUBG + a * 8, p * SUBG + a * 8 + 8)
                ac, asin = hc[a:a + 1], hs[a:a + 1]
                rho_ref[t, 0, at, :] = low_c * ac - low_s * asin
                rho_ref[t, 1, at, :] = low_s * ac + low_c * asin


def rows_kernel(got_ref, fwd_ref, give_ref, rhs_ref, rho_ref, raw_ref, flat):
    flat[...] = got_ref[...].astype(F32)
    core = lax.axis_index("sub") & 1
    at = A_HIGH - LANES
    tails = [flat[f * NQ * MSG + NR2 + 1:f * NQ * MSG + NR2 + 2, at:at + 2] for f in range(NF)]
    row_phases(tails, 1 - core, rho_ref)
    low = quarter_low((NQ, LANES))
    for row in range(NR2):
        x = [flat[pl.ds(f * NQ * MSG + row, NQ, stride=MSG), :] for f in range(NF)]
        for t in range(2):
            at = slice(t * LANES, (t + 1) * LANES)
            a, b = x[2 * t], x[2 * t + 1]
            rhs_ref[row * NQ:(row + 1) * NQ, at] = jnp.where(low, a, roll(b, HALF)).astype(BF)
            rhs_ref[(NR2 + row) * NQ:(NR2 + row + 1) * NQ, at] = jnp.where(
                low, roll(a, LANES - HALF), b
            ).astype(BF)
    both = jnp.dot(fwd_ref[1 - core], rhs_ref[...], preferred_element_type=F32)
    give_ref[...] = combine(both, rho_ref)
    raw_ref[0] = flat[pl.ds(NR2, NDEV, stride=MSG), :]
    raw_ref[1] = flat[pl.ds(NR2 + 1, NDEV, stride=MSG), :]


def times(a, b):
    return a[0] * b[0] - a[1] * b[1], a[0] * b[1] + a[1] * b[0]


def tables_kernel(raw_ref, fwd_ref, rhs_ref, keep_ref, vis_ref, rho_ref, left, basis, small):
    core = lax.axis_index("sub") & 1
    at = A_HIGH - LANES
    row_phases([raw_ref[1, f * NQ:f * NQ + 1, at:at + 2] for f in range(NF)], core, rho_ref)
    got = jnp.concatenate([raw_ref[0].T, raw_ref[1].T], 0)
    n = 5 * SLOT
    vis_ref[...] = got[:n] + got[n:2 * n] + got[2 * n:3 * n]
    both = jnp.dot(fwd_ref[core], rhs_ref[...], preferred_element_type=F32)
    keep_ref[...] = combine(both, rho_ref)
    slot = 0
    for l in range(2):
        for which in range(2):
            turn = vis_ref[which * SLOT + l * 8:which * SLOT + l * 8 + 8, :] * (1.0 / SUBG)
            p1 = sincos_turn(turn)
            ones = jnp.ones_like(turn)

            def ladder(p, unit):
                p2 = times(p, p)
                p3 = times(p2, p)
                p4 = times(p2, p2)
                return [unit, p, p2, p3, p4, times(p4, p), times(p3, p3), times(p4, p3)], p4

            low, p4 = ladder(p1, (ones, jnp.zeros_like(turn)))
            high, _ = ladder(times(p4, p4), (ones, jnp.zeros_like(turn)))
            for i in range(8):
                for part in range(2):
                    small[slot, part, i * 8:i * 8 + 8, :] = low[i][part]
                    small[slot, 2 + part, i * 8:i * 8 + 8, :] = high[i][part] * 0.125
            for k in range(8):
                at = slice(k * LANES, (k + 1) * LANES)
                br, bi, ar, ai = [small[slot, part, pl.ds(k, 8, stride=8), :] for part in range(4)]
                re, im = [], []
                for a in range(8):
                    hr, hi = ar[a:a + 1, :], ai[a:a + 1, :]
                    re.append(hr * br - hi * bi)
                    im.append(hr * bi + hi * br)
                if which == 0:
                    left[l, 0:SUBG, at] = jnp.concatenate(re, 0)
                    left[l, SUBG:, at] = jnp.concatenate(im, 0)
                else:
                    basis[l, 0:SUBG, at] = jnp.concatenate(re, 0).astype(BF)
                    basis[l, SUBG:, at] = jnp.concatenate(im, 0).astype(BF)
            slot += 1


def visibility_kernel(keep_ref, other_ref, vis_ref, left, basis, corrected_ref, back_ref, inner, phasor):
    upper_core = (lax.axis_index("sub") & 1) == 1
    keep, other = keep_ref[...].astype(F32), other_ref[...].astype(F32)
    halves = jnp.where(upper_core, other, keep), jnp.where(upper_core, keep, other)
    subgrids = jnp.where(quarter_low((LANES, LANES)), roll(halves[0], LANES - HALF), halves[1])
    sign = lane_sign(SUBG, SUBG)
    for l in range(2):
        sub = subgrids[l * SUBG:(l + 1) * SUBG]
        matrix = jnp.concatenate([sub * sign, roll(sub, SUBG)], 0).astype(BF)
        inner[l] = jnp.dot(matrix, basis[l], preferred_element_type=F32)
    predicted = [[], [], [], []]
    for l in range(2):
        for k in range(8):
            at = slice(k * LANES, (k + 1) * LANES)
            lr, li = left[l, 0:SUBG, at], left[l, SUBG:, at]
            ir, ii = inner[l, 0:SUBG, at], inner[l, SUBG:, at]
            predicted[l].append(jnp.sum(lr * ir - li * ii, 0, keepdims=True))
            predicted[2 + l].append(jnp.sum(lr * ii + li * ir, 0, keepdims=True))
    rows_of = lambda c: vis_ref[c * SLOT:(c + 1) * SLOT, :]
    mis_r = rows_of(2) - jnp.concatenate(predicted[0] + predicted[1], 0)
    mis_i = rows_of(3) - jnp.concatenate(predicted[2] + predicted[3], 0)
    level = rows_of(4)
    live = level > 0.0
    threshold = jnp.where(live, level, 1.0)
    magnitude = jnp.sqrt(mis_r * mis_r + mis_i * mis_i)
    weight = jnp.where(live, threshold / jnp.maximum(magnitude, threshold), 0.0)
    wr, wi = weight * mis_r, weight * mis_i
    for l in range(2):
        for k in range(8):
            at = slice(k * LANES, (k + 1) * LANES)
            lr, li = left[l, 0:SUBG, at], left[l, SUBG:, at]
            vr, vi = wr[l * 8 + k:l * 8 + k + 1, :], wi[l * 8 + k:l * 8 + k + 1, :]
            phasor[l, 0:SUBG, at] = (lr * vr + li * vi).astype(BF)
            phasor[l, SUBG:, at] = (lr * vi - li * vr).astype(BF)
    sums = []
    for l in range(2):
        product = lax.dot_general(
            phasor[l], basis[l], (((1,), (1,)), ((), ())), preferred_element_type=F32
        )
        sums.append(product[:SUBG] * sign + roll(product[SUBG:], SUBG))
    corrected_ref[...] = jnp.concatenate(sums, 0).astype(BF)
    back_ref[...] = jnp.concatenate([wr, wi], 0)


def partial_images(x, pair, rho_ref, adj_ref):
    core = lax.axis_index("sub") & 1
    x = x.astype(F32)
    moved = jnp.where(core == 1, roll(x, LANES - HALF), roll(x, HALF))
    x = jnp.where(quarter_low(x.shape) != (core == 1), x, moved)
    turned = roll(x, SUBG) * -lane_sign(LANES, SUBG)
    cols = []
    for t in range(2):
        rc, rs = rho_ref[t, 0], rho_ref[t, 1]
        cols.append(
            jnp.concatenate([(x * rc + turned * rs).astype(BF), (x * rs - turned * rc).astype(BF)], 0)
        )
    half = NQ * NR2
    four = lax.axis_index("facet") // 2
    table = jnp.concatenate(
        [
            adj_ref[four, pair, pl.ds(pl.multiple_of(core * half, half), half), :],
            adj_ref[four, pair, pl.ds(pl.multiple_of((1 - core) * half, half), half), :],
        ], 0
    )
    return jnp.dot(table, jnp.concatenate(cols, 1), preferred_element_type=F32)


def mine_kernel(corrected_ref, back_ref, rho_ref, adj_ref, part_ref, tail_ref):
    back = [part.astype(F32) for part in split3(back_ref[...])]
    tail_ref[...] = jnp.concatenate(back + [jnp.zeros((2 * SLOT, LANES), F32)], 0).T
    part_ref[...] = partial_images(corrected_ref[...], lax.axis_index("sub") & 1, rho_ref, adj_ref)


def images_kernel(part_ref, other_ref, tail_ref, rho_ref, adj_ref, msg_ref, flat):
    pair = 1 - (lax.axis_index("sub") & 1)
    images = part_ref[...] + partial_images(other_ref[...], pair, rho_ref, adj_ref)
    low = quarter_low((NQ, LANES))
    for row in range(NR2):
        for t in range(2):
            at = slice(t * LANES, (t + 1) * LANES)
            a = images[row * NQ:(row + 1) * NQ, at]
            b = images[(NR2 + row) * NQ:(NR2 + row + 1) * NQ, at]
            flat[pl.ds(2 * t * NQ * MSG + row, NQ, stride=MSG), :] = jnp.where(low, a, roll(b, HALF))
            flat[pl.ds((2 * t + 1) * NQ * MSG + row, NQ, stride=MSG), :] = jnp.where(
                low, roll(a, LANES - HALF), b
            )
    flat[pl.ds(NR2, NDEV, stride=MSG), :] = tail_ref[...]
    flat[pl.ds(NR2 + 1, NDEV, stride=MSG), :] = jnp.zeros((NDEV, LANES), F32)
    msg_ref[...] = flat[...].astype(BF)


def facet_kernel(
    got_ref, meta_ref, coarse_ref, tw_ref, col_ref, out_hbm, res_hbm, flat, spread, z_ref, turned, out_ref, res_ref, sems,
):
    flat[...] = got_ref[...].astype(F32)
    copies = []
    sign = -lane_sign(NQ, SUBG)
    low = quarter_low((NQ, LANES))
    for h in range(2):
        lane1 = iota((NQ, LANES), 1)
        freq = iota((NQ, LANES), 0) * (N_IMG // NQ) + ((lane1 & (SUBG - 1)) ^ (h * HALF))
        ph_c, ph_s = phase_of(meta_ref[2:3, :LANES], freq)
        images = []
        for row in range(NR2):
            x = [
                flat[pl.ds(c * MSG + row, NQ, stride=2 * MSG), :]
                + flat[pl.ds((2 * NQ + c) * MSG + row, NQ, stride=2 * MSG), :]
                for c in range(2)
            ]
            image = jnp.where(low, x[h], x[1 - h])
            turn = roll(image, SUBG) * sign
            images.append(
                jnp.concatenate([image * ph_c + turn * ph_s, turn * ph_c - image * ph_s], 0).astype(BF)
            )
        spread[h] = jnp.dot(coarse_ref[...], jnp.concatenate(images, 1), preferred_element_type=F32)
    for h in range(2):
        tw_c, tw_s = tw_ref[2 * h], tw_ref[2 * h + 1]
        for row in range(NR2):
            at = slice(row * LANES, (row + 1) * LANES)
            z_ref[h, at, :] = (tw_c * spread[h, :LANES, at] + tw_s * spread[h, LANES:, at]).astype(BF)
        out = lax.dot_general(
            col_ref[h * LANES:(h + 1) * LANES], z_ref[h], (((1,), (1,)), ((), ())),
            preferred_element_type=F32,
        )
        for part in range(2):
            for row in range(NR2):
                turned[h, part, pl.ds(row, NA, stride=NR2), :] = out[
                    part * NA:(part + 1) * NA, row * LANES:(row + 1) * LANES
                ]
            where = slice(h * NR2, (h + 1) * NR2)
            for piece in range(2):
                for a in range(piece * NA // 2, (piece + 1) * NA // 2):
                    out_ref[part, where, a * LANES:(a + 1) * LANES] = turned[
                        h, part, a * NR2:(a + 1) * NR2, :
                    ]
                wide = slice(piece * NA // 2 * LANES, (piece + 1) * NA // 2 * LANES)
                copy = pltpu.make_async_copy(
                    out_ref.at[part, where, wide], out_hbm.at[0, part, where, wide],
                    sems.at[(h * 2 + part) * 2 + piece],
                )
                copy.start()
                copies.append(copy)
    n = 2 * SLOT
    back = flat[pl.ds(NR2, NDEV, stride=MSG), :].T[:3 * n]
    owner, place = meta_ref[0:1, :], meta_ref[1:2, :]
    own = jnp.where(iota((NDEV, NV), 0) == owner, 1.0, 0.0).astype(BF)
    found = jnp.dot(back.astype(BF), own, preferred_element_type=F32)
    found = found[:n] + found[n:2 * n] + found[2 * n:]
    here = iota((SLOT, NV), 0) == place
    for c in range(2):
        res_ref[c:c + 1, :] = jnp.sum(
            jnp.where(here, found[c * SLOT:(c + 1) * SLOT], 0.0), 0, keepdims=True
        )
    copies.append(pltpu.make_async_copy(res_ref, res_hbm, sems.at[8]))
    copies[-1].start()

    for copy in copies:
        copy.wait()


VMEM = pl.BlockSpec(memory_space=pltpu.VMEM)
HBM = pl.BlockSpec(memory_space=pltpu.MemorySpace.HBM)
TABLES = host_tables()


def in_place(arrays):
    return [pltpu.with_memory_space_constraint(x, pltpu.HBM) for x in arrays]


def exchange(message):
    pairs = message.reshape(NDEV * MSG // 2, 2, LANES)
    return lax.all_to_all(pairs, ALL, split_axis=0, concat_axis=0, tiled=True).reshape(message.shape)


def other_core(x):
    return lax.ppermute(x, "sub", [(i, i ^ 1) for i in range(NQ)])


def on_device(slab, offsets, position, observed, subgrid_of, clip):
    t = {name: jnp.asarray(value) for name, value in TABLES.items()}
    limit = pltpu.CompilerParams(vmem_limit_bytes=32 << 20)
    shape = jax.ShapeDtypeStruct
    message = shape((NDEV * MSG, LANES), BF)
    fwd_table = shape((2, 4 * SUBG, NQ * RD), BF)
    square = shape((LANES, LANES), BF)
    phases = shape((2, 2, LANES, LANES), F32)
    flat = pltpu.VMEM((NDEV * MSG, LANES), F32)

    def call(kernel, name, inputs, outs, scratch, in_specs=None, out_specs=None, flops=1 << 20):
        return pl.pallas_call(
            kernel,
            out_shape=outs,
            in_specs=in_specs or [VMEM] * len(inputs),
            out_specs=out_specs or (VMEM,) * len(outs),
            scratch_shapes=scratch,
            compiler_params=limit,
            cost_estimate=pl.CostEstimate(flops=flops, bytes_accessed=1 << 21, transcendentals=0),
            name=name,
        )(*inputs)

    inputs = (
        offsets, slab, position, observed, subgrid_of.reshape(1, NV), subgrid_of.reshape(8, LANES),
        clip.reshape(1, NV // VIS_BLOCK), t["column"], t["tw_fwd"],
    )
    sent, meta, fwd = call(
        send_kernel, "send", in_place(inputs + (t["row_fwd"],)),
        (message, shape((8, NV), jnp.int32), fwd_table),
        [pltpu.SMEM((1, 2), jnp.int32)]
        + [pltpu.VMEM(x.shape, x.dtype) for x in inputs[1:]]
        + [
            pltpu.VMEM((2, NA * RD, LANES), F32),
            flat,
            pltpu.VMEM((LANES, RD * LANES), F32),
            pltpu.VMEM((NR2 * LANES, 2 * LANES), BF),
            pltpu.SemaphoreType.DMA((len(inputs) + 5,)),
        ],
        in_specs=[HBM] * (len(inputs) + 1),
    )
    got = exchange(sent)
    give, rhs, other_rho, raw = call(
        rows_kernel, "rows", (got, fwd),
        (
            square, shape((NQ * RD, 2 * LANES), BF), phases, shape((2, NDEV, LANES), F32),
        ),
        [flat],
    )
    other = other_core(give)
    keep, vis, rho, left, basis = call(
        tables_kernel, "tables", (raw, fwd, rhs),
        (
            square, shape((5 * SLOT, LANES), F32), phases, shape((2, 2 * SUBG, NV), F32),
            shape((2, 2 * SUBG, NV), BF),
        ),
        [pltpu.VMEM((4, 4, SUBG, LANES), F32)],
    )
    corrected, back = call(
        visibility_kernel, "visibilities", (keep, other, vis, left, basis),
        (square, shape((2 * SLOT, LANES), F32)),
        [pltpu.VMEM((2, 2 * SUBG, NV), F32), pltpu.VMEM((2, 2 * SUBG, NV), BF)],
    )
    other = other_core(corrected)
    part, tail = call(
        mine_kernel, "mine", (corrected, back, rho, t["row_adj"]),
        (shape((NQ * RD, 2 * LANES), F32), shape((LANES, LANES), F32)), [],
    )
    (answer,) = call(images_kernel, "images", (part, other, tail, other_rho, t["row_adj"]), (message,), [flat])
    facet_adjoint, residual = call(
        facet_kernel, "facet",
        (exchange(answer), meta, t["coarse_adj"], t["tw_adj"], t["col_adj"]),
        (shape((1, 2, RD, NA * LANES), F32), shape((2, NV), F32)),
        [
            flat,
            pltpu.VMEM((2, 2 * LANES, NR2 * LANES), F32),
            pltpu.VMEM((2, NR2 * LANES, LANES), BF),
            pltpu.VMEM((2, 2, NA * NR2, LANES), F32),
            pltpu.VMEM((2, RD, NA * LANES), F32),
            pltpu.VMEM((2, NV), F32),
            pltpu.SemaphoreType.DMA((9,)),
        ],
        out_specs=(HBM, HBM),
    )
    return (facet_adjoint, residual)


def solution(mesh):
    placed = (
        P("facet", None, "sub", None),
        P("facet", None),
        P(None, ALL),
        P(None, ALL),
        P(ALL, None),
        P(ALL),
    )
    return jax.shard_map(
        on_device,
        mesh=mesh,
        in_specs=placed,
        out_specs=(P("facet", None, "sub", None), P(None, ALL)),
        check_vma=False,
    )
```
